128 devices in a mesh: node: 8 (over y, core), tm: 16 (over x, z).
Axes of the slice: x: 4, y: 4, z: 4, core: 2. Of those that a mesh axis runs over, the one named last changes fastest.
Arguments:
- memory: bfloat16 [131072, 1024], P(('node', 'tm')), may hold values from -6 to 6
- ends_owner: int32 [32768, 2], P(('node', 'tm')), may hold values from 0 to 127, all different within a row; in each aligned block of 256 rows (0 to 255, 256 to 511, ...) at most 5 rows name the same one
- ends_row: int32 [32768, 2], P(('node', 'tm')), may hold values from 0 to 1023
- event_mask: int32 [32768], P(('node', 'tm')), may hold values 0 or 1
- edge_feat: bfloat16 [32768, 128], P(('node', 'tm')), may hold values from -6 to 6
- msg_w1: bfloat16 [2176, 1024], replicated, may hold values from -0.125 to 0.125
- msg_b1: float32 [1024], replicated, may hold values from -4 to 4
- msg_w2: bfloat16 [1024, 1024], replicated, may hold values from -0.1875 to 0.1875
- msg_b2: float32 [1024], replicated, may hold values from -3 to 3
- gru_in: bfloat16 [1024, 3072], replicated, may hold values from -0.1875 to 0.1875
- gru_hid: bfloat16 [1024, 3072], replicated, may hold values from -0.1875 to 0.1875
- gru_bias: float32 [3072], replicated, may hold values from -3 to 3
Outputs:
- new_memory: bfloat16 [131072, 1024], P(('node', 'tm'))
The draws below stay inside these ranges and needn't reach their ends.
Inputs may be any that keep to these rules, and one draw needn't show every extreme that they name: `ends_owner`: within the events of one device (aligned blocks of 256 rows) no device is named by more than 5 endpoints, and some device by exactly 5; an event's two endpoints have different owners.
All inputs are finite; a program needn't handle non-finite values. No bound on the sum of `event_mask` on one device may be relied on, other than what follows from the above.
Results may differ from the reference program's by a relative error of at most 0.0026.
Values may be sent and summed in bfloat16 or wider, within the bound.
No kernel may reach another device: no remote copies, remote signals or barrier semaphores. Data moves between devices by JAX's collectives and lax.ppermute only.
A program may use at most 128 MiB of HBM per device.

```python
import math
import jax
import jax.numpy as jnp
import numpy as np
from jax import lax

DM = 1024
HID = 1024
FE = 128
NODE_DEV = 1024
E_DEV = 256
CAP = 5
EVENTS = 32768
NODES = 131072
DEVICES = 128


def set_ends(drawn, key, smallest, largest):
    index_at = [jax.random.randint(jax.random.fold_in(key, axis), (), 0, length) for axis, length in enumerate(drawn.shape)]
    main_axis = drawn.shape.index(max(drawn.shape))
    neighbour = index_at[:main_axis] + [(index_at[main_axis] + 1) % drawn.shape[main_axis]] + index_at[main_axis + 1:]
    return drawn.at[tuple(index_at)].set(smallest).at[tuple(neighbour)].set(largest)


def block_levels(stream_key, dims, cuts, smallest, largest):
    def one(dim, parts):
        steps = jax.random.uniform(jax.random.fold_in(jax.random.fold_in(stream_key, 6), dim), (parts,), jnp.float32, smallest / len(cuts), largest / len(cuts))
        return jnp.repeat(jnp.exp(steps), dims[dim] // parts).reshape((-1,) + (1,) * (len(dims) - dim - 1))

    loudness = one(*cuts[0])
    for cut in cuts[1:]:
        loudness = loudness * one(*cut)
    return loudness


def deal_out(rng, own, number, rows, amount, top, bound, skew):
    sequence = jax.random.permutation(rng, amount)
    heavy_load, ordinary = portions_of(amount, rows * top, bound, skew, True), portions_of(amount, rows * top, bound, skew, False)
    places = jnp.arange(amount)

    def named(sizes, rotation):
        used = int((sizes > 0).sum())
        fixed = max(1, used // 4)
        moved = fixed + (places - fixed + rotation * (used - fixed)) % max(1, amount - fixed)
        return jnp.zeros((amount,), jnp.int32).at[sequence[jnp.where(places < fixed, places, moved)]].set(jnp.asarray(sizes, jnp.int32))

    sizes = jnp.where(number % 4 == 0, named(heavy_load, number // 4), named(ordinary, number - number // 4 - 1))
    mixed = jax.random.permutation(jax.random.fold_in(own, 3), amount)
    source_of, sink = mixed[0:amount // 2 * 2:2], mixed[1:amount // 2 * 2:2]
    slack = jnp.minimum(sizes[source_of] - 1, bound - sizes[sink]) // 2
    slack = jnp.where((source_of == sequence[0]) | (sink == sequence[0]) | (sizes[sink] == 0), 0, jnp.maximum(slack, 0))
    moved = jax.random.randint(jax.random.fold_in(own, 4), (amount // 2,), 0, 1 << 20) % (slack + 1)
    sizes = sizes.at[source_of].add(-moved).at[sink].add(moved)
    items = jnp.searchsorted(jnp.cumsum(sizes), jnp.arange(rows * top), side="right").astype(jnp.int32)
    listing = items.reshape(top, rows).T
    listing = listing[jax.random.permutation(jax.random.fold_in(own, 1), rows)]
    rotation = jax.random.randint(jax.random.fold_in(own, 2), (rows, 1), 0, top)
    return jnp.take_along_axis(listing, (jnp.arange(top)[None, :] + rotation) % top, axis=1)


def portions_of(amount, total, most, lean, full):
    loads = [(1 << 20) // math.isqrt(rank ** lean) + 1 for rank in range(1, amount + 1)]
    largest = most if full else min(most, max(-(-total // amount), total * loads[0] // sum(loads)))
    least = 1 if total - largest >= amount - 1 else 0
    holding, rest = [largest] + [least] * (amount - 1), total - largest - least * (amount - 1)
    while rest > 0:
        movable = [i for i in range(1, amount) if holding[i] < largest] or [i for i in range(1, amount) if holding[i] < most]
        mass, left = sum([loads[i] for i in movable]), rest
        for i in movable:
            extra = min(most - holding[i], max(1, left * loads[i] // mass), rest)
            holding[i] = holding[i] + extra
            rest = rest - extra
    return np.array(holding)


def gaussian(key, extent, spread, most, cuts=(), kind=jnp.bfloat16):
    gain = block_levels(key, extent, cuts, -0.22, 0.18) if cuts else 1.0
    result = jax.random.normal(key, extent, jnp.float32) * spread * gain
    return jnp.minimum(jnp.maximum(result, -most), most).astype(kind)


def setup_inputs(seed: int = 0) -> dict:
    splits = jax.random.split(jax.random.key(seed), 13)
    memory = gaussian(splits[0], (NODES, DM), 1.0, 6.0, ((0, 128),))
    ends_owner_keys = jax.random.split(jax.random.fold_in(splits[1], 1), EVENTS // E_DEV)
    ends_owner_turns = jax.random.permutation(jax.random.fold_in(splits[1], 3), EVENTS // E_DEV)
    ends_owner = jax.vmap(lambda own, number: deal_out(jax.random.fold_in(splits[1], 2), own, number, E_DEV, DEVICES, 2, CAP, 1))(ends_owner_keys, ends_owner_turns).reshape((EVENTS, 2))
    ends_row = set_ends(jax.random.randint(splits[2], (EVENTS, 2), 0, NODE_DEV), jax.random.fold_in(splits[2], 1), 0, NODE_DEV - 1).astype(jnp.int32)
    event_mask = set_ends((jax.random.randint(splits[3], (EVENTS,), 0, 4) < 3).astype(jnp.int32), jax.random.fold_in(splits[3], 1), 0, 1)
    edge_feat = gaussian(splits[4], (EVENTS, FE), 1.0, 6.0, ((0, 128),))
    msg_w1 = gaussian(splits[5], (2 * DM + FE, HID), (2 * DM + FE) ** -0.5, 0.125)
    msg_b1 = gaussian(splits[6], (HID,), 1.0, 4.0, (), jnp.float32)
    msg_w2 = gaussian(splits[7], (HID, DM), HID ** -0.5, 0.1875)
    msg_b2 = gaussian(splits[8], (DM,), 0.5, 3.0, (), jnp.float32)
    gru_in = gaussian(splits[9], (DM, 3 * DM), DM ** -0.5, 0.1875)
    gru_hid = gaussian(splits[10], (DM, 3 * DM), DM ** -0.5, 0.1875)
    gru_bias = gaussian(splits[11], (3 * DM,), 0.5, 3.0, (), jnp.float32)
    return dict(memory=memory, ends_owner=ends_owner, ends_row=ends_row, event_mask=event_mask, edge_feat=edge_feat, msg_w1=msg_w1, msg_b1=msg_b1, msg_w2=msg_w2, msg_b2=msg_b2, gru_in=gru_in, gru_hid=gru_hid, gru_bias=gru_bias)


def memory_update(aggregate, memory, gru_in, gru_hid, gru_bias, touched):
    feature_width = memory.shape[1]
    gates_in = jnp.dot(aggregate, gru_in, preferred_element_type=jnp.float32) + gru_bias
    gates_hid = jnp.dot(memory, gru_hid, preferred_element_type=jnp.float32)
    reset = jax.nn.sigmoid(gates_in[:, :feature_width] + gates_hid[:, :feature_width])
    update = jax.nn.sigmoid(gates_in[:, feature_width:2 * feature_width] + gates_hid[:, feature_width:2 * feature_width])
    candidate = jnp.tanh(gates_in[:, 2 * feature_width:] + reset * gates_hid[:, 2 * feature_width:])
    previous = memory.astype(jnp.float32)
    renewed = (1.0 - update) * candidate + update * previous
    return jnp.where(touched[:, None], renewed, previous).astype(jnp.bfloat16)


def reference(memory, ends_owner, ends_row, event_mask, edge_feat, msg_w1, msg_b1, msg_w2, msg_b2, gru_in, gru_hid, gru_bias):
    node_total = memory.shape[0]
    ids = (ends_owner * NODE_DEV + ends_row).astype(jnp.int32)
    block_ids = ids.reshape(-1, E_DEV, 2)
    block_mask = event_mask.reshape(-1, E_DEV)
    block_feat = edge_feat.reshape(-1, E_DEV, FE)

    def one_block(carry, item):
        summed, tally = carry
        bid, bmask, bfeat = item
        pairs = jnp.take(memory, bid.reshape(-1), axis=0).reshape(E_DEV, 2 * DM)
        inputs = jnp.concatenate([pairs, bfeat], axis=1)
        hidden = jax.nn.relu(jnp.dot(inputs, msg_w1, preferred_element_type=jnp.float32) + msg_b1).astype(jnp.bfloat16)
        weight_mask = bmask.astype(jnp.float32)
        message = ((jnp.dot(hidden, msg_w2, preferred_element_type=jnp.float32) + msg_b2) * weight_mask[:, None]).astype(jnp.bfloat16)
        summed = summed.at[bid[:, 1]].add(message.astype(jnp.float32))
        tally = tally.at[bid[:, 1]].add(weight_mask)
        return (summed, tally), None

    start = (jnp.zeros((node_total, DM), jnp.float32), jnp.zeros((node_total,), jnp.float32))
    (summed, tally), unused = lax.scan(one_block, start, (block_ids, block_mask, block_feat))
    aggregate = (summed / jnp.maximum(tally, 1.0)[:, None]).astype(jnp.bfloat16)

    def one_owner(item):
        agg_rows, mem_rows, tally_rows = item
        return memory_update(agg_rows, mem_rows, gru_in, gru_hid, gru_bias, tally_rows > 0.5)

    renewed = lax.map(one_owner, (aggregate.reshape(-1, NODE_DEV, DM), memory.reshape(-1, NODE_DEV, DM), tally.reshape(-1, NODE_DEV)))
    return renewed.reshape(node_total, DM)
```

```python
import jax
import jax.numpy as jnp
from jax import lax
from jax.experimental import pallas as pl
from jax.experimental.pallas import tpu as pltpu
from jax.sharding import PartitionSpec as P

AXES = ("node", "tm")
LANES = 128
SUB = 8
ACTIVE = 1024
TILE = 256
MIB = 1 << 20

VM = pl.BlockSpec(memory_space=pltpu.VMEM)
SM = pl.BlockSpec(memory_space=pltpu.SMEM)


def plan_kernel(capacity, owner_ref, row_ref, mask_ref, ids_ref, place_ref):
    devices = ids_ref.shape[0]
    events = owner_ref.shape[1]
    ends = 2 * events
    owner = jnp.concatenate([owner_ref[0:1, :], owner_ref[1:2, :]], axis=1)
    code = jnp.concatenate([row_ref[0:1, :], row_ref[1:2, :] + ACTIVE * mask_ref[...]], axis=1)
    named = lax.broadcasted_iota(jnp.int32, (devices, ends), 0) == owner
    named_b = named.astype(jnp.float32).astype(jnp.bfloat16)
    before = (
        lax.broadcasted_iota(jnp.int32, (ends, ends), 0) < lax.broadcasted_iota(jnp.int32, (ends, ends), 1)
    ).astype(jnp.float32).astype(jnp.bfloat16)
    count = jnp.dot(named_b, before, preferred_element_type=jnp.float32)
    position = jnp.sum(jnp.where(named, count, 0.0), axis=0, keepdims=True).astype(jnp.int32)
    place = owner * capacity + position
    place_ref[0:1, :] = place[:, :events]
    place_ref[1:2, :] = place[:, events:]
    here = lax.broadcasted_iota(jnp.int32, (LANES, ends), 0) == position
    low = jnp.where(here, (code & 31).astype(jnp.float32), 0.0).astype(jnp.bfloat16)
    high = jnp.where(here, (code >> 5).astype(jnp.float32), 0.0).astype(jnp.bfloat16)
    contract = (((1,), (1,)), ((), ()))
    low_sum = lax.dot_general(named_b, low, contract, preferred_element_type=jnp.float32)
    high_sum = lax.dot_general(named_b, high, contract, preferred_element_type=jnp.float32)
    ids_ref[...] = (low_sum + 32.0 * high_sum).astype(jnp.int32)


def answer_kernel(capacity, ids_ref, memory_ref, out_ref):
    devices = ids_ref.shape[0]
    group = 8

    def step(i, carry):
        for a in range(group):
            p = i * group + a
            for k in range(capacity):
                row = ids_ref[p, k] & (ACTIVE - 1)
                out_ref[p * capacity + k] = memory_ref[row]
        return carry

    lax.fori_loop(0, devices // group, step, 0)


def compact_kernel(capacity, ids_ref, slot_ref, index_ref, count_ref, node_ref, of_ref, size_ref):
    devices = ids_ref.shape[0]
    rows = of_ref.shape[0]

    def clear(i, carry):
        for a in range(16):
            of_ref[i * 16 + a] = -1
        return carry

    lax.fori_loop(0, rows // 16, clear, 0)

    def step(p, carry):
        taken, nodes = carry
        for k in range(capacity):
            code = ids_ref[p, k]
            active = code >= ACTIVE
            node = code & (ACTIVE - 1)
            known = of_ref[node]
            fresh = active & (known < 0)
            index = jnp.where(known < 0, nodes, known)
            of_ref[node] = jnp.where(active, index, known)
            slot_ref[taken] = p * capacity + k
            index_ref[taken] = index
            old = count_ref[index]
            was = jnp.where(known < 0, 0, old)
            count_ref[index] = jnp.where(active, was + 1, was)
            node_ref[index] = jnp.where(fresh, node, jnp.where(known < 0, 0, node_ref[index]))
            taken = taken + active.astype(jnp.int32)
            nodes = nodes + fresh.astype(jnp.int32)
        return taken, nodes

    taken, nodes = lax.fori_loop(0, devices, step, (jnp.int32(0), jnp.int32(0)))
    size_ref[0] = taken
    size_ref[1] = nodes


def to_matrix(tiles_ref, start, rows):
    parts = [tiles_ref[pl.ds(start * SUB + c, rows, stride=SUB), :].astype(jnp.bfloat16) for c in range(SUB)]
    return jnp.concatenate(parts, axis=1)


def hidden_gates_kernel(node_ref, size_ref, memory_ref, gru_ref, previous_ref, gates_ref, tiles_ref):
    nodes = size_ref[1]
    steps = pl.cdiv(nodes, TILE)
    width = previous_ref.shape[1]

    def block(t, carry):
        def copy(i, c):
            for a in range(16):
                u = i * 16 + a
                row = node_ref[t * TILE + u] & (ACTIVE - 1)
                tiles_ref[pl.ds(pl.multiple_of(u * SUB, SUB), SUB), :] = memory_ref[row].astype(jnp.float32)
            return c

        lax.fori_loop(0, TILE // 16, copy, 0)
        here = pl.ds(pl.multiple_of(t * TILE, TILE), TILE)
        previous_ref[here, :] = to_matrix(tiles_ref, 0, TILE)

        def columns(j, c):
            cols = pl.ds(pl.multiple_of(j * 256, 256), 256)
            gates_ref[here, cols] = jnp.dot(
                previous_ref[here, :], gru_ref[:, cols], preferred_element_type=jnp.float32
            )
            return c

        lax.fori_loop(0, 3 * width // 256, columns, 0)
        return carry

    lax.fori_loop(0, steps, block, 0)


def message_kernel(
    place_ref, rows_ref, feat_ref, w1_ref, b1_ref, w2_ref, b2_ref, out_ref, tiles_ref, inputs_ref, hidden_ref
):
    events = feat_ref.shape[0]
    width = w2_ref.shape[1]
    hid = w2_ref.shape[0]
    group = 16
    for half in range(2):

        def fetch(i, c):
            for a in range(group):
                e = i * group + a
                tiles_ref[pl.ds(pl.multiple_of(e * SUB, SUB), SUB), :] = rows_ref[place_ref[half, e]].astype(
                    jnp.float32
                )
            return c

        lax.fori_loop(0, events // group, fetch, 0)
        inputs_ref[:, half * width : (half + 1) * width] = to_matrix(tiles_ref, 0, events)
    inputs_ref[:, 2 * width :] = feat_ref[...]
    for j in range(hid // 256):
        cols = slice(j * 256, (j + 1) * 256)
        h = jnp.dot(inputs_ref[...], w1_ref[:, cols], preferred_element_type=jnp.float32) + b1_ref[:, cols]
        hidden_ref[:, cols] = jnp.maximum(h, 0.0).astype(jnp.bfloat16)
    for j in range(width // 256):
        cols = slice(j * 256, (j + 1) * 256)
        m = jnp.dot(hidden_ref[...], w2_ref[:, cols], preferred_element_type=jnp.float32) + b2_ref[:, cols]
        for c in range(2):
            tiles_ref[pl.ds(2 * j + c, events, stride=SUB), :] = m[:, c * LANES : (c + 1) * LANES]
    out_ref[...] = jnp.zeros_like(out_ref)

    def send(i, c):
        for a in range(group):
            e = i * group + a
            out_ref[place_ref[1, e]] = tiles_ref[pl.ds(pl.multiple_of(e * SUB, SUB), SUB), :].astype(jnp.bfloat16)
        return c

    lax.fori_loop(0, events // group, send, 0)


def update_kernel(
    slot_ref,
    index_ref,
    count_ref,
    size_ref,
    incoming_ref,
    of_ref,
    memory_ref,
    previous_ref,
    gates_ref,
    gru_ref,
    bias_ref,
    out_ref,
    tiles_ref,
    aggregate_ref,
    renewed_ref,
):
    width = memory_ref.shape[1]
    taken = size_ref[0]
    nodes = size_ref[1]
    steps = pl.cdiv(nodes, TILE)

    def clear(t, c):
        start = pl.multiple_of(t * TILE * SUB, TILE * SUB)
        tiles_ref[pl.ds(start, TILE * SUB), :] = jnp.zeros((TILE * SUB, LANES), jnp.float32)
        return c

    lax.fori_loop(0, steps, clear, 0)

    def add(i, c):
        slot = slot_ref[i]
        here = pl.ds(pl.multiple_of(index_ref[i] * SUB, SUB), SUB)
        tiles_ref[here, :] += incoming_ref[slot].astype(jnp.float32)
        return c

    lax.fori_loop(0, taken, add, 0)

    def mean(i, c):
        here = pl.ds(pl.multiple_of(i * SUB, SUB), SUB)
        tiles_ref[here, :] = tiles_ref[here, :] / count_ref[i].astype(jnp.float32)
        return c

    lax.fori_loop(0, nodes, mean, 0)

    def block(t, c):
        here = pl.ds(pl.multiple_of(t * TILE, TILE), TILE)
        aggregate_ref[...] = to_matrix(tiles_ref, pl.multiple_of(t * TILE, TILE), TILE)
        for j in range(width // 256):
            pre = []
            for g in range(3):
                cols = slice(g * width + j * 256, g * width + (j + 1) * 256)
                pre.append(
                    jnp.dot(aggregate_ref[...], gru_ref[:, cols], preferred_element_type=jnp.float32)
                    + bias_ref[:, cols]
                )
            hid = [gates_ref[here, g * width + j * 256 : g * width + (j + 1) * 256] for g in range(3)]
            reset = jax.nn.sigmoid(pre[0] + hid[0])
            update = jax.nn.sigmoid(pre[1] + hid[1])
            candidate = jnp.tanh(pre[2] + reset * hid[2])
            previous = previous_ref[here, j * 256 : (j + 1) * 256].astype(jnp.float32)
            renewed = (1.0 - update) * candidate + update * previous
            renewed_ref[here, j * 256 : (j + 1) * 256] = renewed.astype(jnp.bfloat16)
        return c

    @pl.when(nodes == 0)
    def _():
        renewed_ref[...] = jnp.zeros_like(renewed_ref)

    lax.fori_loop(0, steps, block, 0)
    rows = 128

    def place(t):
        def band(i, c):
            here = pl.ds(pl.multiple_of(i * rows, rows), rows)
            of = of_ref[here, :]
            lane = lax.broadcasted_iota(jnp.int32, (rows, TILE), 1) + t * TILE
            pick = (of == lane).astype(jnp.float32).astype(jnp.bfloat16)
            found = jnp.dot(
                pick, renewed_ref[t * TILE : (t + 1) * TILE, :], preferred_element_type=jnp.float32
            )
            base = memory_ref if t == 0 else out_ref
            mine = (of >= t * TILE) & (of < (t + 1) * TILE)
            out_ref[here, :] = jnp.where(mine, found, base[here, :].astype(jnp.float32)).astype(jnp.bfloat16)
            return c

        lax.fori_loop(0, out_ref.shape[0] // rows, band, 0)

    place(0)
    for t in range(1, renewed_ref.shape[0] // TILE):

        @pl.when(t < steps)
        def _():
            place(t)


def on_device(
    memory,
    ends_owner,
    ends_row,
    event_mask,
    edge_feat,
    msg_w1,
    msg_b1,
    msg_w2,
    msg_b2,
    gru_in,
    gru_hid,
    gru_bias,
):
    devices = lax.axis_size(AXES)
    events = ends_owner.shape[0]
    node_rows, width = memory.shape
    hid = msg_w2.shape[0]
    capacity = 5 * events // (2 * devices)
    slots = devices * capacity
    padded = pl.cdiv(slots, TILE) * TILE
    cells = width // LANES
    f32, bf16, i32 = jnp.float32, jnp.bfloat16, jnp.int32
    shape = jax.ShapeDtypeStruct

    ids, place = pl.pallas_call(
        lambda *refs: plan_kernel(capacity, *refs),
        out_shape=(shape((devices, LANES), i32), shape((2, events), i32)),
        in_specs=[VM, VM, VM],
        out_specs=(VM, VM),
        name="plan",
    )(ends_owner.T, ends_row.T, event_mask.reshape(1, events))

    arrived = lax.all_to_all(
        ids.reshape(devices, 1, LANES), AXES, split_axis=0, concat_axis=0, tiled=True
    ).reshape(devices, LANES)
    tiles = memory.reshape(node_rows, cells, LANES)

    answers = pl.pallas_call(
        lambda *refs: answer_kernel(capacity, *refs),
        out_shape=shape((slots, cells, LANES), bf16),
        in_specs=[SM, VM],
        out_specs=VM,
        name="answer",
    )(arrived, tiles)
    returned = lax.all_to_all(
        answers.reshape(devices, capacity, cells, LANES), AXES, split_axis=0, concat_axis=0, tiled=True
    ).reshape(slots, cells, LANES)

    slot, index, count, node, of, size = pl.pallas_call(
        lambda *refs: compact_kernel(capacity, *refs),
        out_shape=(
            shape((1024,), i32),
            shape((1024,), i32),
            shape((1024,), i32),
            shape((1024,), i32),
            shape((node_rows,), i32),
            shape((8,), i32),
        ),
        in_specs=[SM],
        out_specs=(SM, SM, SM, SM, SM, SM),
        cost_estimate=pl.CostEstimate(flops=4_000_000_000, bytes_accessed=20_000_000, transcendentals=0),
        name="compact",
    )(arrived)

    previous, gates = pl.pallas_call(
        hidden_gates_kernel,
        out_shape=(shape((padded, width), bf16), shape((padded, 3 * width), f32)),
        in_specs=[SM, SM, VM, VM],
        out_specs=(VM, VM),
        scratch_shapes=[pltpu.VMEM((TILE * SUB, LANES), f32)],
        compiler_params=pltpu.CompilerParams(vmem_limit_bytes=40 * MIB),
        cost_estimate=pl.CostEstimate(flops=4_000_000_000, bytes_accessed=20_000_000, transcendentals=0),
        name="hidden_gates",
    )(node, size, tiles, gru_hid)

    outgoing = pl.pallas_call(
        message_kernel,
        out_shape=shape((slots, cells, LANES), bf16),
        in_specs=[SM, VM, VM, VM, VM, VM, VM],
        out_specs=VM,
        scratch_shapes=[
            pltpu.VMEM((events * SUB, LANES), f32),
            pltpu.VMEM((events, msg_w1.shape[0]), bf16),
            pltpu.VMEM((events, hid), bf16),
        ],
        compiler_params=pltpu.CompilerParams(vmem_limit_bytes=24 * MIB),
        name="message",
    )(place, returned, edge_feat, msg_w1, msg_b1.reshape(1, hid), msg_w2, msg_b2.reshape(1, width))
    incoming = lax.all_to_all(
        outgoing.reshape(devices, capacity, cells, LANES), AXES, split_axis=0, concat_axis=0, tiled=True
    ).reshape(slots, cells, LANES)

    return pl.pallas_call(
        update_kernel,
        out_shape=shape((node_rows, width), bf16),
        in_specs=[SM, SM, SM, SM, VM, VM, VM, VM, VM, VM, VM],
        out_specs=VM,
        scratch_shapes=[
            pltpu.VMEM((padded * SUB, LANES), f32),
            pltpu.VMEM((TILE, width), bf16),
            pltpu.VMEM((padded, width), bf16),
        ],
        compiler_params=pltpu.CompilerParams(vmem_limit_bytes=48 * MIB),
        name="update",
    )(
        slot,
        index,
        count,
        size,
        incoming,
        of.reshape(node_rows, 1),
        memory,
        previous,
        gates,
        gru_in,
        gru_bias.reshape(1, 3 * width),
    )


def solution(mesh):
    row = P(AXES, None)
    return jax.shard_map(
        on_device,
        mesh=mesh,
        in_specs=(row, row, row, P(AXES), row, P(), P(), P(), P(), P(), P(), P()),
        out_specs=row,
        check_vma=False,
    )
```

```python
import jax
import jax.numpy as jnp
from jax import lax
from jax.experimental import pallas as pl
from jax.experimental.pallas import tpu as pltpu
from jax.sharding import PartitionSpec as P

AXES = ("node", "tm")
LANES = 128
SUB = 8
ACTIVE = 1024
TILE = 256
COLS = 256
UNROLL = 16
MIB = 1 << 20
WHOLE = 58 * MIB
MOST = 51 * MIB
ANSWER = 51968 * 1024

VM = pl.BlockSpec(memory_space=pltpu.VMEM)
SM = pl.BlockSpec(memory_space=pltpu.SMEM)
HBM = pl.BlockSpec(memory_space=pltpu.HBM)


def plan_kernel(capacity, owner_ref, row_ref, mask_ref, ids_ref, place_ref):
    devices = ids_ref.shape[0]
    events = owner_ref.shape[1]
    ends = 2 * events
    owner = jnp.concatenate([owner_ref[0:1, :], owner_ref[1:2, :]], axis=1)
    code = jnp.concatenate([row_ref[0:1, :], row_ref[1:2, :] + ACTIVE * mask_ref[...]], axis=1)
    named = lax.broadcasted_iota(jnp.int32, (devices, ends), 0) == owner
    named_b = named.astype(jnp.float32).astype(jnp.bfloat16)
    before = (
        lax.broadcasted_iota(jnp.int32, (ends, ends), 0) < lax.broadcasted_iota(jnp.int32, (ends, ends), 1)
    ).astype(jnp.float32).astype(jnp.bfloat16)
    count = jnp.dot(named_b, before, preferred_element_type=jnp.float32)
    position = jnp.sum(jnp.where(named, count, 0.0), axis=0, keepdims=True).astype(jnp.int32)
    place = owner * capacity + position
    place_ref[0:1, :] = place[:, :events]
    place_ref[1:2, :] = place[:, events:]
    here = lax.broadcasted_iota(jnp.int32, (LANES, ends), 0) == position
    low = jnp.where(here, (code & 31).astype(jnp.float32), 0.0).astype(jnp.bfloat16)
    high = jnp.where(here, (code >> 5).astype(jnp.float32), 0.0).astype(jnp.bfloat16)
    contract = (((1,), (1,)), ((), ()))
    low_sum = lax.dot_general(named_b, low, contract, preferred_element_type=jnp.float32)
    high_sum = lax.dot_general(named_b, high, contract, preferred_element_type=jnp.float32)
    ids_ref[...] = (low_sum + 32.0 * high_sum).astype(jnp.int32)


def answer_kernel(capacity, ids_ref, memory_ref, out_ref, codes_ref, turned_ref, wanted_ref, rows_ref, load_sem, sems):
    devices = ids_ref.shape[0]
    turned = jnp.transpose(ids_ref[...])[:SUB, :]
    codes_ref[...] = turned
    turned_ref[...] = turned
    load = pltpu.make_async_copy(turned_ref, wanted_ref, load_sem)
    load.start()
    load.wait()
    group = 8
    chunks = sems.shape[0]
    part = devices // chunks
    sends = []
    for q in range(chunks):

        def step(i, carry):
            for a in range(group):
                p = q * part + i * group + a
                for k in range(capacity):
                    rows_ref[p * capacity + k] = memory_ref[wanted_ref[k, p] & (ACTIVE - 1)]
            return carry

        lax.fori_loop(0, part // group, step, 0)
        here = pl.ds(q * part * capacity, part * capacity)
        send = pltpu.make_async_copy(rows_ref.at[here], out_ref.at[here], sems.at[q])
        send.start()
        sends.append(send)
    for send in sends:
        send.wait()


def compact_kernel(capacity, spare_row, ids_ref, slot_ref, index_ref, count_ref, node_ref, of_ref, size_ref):
    devices = ids_ref.shape[1]
    rows = of_ref.shape[0]

    def clear(i, carry):
        for a in range(16):
            of_ref[i * 16 + a] = -1
        return carry

    lax.fori_loop(0, rows // 16, clear, 0)

    def step(p, carry):
        taken, nodes = carry
        for k in range(capacity):
            code = ids_ref[k, p]
            active = code >= ACTIVE
            node = code & (ACTIVE - 1)
            known = of_ref[node]
            fresh = active & (known < 0)
            index = jnp.where(known < 0, nodes, known)
            of_ref[node] = jnp.where(active, index, known)
            slot_ref[taken] = p * capacity + k
            index_ref[taken] = index
            old = count_ref[index]
            was = jnp.where(known < 0, 0, old)
            count_ref[index] = jnp.where(active, was + 1, was)
            node_ref[index] = jnp.where(fresh, node, jnp.where(known < 0, 0, node_ref[index]))
            taken = taken + active.astype(jnp.int32)
            nodes = nodes + fresh.astype(jnp.int32)
        return taken, nodes

    taken, nodes = lax.fori_loop(0, devices, step, (jnp.int32(0), jnp.int32(0)))
    size_ref[0] = taken
    size_ref[1] = nodes
    for a in range(UNROLL):
        slot_ref[taken + a] = 0
        index_ref[taken + a] = spare_row
        count_ref[nodes + a] = 1


def to_matrix(tiles_ref, start, rows):
    parts = [tiles_ref[pl.ds(start * SUB + c, rows, stride=SUB), :].astype(jnp.bfloat16) for c in range(SUB)]
    return jnp.concatenate(parts, axis=1)


def hidden_gates_kernel(
    node_ref, size_ref, memory_ref, gru_ref, previous_ref, gates_ref, tiles_ref, rows_ref, made_ref, sems
):
    steps = jnp.maximum(pl.cdiv(size_ref[1], TILE), 1)
    width = rows_ref.shape[1]

    def block(t, carry):
        def copy(i, c):
            for a in range(16):
                u = i * 16 + a
                row = node_ref[t * TILE + u] & (ACTIVE - 1)
                tiles_ref[pl.ds(pl.multiple_of(u * SUB, SUB), SUB), :] = memory_ref[row].astype(jnp.float32)
            return c

        lax.fori_loop(0, TILE // 16, copy, 0)
        here = pl.ds(pl.multiple_of(t * TILE, TILE), TILE)
        rows_ref[...] = to_matrix(tiles_ref, 0, TILE)
        for j in range(width // COLS):
            for g in range(3):
                made_ref[:, (j * 3 + g) * COLS : (j * 3 + g + 1) * COLS] = jnp.dot(
                    rows_ref[...],
                    gru_ref[:, g * width + j * COLS : g * width + (j + 1) * COLS],
                    preferred_element_type=jnp.float32,
                )
        first = pltpu.make_async_copy(rows_ref, previous_ref.at[here], sems.at[0])
        second = pltpu.make_async_copy(made_ref, gates_ref.at[here], sems.at[1])
        first.start()
        second.start()
        first.wait()
        second.wait()
        return carry

    lax.fori_loop(0, steps, block, 0)


def message_kernel(
    place_ref,
    size_ref,
    rows_ref,
    feat_ref,
    w1_hbm,
    b1_ref,
    w2_hbm,
    b2_ref,
    out_ref,
    w1_ref,
    w2_ref,
    tiles_ref,
    inputs_ref,
    hidden_ref,
    sent_ref,
    sem,
    sems,
):
    events = feat_ref.shape[0]
    hid, width = w2_ref.shape
    group = 16
    parts = hid // COLS
    loads = []
    for source, target in ((w1_hbm, w1_ref), (w2_hbm, w2_ref)):
        for j in range(source.shape[1] // COLS):
            cols = pl.ds(j * COLS, COLS)
            load = pltpu.make_async_copy(source.at[:, cols], target.at[:, cols], sems.at[len(loads)])
            load.start()
            loads.append(load)
    for half in range(2):

        def fetch(i, c):
            for a in range(group):
                e = i * group + a
                tiles_ref[pl.ds(pl.multiple_of(e * SUB, SUB), SUB), :] = rows_ref[place_ref[half, e]].astype(
                    jnp.float32
                )
            return c

        lax.fori_loop(0, events // group, fetch, 0)
        inputs_ref[:, half * width : (half + 1) * width] = to_matrix(tiles_ref, 0, events)
    inputs_ref[:, 2 * width :] = feat_ref[...]
    for j in range(parts):
        cols = slice(j * COLS, (j + 1) * COLS)
        loads[j].wait()
        h = jnp.dot(inputs_ref[...], w1_ref[:, cols], preferred_element_type=jnp.float32) + b1_ref[:, cols]
        hidden_ref[:, cols] = jnp.maximum(h, 0.0).astype(jnp.bfloat16)
    for j in range(width // COLS):
        cols = slice(j * COLS, (j + 1) * COLS)
        loads[parts + j].wait()
        m = jnp.dot(hidden_ref[...], w2_ref[:, cols], preferred_element_type=jnp.float32) + b2_ref[:, cols]
        for c in range(COLS // LANES):
            tiles_ref[pl.ds(j * (COLS // LANES) + c, events, stride=SUB), :] = m[:, c * LANES : (c + 1) * LANES]

    def send(i, c):
        for a in range(group):
            e = i * group + a
            sent_ref[place_ref[1, e]] = tiles_ref[pl.ds(pl.multiple_of(e * SUB, SUB), SUB), :].astype(jnp.bfloat16)
        return c

    lax.fori_loop(0, events // group, send, 0)
    leave = pltpu.make_async_copy(sent_ref, out_ref, sem)
    leave.start()
    leave.wait()


def update_kernel(
    slot_ref,
    index_ref,
    count_ref,
    size_ref,
    incoming_ref,
    of_hbm,
    memory_hbm,
    previous_hbm,
    gates_hbm,
    gru_hbm,
    bias_ref,
    out_ref,
    of_ref,
    memory_ref,
    previous_ref,
    gates_ref,
    gru_ref,
    even_ref,
    odd_ref,
    aggregate_ref,
    renewed_ref,
    load_sems,
    sems,
):
    width = memory_ref.shape[1]
    taken = size_ref[0]
    nodes = size_ref[1]
    steps = jnp.maximum(pl.cdiv(nodes, TILE), 1)
    parts = width // COLS

    def load(source, target):
        copy = pltpu.make_async_copy(source, target, load_sems.at[len(loads)])
        loads.append(copy)
        return copy

    loads, early = [], []
    first = load(previous_hbm.at[pl.ds(0, TILE)], previous_ref)
    for j in range(parts):
        block_cols = pl.ds(j * 3 * COLS, 3 * COLS)
        group = [load(gates_hbm.at[pl.ds(0, TILE), block_cols], gates_ref.at[:, block_cols])]
        for g in range(3):
            cols = pl.ds(g * width + j * COLS, COLS)
            group.append(load(gru_hbm.at[:, cols], gru_ref.at[:, cols]))
        early.append(group)
    early[0].append(first)
    late = [load(of_hbm, of_ref), load(memory_hbm, memory_ref)]
    for copy in loads:
        copy.start()

    def clear(t, c):
        here = pl.ds(pl.multiple_of(t * TILE * SUB, TILE * SUB), TILE * SUB)
        even_ref[here, :] = jnp.zeros((TILE * SUB, LANES), jnp.float32)
        odd_ref[here, :] = jnp.zeros((TILE * SUB, LANES), jnp.float32)
        return c

    lax.fori_loop(0, steps, clear, 0)

    def add(i, c):
        for a in range(UNROLL):
            into = odd_ref if a % 2 else even_ref
            here = pl.ds(pl.multiple_of(index_ref[i * UNROLL + a] * SUB, SUB), SUB)
            into[here, :] += incoming_ref[slot_ref[i * UNROLL + a]].astype(jnp.float32)
        return c

    lax.fori_loop(0, pl.cdiv(taken, UNROLL), add, 0)

    def mean(i, c):
        for a in range(UNROLL):
            u = i * UNROLL + a
            here = pl.ds(pl.multiple_of(u * SUB, SUB), SUB)
            even_ref[here, :] = (even_ref[here, :] + odd_ref[here, :]) / count_ref[u].astype(jnp.float32)
        return c

    lax.fori_loop(0, pl.cdiv(nodes, UNROLL), mean, 0)

    def block(t, c):
        here = pl.ds(pl.multiple_of(t * TILE, TILE), TILE)

        @pl.when(t > 0)
        def _():
            again = [
                pltpu.make_async_copy(previous_hbm.at[here], previous_ref, load_sems.at[0]),
                pltpu.make_async_copy(gates_hbm.at[here], gates_ref, load_sems.at[1]),
            ]
            for copy in again:
                copy.start()
            for copy in again:
                copy.wait()

        aggregate_ref[...] = to_matrix(even_ref, pl.multiple_of(t * TILE, TILE), TILE)
        for j in range(parts):

            @pl.when(t == 0)
            def _(j=j):
                for copy in early[j]:
                    copy.wait()

            pre = []
            for g in range(3):
                cols = slice(g * width + j * COLS, g * width + (j + 1) * COLS)
                hid = gates_ref[:, (j * 3 + g) * COLS : (j * 3 + g + 1) * COLS]
                into = (
                    jnp.dot(aggregate_ref[...], gru_ref[:, cols], preferred_element_type=jnp.float32)
                    + bias_ref[:, cols]
                )
                pre.append((into, hid))
            reset = jax.nn.sigmoid(pre[0][0] + pre[0][1])
            update = jax.nn.sigmoid(pre[1][0] + pre[1][1])
            candidate = jnp.tanh(pre[2][0] + reset * pre[2][1])
            previous = previous_ref[:, j * COLS : (j + 1) * COLS].astype(jnp.float32)
            renewed = (1.0 - update) * candidate + update * previous
            renewed_ref[here, j * COLS : (j + 1) * COLS] = renewed.astype(jnp.bfloat16)
        return c

    lax.fori_loop(0, steps, block, 0)
    for copy in late:
        copy.wait()
    bands = sems.shape[0]
    rows = memory_ref.shape[0] // bands
    sends = []
    for i in range(bands):
        here = pl.ds(i * rows, rows)

        def place(t, i=i):
            of = of_ref[i * rows : (i + 1) * rows, :]
            lane = lax.broadcasted_iota(jnp.int32, (rows, TILE), 1) + t * TILE
            pick = (of == lane).astype(jnp.float32).astype(jnp.bfloat16)
            found = jnp.dot(
                pick, renewed_ref[t * TILE : (t + 1) * TILE, :], preferred_element_type=jnp.float32
            )
            mine = (of >= t * TILE) & (of < (t + 1) * TILE)
            kept = memory_ref[i * rows : (i + 1) * rows, :].astype(jnp.float32)
            memory_ref[i * rows : (i + 1) * rows, :] = jnp.where(mine, found, kept).astype(jnp.bfloat16)

        place(0)
        for t in range(1, renewed_ref.shape[0] // TILE):

            @pl.when(t < steps)
            def _():
                place(t)

        send = pltpu.make_async_copy(memory_ref.at[here], out_ref.at[here], sems.at[i])
        send.start()
        sends.append(send)
    for send in sends:
        send.wait()


def on_device(
    memory,
    ends_owner,
    ends_row,
    event_mask,
    edge_feat,
    msg_w1,
    msg_b1,
    msg_w2,
    msg_b2,
    gru_in,
    gru_hid,
    gru_bias,
):
    devices = lax.axis_size(AXES)
    events = ends_owner.shape[0]
    node_rows, width = memory.shape
    hid = msg_w2.shape[0]
    capacity = 5 * events // (2 * devices)
    slots = devices * capacity
    padded = pl.cdiv(slots, TILE) * TILE
    cells = width // LANES
    f32, bf16, i32 = jnp.float32, jnp.bfloat16, jnp.int32
    shape = jax.ShapeDtypeStruct

    ids, place = pl.pallas_call(
        lambda *refs: plan_kernel(capacity, *refs),
        out_shape=(shape((devices, LANES), i32), shape((2, events), i32)),
        in_specs=[VM, VM, VM],
        out_specs=(VM, VM),
        compiler_params=pltpu.CompilerParams(vmem_limit_bytes=WHOLE),
        name="plan",
    )(ends_owner.T, ends_row.T, event_mask.reshape(1, events))

    arrived = lax.all_to_all(
        ids.reshape(devices, 1, LANES), AXES, split_axis=0, concat_axis=0, tiled=True
    ).reshape(devices, LANES)
    tiles = memory.reshape(node_rows, cells, LANES)

    answers, codes = pl.pallas_call(
        lambda *refs: answer_kernel(capacity, *refs),
        out_shape=(shape((slots, cells, LANES), bf16), shape((SUB, devices), i32)),
        in_specs=[VM, VM],
        out_specs=(HBM, VM),
        scratch_shapes=[
            pltpu.VMEM((SUB, devices), i32),
            pltpu.SMEM((SUB, devices), i32),
            pltpu.VMEM((slots, cells, LANES), bf16),
            pltpu.SemaphoreType.DMA,
            pltpu.SemaphoreType.DMA((4,)),
        ],
        compiler_params=pltpu.CompilerParams(vmem_limit_bytes=ANSWER),
        name="answer",
    )(arrived, tiles)
    returned = lax.all_to_all(
        answers.reshape(devices, capacity, cells, LANES), AXES, split_axis=0, concat_axis=0, tiled=True
    ).reshape(slots, cells, LANES)

    slot, index, count, node, of, size = pl.pallas_call(
        lambda *refs: compact_kernel(capacity, padded, *refs),
        out_shape=(
            shape((1024,), i32),
            shape((1024,), i32),
            shape((1024,), i32),
            shape((1024,), i32),
            shape((node_rows,), i32),
            shape((8,), i32),
        ),
        in_specs=[SM],
        out_specs=(SM, SM, SM, SM, SM, SM),
        compiler_params=pltpu.CompilerParams(vmem_limit_bytes=WHOLE),
        cost_estimate=pl.CostEstimate(flops=4_000_000_000, bytes_accessed=20_000_000, transcendentals=0),
        name="compact",
    )(codes)

    previous, gates = pl.pallas_call(
        hidden_gates_kernel,
        out_shape=(shape((padded, width), bf16), shape((padded, 3 * width), f32)),
        in_specs=[SM, SM, VM, VM],
        out_specs=(HBM, HBM),
        scratch_shapes=[
            pltpu.VMEM((TILE * SUB, LANES), f32),
            pltpu.VMEM((TILE, width), bf16),
            pltpu.VMEM((TILE, 3 * width), f32),
            pltpu.SemaphoreType.DMA((2,)),
        ],
        compiler_params=pltpu.CompilerParams(vmem_limit_bytes=WHOLE),
        cost_estimate=pl.CostEstimate(flops=4_000_000_000, bytes_accessed=20_000_000, transcendentals=0),
        name="hidden_gates",
    )(node, size, tiles, gru_hid)

    outgoing = pl.pallas_call(
        message_kernel,
        out_shape=shape((slots, cells, LANES), bf16),
        in_specs=[SM, SM, VM, VM, HBM, VM, HBM, VM],
        out_specs=HBM,
        scratch_shapes=[
            pltpu.VMEM(msg_w1.shape, bf16),
            pltpu.VMEM(msg_w2.shape, bf16),
            pltpu.VMEM((events * SUB, LANES), f32),
            pltpu.VMEM((events, msg_w1.shape[0]), bf16),
            pltpu.VMEM((events, hid), bf16),
            pltpu.VMEM((slots, cells, LANES), bf16),
            pltpu.SemaphoreType.DMA,
            pltpu.SemaphoreType.DMA((hid // COLS + width // COLS,)),
        ],
        compiler_params=pltpu.CompilerParams(vmem_limit_bytes=MOST),
        name="message",
    )(place, size, returned, edge_feat, msg_w1, msg_b1.reshape(1, hid), msg_w2, msg_b2.reshape(1, width))
    incoming = lax.all_to_all(
        outgoing.reshape(devices, capacity, cells, LANES), AXES, split_axis=0, concat_axis=0, tiled=True
    ).reshape(slots, cells, LANES)

    return pl.pallas_call(
        update_kernel,
        out_shape=shape((node_rows, width), bf16),
        in_specs=[SM, SM, SM, SM, VM, HBM, HBM, HBM, HBM, HBM, VM],
        out_specs=HBM,
        scratch_shapes=[
            pltpu.VMEM((node_rows, 1), i32),
            pltpu.VMEM((node_rows, width), bf16),
            pltpu.VMEM((TILE, width), bf16),
            pltpu.VMEM((TILE, 3 * width), f32),
            pltpu.VMEM((width, 3 * width), bf16),
            pltpu.VMEM(((padded + 1) * SUB, LANES), f32),
            pltpu.VMEM(((padded + 1) * SUB, LANES), f32),
            pltpu.VMEM((TILE, width), bf16),
            pltpu.VMEM((padded, width), bf16),
            pltpu.SemaphoreType.DMA((4 * (width // COLS) + 3,)),
            pltpu.SemaphoreType.DMA((8,)),
        ],
        compiler_params=pltpu.CompilerParams(vmem_limit_bytes=MOST),
        name="update",
    )(
        slot,
        index,
        count,
        size,
        incoming,
        of.reshape(node_rows, 1),
        memory,
        previous,
        gates,
        gru_in,
        gru_bias.reshape(1, 3 * width),
    )


def solution(mesh):
    row = P(AXES, None)
    return jax.shard_map(
        on_device,
        mesh=mesh,
        in_specs=(row, row, row, P(AXES), row, P(), P(), P(), P(), P(), P(), P()),
        out_specs=row,
        check_vma=False,
    )
```

```python
import jax
import jax.numpy as jnp
from jax import lax
from jax.experimental import pallas as pl
from jax.experimental.pallas import tpu as pltpu
from jax.sharding import PartitionSpec as P

AXES = ("node", "tm")
LANES = 128
SUB = 8
ACTIVE = 1024
TILE = 256
COLS = 256
UNROLL = 16
MIB = 1 << 20
WHOLE = 58 * MIB
MOST = 51 * MIB
ANSWER = 51968 * 1024

VM = pl.BlockSpec(memory_space=pltpu.VMEM)
SM = pl.BlockSpec(memory_space=pltpu.SMEM)
HBM = pl.BlockSpec(memory_space=pltpu.HBM)


def plan_kernel(capacity, owner_ref, row_ref, mask_ref, ids_ref, place_ref):
    devices = ids_ref.shape[0]
    events = owner_ref.shape[1]
    ends = 2 * events
    owner = jnp.concatenate([owner_ref[0:1, :], owner_ref[1:2, :]], axis=1)
    code = jnp.concatenate([row_ref[0:1, :], row_ref[1:2, :] + ACTIVE * mask_ref[...]], axis=1)
    named = lax.broadcasted_iota(jnp.int32, (devices, ends), 0) == owner
    named_b = named.astype(jnp.float32).astype(jnp.bfloat16)
    before = (
        lax.broadcasted_iota(jnp.int32, (ends, ends), 0) < lax.broadcasted_iota(jnp.int32, (ends, ends), 1)
    ).astype(jnp.float32).astype(jnp.bfloat16)
    count = jnp.dot(named_b, before, preferred_element_type=jnp.float32)
    position = jnp.sum(jnp.where(named, count, 0.0), axis=0, keepdims=True).astype(jnp.int32)
    place = owner * capacity + position
    place_ref[0:1, :] = place[:, :events]
    place_ref[1:2, :] = place[:, events:]
    here = lax.broadcasted_iota(jnp.int32, (LANES, ends), 0) == position
    low = jnp.where(here, (code & 31).astype(jnp.float32), 0.0).astype(jnp.bfloat16)
    high = jnp.where(here, (code >> 5).astype(jnp.float32), 0.0).astype(jnp.bfloat16)
    contract = (((1,), (1,)), ((), ()))
    low_sum = lax.dot_general(named_b, low, contract, preferred_element_type=jnp.float32)
    high_sum = lax.dot_general(named_b, high, contract, preferred_element_type=jnp.float32)
    ids_ref[...] = (low_sum + 32.0 * high_sum).astype(jnp.int32)


def answer_kernel(capacity, ids_ref, memory_ref, out_ref, codes_ref, turned_ref, wanted_ref, rows_ref, load_sem, sems):
    devices = ids_ref.shape[0]
    turned = jnp.transpose(ids_ref[...])[:SUB, :]
    codes_ref[...] = turned
    turned_ref[...] = turned
    load = pltpu.make_async_copy(turned_ref, wanted_ref, load_sem)
    load.start()
    load.wait()
    group = 8
    chunks = sems.shape[0]
    part = devices // chunks
    sends = []
    for q in range(chunks):

        def step(i, carry):
            for a in range(group):
                p = q * part + i * group + a
                for k in range(capacity):
                    rows_ref[p * capacity + k] = memory_ref[wanted_ref[k, p] & (ACTIVE - 1)]
            return carry

        lax.fori_loop(0, part // group, step, 0)
        here = pl.ds(q * part * capacity, part * capacity)
        send = pltpu.make_async_copy(rows_ref.at[here], out_ref.at[here], sems.at[q])
        send.start()
        sends.append(send)
    for send in sends:
        send.wait()


def compact_kernel(capacity, spare_row, ids_ref, slot_ref, index_ref, count_ref, node_ref, of_ref, size_ref):
    devices = ids_ref.shape[1]
    rows = of_ref.shape[0]

    def clear(i, carry):
        for a in range(16):
            of_ref[i * 16 + a] = -1
        return carry

    lax.fori_loop(0, rows // 16, clear, 0)

    def step(p, carry):
        taken, nodes = carry
        for k in range(capacity):
            code = ids_ref[k, p]
            active = code >= ACTIVE
            node = code & (ACTIVE - 1)
            known = of_ref[node]
            fresh = active & (known < 0)
            index = jnp.where(known < 0, nodes, known)
            of_ref[node] = jnp.where(active, index, known)
            slot_ref[taken] = p * capacity + k
            index_ref[taken] = index
            old = count_ref[index]
            was = jnp.where(known < 0, 0, old)
            count_ref[index] = jnp.where(active, was + 1, was)
            node_ref[index] = jnp.where(fresh, node, jnp.where(known < 0, 0, node_ref[index]))
            taken = taken + active.astype(jnp.int32)
            nodes = nodes + fresh.astype(jnp.int32)
        return taken, nodes

    taken, nodes = lax.fori_loop(0, devices, step, (jnp.int32(0), jnp.int32(0)))
    size_ref[0] = taken
    size_ref[1] = nodes
    for a in range(UNROLL):
        slot_ref[taken + a] = 0
        index_ref[taken + a] = spare_row
        count_ref[nodes + a] = 1


def to_matrix(tiles_ref, start, rows):
    parts = [tiles_ref[pl.ds(start * SUB + c, rows, stride=SUB), :].astype(jnp.bfloat16) for c in range(SUB)]
    return jnp.concatenate(parts, axis=1)


def hidden_gates_kernel(
    node_ref, size_ref, memory_ref, gru_ref, previous_ref, gates_ref, tiles_ref, rows_ref, made_ref, sems
):
    steps = jnp.maximum(pl.cdiv(size_ref[1], TILE), 1)
    width = rows_ref.shape[1]

    def block(t, carry):
        def copy(i, c):
            for a in range(16):
                u = i * 16 + a
                row = node_ref[t * TILE + u] & (ACTIVE - 1)
                tiles_ref[pl.ds(pl.multiple_of(u * SUB, SUB), SUB), :] = memory_ref[row].astype(jnp.float32)
            return c

        lax.fori_loop(0, TILE // 16, copy, 0)
        here = pl.ds(pl.multiple_of(t * TILE, TILE), TILE)
        rows_ref[...] = to_matrix(tiles_ref, 0, TILE)
        for j in range(width // COLS):
            for g in range(3):
                made_ref[:, (j * 3 + g) * COLS : (j * 3 + g + 1) * COLS] = jnp.dot(
                    rows_ref[...],
                    gru_ref[:, g * width + j * COLS : g * width + (j + 1) * COLS],
                    preferred_element_type=jnp.float32,
                )
        first = pltpu.make_async_copy(rows_ref, previous_ref.at[here], sems.at[0])
        second = pltpu.make_async_copy(made_ref, gates_ref.at[here], sems.at[1])
        first.start()
        second.start()
        first.wait()
        second.wait()
        return carry

    lax.fori_loop(0, steps, block, 0)


def message_kernel(
    place_ref,
    rows_ref,
    feat_ref,
    w1_hbm,
    b1_ref,
    w2_hbm,
    b2_ref,
    out_ref,
    w1_ref,
    w2_ref,
    tiles_ref,
    inputs_ref,
    hidden_ref,
    sent_ref,
    sem,
    sems,
):
    events = feat_ref.shape[0]
    hid, width = w2_ref.shape
    group = 16
    loads = []
    for source, target in ((w1_hbm, w1_ref), (w2_hbm, w2_ref)):
        load = pltpu.make_async_copy(source, target, sems.at[len(loads)])
        load.start()
        loads.append(load)
    for half in range(2):

        def fetch(i, c):
            for a in range(group):
                e = i * group + a
                tiles_ref[pl.ds(pl.multiple_of(e * SUB, SUB), SUB), :] = rows_ref[place_ref[half, e]].astype(
                    jnp.float32
                )
            return c

        lax.fori_loop(0, events // group, fetch, 0)
        inputs_ref[:, half * width : (half + 1) * width] = to_matrix(tiles_ref, 0, events)
    inputs_ref[:, 2 * width :] = feat_ref[...]
    loads[0].wait()
    for j in range(hid // COLS):
        cols = slice(j * COLS, (j + 1) * COLS)
        h = jnp.dot(inputs_ref[...], w1_ref[:, cols], preferred_element_type=jnp.float32) + b1_ref[:, cols]
        hidden_ref[:, cols] = jnp.maximum(h, 0.0).astype(jnp.bfloat16)
    loads[1].wait()
    for j in range(width // COLS):
        cols = slice(j * COLS, (j + 1) * COLS)
        m = jnp.dot(hidden_ref[...], w2_ref[:, cols], preferred_element_type=jnp.float32) + b2_ref[:, cols]
        for c in range(COLS // LANES):
            tiles_ref[pl.ds(j * (COLS // LANES) + c, events, stride=SUB), :] = m[:, c * LANES : (c + 1) * LANES]

    def send(i, c):
        for a in range(group):
            e = i * group + a
            sent_ref[place_ref[1, e]] = tiles_ref[pl.ds(pl.multiple_of(e * SUB, SUB), SUB), :].astype(jnp.bfloat16)
        return c

    lax.fori_loop(0, events // group, send, 0)
    leave = pltpu.make_async_copy(sent_ref, out_ref, sem)
    leave.start()
    leave.wait()


def update_kernel(
    slot_ref,
    index_ref,
    count_ref,
    size_ref,
    incoming_ref,
    of_ref,
    memory_hbm,
    previous_hbm,
    gates_hbm,
    gru_hbm,
    bias_ref,
    out_ref,
    memory_ref,
    previous_ref,
    gates_ref,
    gru_ref,
    even_ref,
    odd_ref,
    aggregate_ref,
    renewed_ref,
    load_sems,
    sems,
):
    width = memory_ref.shape[1]
    taken = size_ref[0]
    nodes = size_ref[1]
    steps = jnp.maximum(pl.cdiv(nodes, TILE), 1)
    parts = width // COLS

    def load(source, target):
        copy = pltpu.make_async_copy(source, target, load_sems.at[len(loads)])
        loads.append(copy)
        return copy

    loads = []
    early = [
        load(gru_hbm, gru_ref),
        load(gates_hbm.at[pl.ds(0, TILE)], gates_ref),
        load(previous_hbm.at[pl.ds(0, TILE)], previous_ref),
    ]
    late = load(memory_hbm, memory_ref)
    for copy in loads:
        copy.start()

    def clear(t, c):
        here = pl.ds(pl.multiple_of(t * TILE * SUB, TILE * SUB), TILE * SUB)
        even_ref[here, :] = jnp.zeros((TILE * SUB, LANES), jnp.float32)
        odd_ref[here, :] = jnp.zeros((TILE * SUB, LANES), jnp.float32)
        return c

    lax.fori_loop(0, steps, clear, 0)

    def add(i, c):
        for a in range(UNROLL):
            into = odd_ref if a % 2 else even_ref
            here = pl.ds(pl.multiple_of(index_ref[i * UNROLL + a] * SUB, SUB), SUB)
            into[here, :] += incoming_ref[slot_ref[i * UNROLL + a]].astype(jnp.float32)
        return c

    lax.fori_loop(0, pl.cdiv(taken, UNROLL), add, 0)

    def mean(i, c):
        for a in range(UNROLL):
            u = i * UNROLL + a
            here = pl.ds(pl.multiple_of(u * SUB, SUB), SUB)
            even_ref[here, :] = (even_ref[here, :] + odd_ref[here, :]) / count_ref[u].astype(jnp.float32)
        return c

    lax.fori_loop(0, pl.cdiv(nodes, UNROLL), mean, 0)

    def block(t, c):
        here = pl.ds(pl.multiple_of(t * TILE, TILE), TILE)

        @pl.when(t > 0)
        def _():
            again = [
                pltpu.make_async_copy(gates_hbm.at[here], gates_ref, load_sems.at[1]),
                pltpu.make_async_copy(previous_hbm.at[here], previous_ref, load_sems.at[2]),
            ]
            for copy in again:
                copy.start()
            for copy in again:
                copy.wait()

        aggregate_ref[...] = to_matrix(even_ref, pl.multiple_of(t * TILE, TILE), TILE)
        for j in range(parts):
            pre = []
            for g in range(3):
                cols = slice(g * width + j * COLS, g * width + (j + 1) * COLS)
                hid = gates_ref[:, (j * 3 + g) * COLS : (j * 3 + g + 1) * COLS]
                into = (
                    jnp.dot(aggregate_ref[...], gru_ref[:, cols], preferred_element_type=jnp.float32)
                    + bias_ref[:, cols]
                )
                pre.append((into, hid))
            reset = jax.nn.sigmoid(pre[0][0] + pre[0][1])
            update = jax.nn.sigmoid(pre[1][0] + pre[1][1])
            candidate = jnp.tanh(pre[2][0] + reset * pre[2][1])
            previous = previous_ref[:, j * COLS : (j + 1) * COLS].astype(jnp.float32)
            renewed = (1.0 - update) * candidate + update * previous
            renewed_ref[here, j * COLS : (j + 1) * COLS] = renewed.astype(jnp.bfloat16)
        return c

    for copy in early:
        copy.wait()
    lax.fori_loop(0, steps, block, 0)
    late.wait()
    bands = sems.shape[0]
    rows = memory_ref.shape[0] // bands
    sends = []
    for i in range(bands):
        here = pl.ds(i * rows, rows)

        def place(t, i=i):
            of = of_ref[i * rows : (i + 1) * rows, :]
            lane = lax.broadcasted_iota(jnp.int32, (rows, TILE), 1) + t * TILE
            pick = (of == lane).astype(jnp.float32).astype(jnp.bfloat16)
            found = jnp.dot(
                pick, renewed_ref[t * TILE : (t + 1) * TILE, :], preferred_element_type=jnp.float32
            )
            mine = (of >= t * TILE) & (of < (t + 1) * TILE)
            kept = memory_ref[i * rows : (i + 1) * rows, :].astype(jnp.float32)
            memory_ref[i * rows : (i + 1) * rows, :] = jnp.where(mine, found, kept).astype(jnp.bfloat16)

        place(0)
        for t in range(1, renewed_ref.shape[0] // TILE):

            @pl.when(t < steps)
            def _():
                place(t)

        send = pltpu.make_async_copy(memory_ref.at[here], out_ref.at[here], sems.at[i])
        send.start()
        sends.append(send)
    for send in sends:
        send.wait()


def on_device(
    memory,
    ends_owner,
    ends_row,
    event_mask,
    edge_feat,
    msg_w1,
    msg_b1,
    msg_w2,
    msg_b2,
    gru_in,
    gru_hid,
    gru_bias,
):
    devices = lax.axis_size(AXES)
    events = ends_owner.shape[0]
    node_rows, width = memory.shape
    hid = msg_w2.shape[0]
    capacity = 5 * events // (2 * devices)
    slots = devices * capacity
    padded = pl.cdiv(slots, TILE) * TILE
    cells = width // LANES
    f32, bf16, i32 = jnp.float32, jnp.bfloat16, jnp.int32
    shape = jax.ShapeDtypeStruct

    ids, place = pl.pallas_call(
        lambda *refs: plan_kernel(capacity, *refs),
        out_shape=(shape((devices, LANES), i32), shape((2, events), i32)),
        in_specs=[VM, VM, VM],
        out_specs=(VM, VM),
        compiler_params=pltpu.CompilerParams(vmem_limit_bytes=WHOLE),
        name="plan",
    )(ends_owner.T, ends_row.T, event_mask.reshape(1, events))

    arrived = lax.all_to_all(
        ids.reshape(devices, 1, LANES), AXES, split_axis=0, concat_axis=0, tiled=True
    ).reshape(devices, LANES)
    tiles = memory.reshape(node_rows, cells, LANES)

    answers, codes = pl.pallas_call(
        lambda *refs: answer_kernel(capacity, *refs),
        out_shape=(shape((slots, cells, LANES), bf16), shape((SUB, devices), i32)),
        in_specs=[VM, VM],
        out_specs=(HBM, VM),
        scratch_shapes=[
            pltpu.VMEM((SUB, devices), i32),
            pltpu.SMEM((SUB, devices), i32),
            pltpu.VMEM((slots, cells, LANES), bf16),
            pltpu.SemaphoreType.DMA,
            pltpu.SemaphoreType.DMA((4,)),
        ],
        compiler_params=pltpu.CompilerParams(vmem_limit_bytes=ANSWER),
        name="answer",
    )(arrived, tiles)
    returned = lax.all_to_all(
        answers.reshape(devices, capacity, cells, LANES), AXES, split_axis=0, concat_axis=0, tiled=True
    ).reshape(slots, cells, LANES)

    slot, index, count, node, of, size = pl.pallas_call(
        lambda *refs: compact_kernel(capacity, padded, *refs),
        out_shape=(
            shape((1024,), i32),
            shape((1024,), i32),
            shape((1024,), i32),
            shape((1024,), i32),
            shape((node_rows,), i32),
            shape((8,), i32),
        ),
        in_specs=[SM],
        out_specs=(SM, SM, SM, SM, SM, SM),
        compiler_params=pltpu.CompilerParams(vmem_limit_bytes=WHOLE),
        cost_estimate=pl.CostEstimate(flops=4_000_000_000, bytes_accessed=20_000_000, transcendentals=0),
        name="compact",
    )(codes)

    previous, gates = pl.pallas_call(
        hidden_gates_kernel,
        out_shape=(shape((padded, width), bf16), shape((padded, 3 * width), f32)),
        in_specs=[SM, SM, VM, VM],
        out_specs=(HBM, HBM),
        scratch_shapes=[
            pltpu.VMEM((TILE * SUB, LANES), f32),
            pltpu.VMEM((TILE, width), bf16),
            pltpu.VMEM((TILE, 3 * width), f32),
            pltpu.SemaphoreType.DMA((2,)),
        ],
        compiler_params=pltpu.CompilerParams(vmem_limit_bytes=WHOLE),
        cost_estimate=pl.CostEstimate(flops=4_000_000_000, bytes_accessed=20_000_000, transcendentals=0),
        name="hidden_gates",
    )(node, size, tiles, gru_hid)

    returned, size = lax.optimization_barrier((returned, size))
    outgoing = pl.pallas_call(
        message_kernel,
        out_shape=shape((slots, cells, LANES), bf16),
        in_specs=[SM, VM, VM, HBM, VM, HBM, VM],
        out_specs=HBM,
        scratch_shapes=[
            pltpu.VMEM(msg_w1.shape, bf16),
            pltpu.VMEM(msg_w2.shape, bf16),
            pltpu.VMEM((events * SUB, LANES), f32),
            pltpu.VMEM((events, msg_w1.shape[0]), bf16),
            pltpu.VMEM((events, hid), bf16),
            pltpu.VMEM((slots, cells, LANES), bf16),
            pltpu.SemaphoreType.DMA,
            pltpu.SemaphoreType.DMA((2,)),
        ],
        compiler_params=pltpu.CompilerParams(vmem_limit_bytes=MOST),
        name="message",
    )(place, returned, edge_feat, msg_w1, msg_b1.reshape(1, hid), msg_w2, msg_b2.reshape(1, width))
    incoming = lax.all_to_all(
        outgoing.reshape(devices, capacity, cells, LANES), AXES, split_axis=0, concat_axis=0, tiled=True
    ).reshape(slots, cells, LANES)

    return pl.pallas_call(
        update_kernel,
        out_shape=shape((node_rows, width), bf16),
        in_specs=[SM, SM, SM, SM, VM, VM, HBM, HBM, HBM, HBM, VM],
        out_specs=HBM,
        scratch_shapes=[
            pltpu.VMEM((node_rows, width), bf16),
            pltpu.VMEM((TILE, width), bf16),
            pltpu.VMEM((TILE, 3 * width), f32),
            pltpu.VMEM((width, 3 * width), bf16),
            pltpu.VMEM(((padded + 1) * SUB, LANES), f32),
            pltpu.VMEM(((padded + 1) * SUB, LANES), f32),
            pltpu.VMEM((TILE, width), bf16),
            pltpu.VMEM((padded, width), bf16),
            pltpu.SemaphoreType.DMA((4,)),
            pltpu.SemaphoreType.DMA((8,)),
        ],
        compiler_params=pltpu.CompilerParams(vmem_limit_bytes=MOST),
        name="update",
    )(
        slot,
        index,
        count,
        size,
        incoming,
        of.reshape(node_rows, 1),
        memory,
        previous,
        gates,
        gru_in,
        gru_bias.reshape(1, 3 * width),
    )


def solution(mesh):
    row = P(AXES, None)
    return jax.shard_map(
        on_device,
        mesh=mesh,
        in_specs=(row, row, row, P(AXES), row, P(), P(), P(), P(), P(), P(), P()),
        out_specs=row,
        check_vma=False,
    )
```

```python
import jax
import jax.numpy as jnp
from jax import lax
from jax.experimental import pallas as pl
from jax.experimental.pallas import tpu as pltpu
from jax.sharding import PartitionSpec as P

AXES = ("node", "tm")
LANES = 128
SUB = 8
ACTIVE = 1024
TILE = 256
COLS = 256
GATES = jnp.bfloat16
UNROLL = 16
BAND = 512
MIB = 1 << 20
WHOLE = 58 * MIB
MOST = 51 * MIB
ANSWER = 51968 * 1024

VM = pl.BlockSpec(memory_space=pltpu.VMEM)
SM = pl.BlockSpec(memory_space=pltpu.SMEM)
HBM = pl.BlockSpec(memory_space=pltpu.HBM)


def plan_kernel(capacity, owner_ref, row_ref, mask_ref, ids_ref, place_ref):
    devices = ids_ref.shape[0]
    events = owner_ref.shape[1]
    ends = 2 * events
    owner = jnp.concatenate([owner_ref[0:1, :], owner_ref[1:2, :]], axis=1)
    code = jnp.concatenate([row_ref[0:1, :], row_ref[1:2, :] + ACTIVE * mask_ref[...]], axis=1)
    named = lax.broadcasted_iota(jnp.int32, (devices, ends), 0) == owner
    named_b = named.astype(jnp.float32).astype(jnp.bfloat16)
    block = (LANES, LANES)
    before = lax.broadcasted_iota(jnp.int32, block, 0) < lax.broadcasted_iota(jnp.int32, block, 1)
    table = jnp.concatenate([before.astype(jnp.float32), jnp.ones(block, jnp.float32)], axis=1).astype(jnp.bfloat16)
    total = jnp.zeros((devices, LANES), jnp.float32)
    counts = []
    for i in range(ends // LANES):
        both = jnp.dot(named_b[:, i * LANES : (i + 1) * LANES], table, preferred_element_type=jnp.float32)
        counts.append(both[:, :LANES] + total)
        total = total + both[:, LANES:]
    count = jnp.concatenate(counts, axis=1)
    position = jnp.sum(jnp.where(named, count, 0.0), axis=0, keepdims=True).astype(jnp.int32)
    place = owner * capacity + position
    place_ref[0:1, :] = place[:, :events]
    place_ref[1:2, :] = place[:, events:]
    here = lax.broadcasted_iota(jnp.int32, (LANES, ends), 0) == position
    low = jnp.where(here, (code & 31).astype(jnp.float32), 0.0).astype(jnp.bfloat16)
    high = jnp.where(here, (code >> 5).astype(jnp.float32), 0.0).astype(jnp.bfloat16)
    contract = (((1,), (1,)), ((), ()))
    low_sum = lax.dot_general(named_b, low, contract, preferred_element_type=jnp.float32)
    high_sum = lax.dot_general(named_b, high, contract, preferred_element_type=jnp.float32)
    ids_ref[...] = (low_sum + 32.0 * high_sum).astype(jnp.int32)


def answer_kernel(
    capacity,
    ids_ref,
    memory_hbm,
    out_ref,
    codes_ref,
    memory_ref,
    turned_ref,
    wanted_ref,
    rows_ref,
    memory_sem,
    load_sem,
    sems,
):
    devices = ids_ref.shape[0]
    memory_load = pltpu.make_async_copy(memory_hbm, memory_ref, memory_sem)
    memory_load.start()
    turned = jnp.transpose(ids_ref[...])[:SUB, :]
    codes_ref[...] = turned
    turned_ref[...] = turned
    load = pltpu.make_async_copy(turned_ref, wanted_ref, load_sem)
    load.start()
    load.wait()
    memory_load.wait()
    group = 8
    chunks = sems.shape[0]
    part = devices // chunks
    sends = []
    for q in range(chunks):

        def step(i, carry):
            for a in range(group):
                p = q * part + i * group + a
                for k in range(capacity):
                    rows_ref[p * capacity + k] = memory_ref[wanted_ref[k, p] & (ACTIVE - 1)]
            return carry

        lax.fori_loop(0, part // group, step, 0)
        here = pl.ds(q * part * capacity, part * capacity)
        send = pltpu.make_async_copy(rows_ref.at[here], out_ref.at[here], sems.at[q])
        send.start()
        sends.append(send)
    for send in sends:
        send.wait()


def compact_kernel(
    capacity, spare_row, codes_ref, slot_ref, index_ref, count_ref, node_ref, of_ref, size_ref, ids_ref, load_sem
):
    devices = ids_ref.shape[1]
    rows = of_ref.shape[0]
    load = pltpu.make_async_copy(codes_ref, ids_ref, load_sem)
    load.start()
    load.wait()

    def clear(i, carry):
        for a in range(16):
            of_ref[i * 16 + a] = -1
        return carry

    lax.fori_loop(0, rows // 16, clear, 0)

    def step(p, carry):
        taken, nodes = carry
        for k in range(capacity):
            code = ids_ref[k, p]
            active = code >= ACTIVE
            node = code & (ACTIVE - 1)
            known = of_ref[node]
            fresh = active & (known < 0)
            index = jnp.where(known < 0, nodes, known)
            of_ref[node] = jnp.where(active, index, known)
            slot_ref[taken] = p * capacity + k
            index_ref[taken] = index
            old = count_ref[index]
            was = jnp.where(known < 0, 0, old)
            count_ref[index] = jnp.where(active, was + 1, was)
            node_ref[index] = jnp.where(fresh, node, jnp.where(known < 0, 0, node_ref[index]))
            taken = taken + active.astype(jnp.int32)
            nodes = nodes + fresh.astype(jnp.int32)
        return taken, nodes

    taken, nodes = lax.fori_loop(0, devices, step, (jnp.int32(0), jnp.int32(0)))
    size_ref[0] = taken
    size_ref[1] = nodes
    for a in range(UNROLL):
        slot_ref[taken + a] = 0
        index_ref[taken + a] = spare_row
        count_ref[nodes + a] = 1


def to_matrix(tiles_ref, start, rows):
    parts = [tiles_ref[pl.ds(start * SUB + c, rows, stride=SUB), :].astype(jnp.bfloat16) for c in range(SUB)]
    return jnp.concatenate(parts, axis=1)


def hidden_gates_kernel(
    node_ref,
    size_ref,
    memory_ref,
    gru_ref,
    plain_ref,
    of_ref,
    previous_ref,
    gates_ref,
    kept_ref,
    tiles_ref,
    rows_ref,
    made_ref,
    left_ref,
    sems,
):
    left_ref[...] = jnp.where(of_ref[...] < 0, plain_ref[...].astype(jnp.float32), 0.0).astype(jnp.bfloat16)
    third = pltpu.make_async_copy(left_ref, kept_ref, sems.at[2])
    third.start()
    steps = jnp.maximum(pl.cdiv(size_ref[1], TILE), 1)
    width = rows_ref.shape[1]

    def block(t, carry):
        def copy(i, c):
            for a in range(16):
                u = i * 16 + a
                row = node_ref[t * TILE + u] & (ACTIVE - 1)
                tiles_ref[pl.ds(pl.multiple_of(u * SUB, SUB), SUB), :] = memory_ref[row].astype(jnp.float32)
            return c

        lax.fori_loop(0, TILE // 16, copy, 0)
        here = pl.ds(pl.multiple_of(t * TILE, TILE), TILE)
        rows_ref[...] = to_matrix(tiles_ref, 0, TILE)
        for j in range(width // COLS):
            for g in range(3):
                made_ref[:, (j * 3 + g) * COLS : (j * 3 + g + 1) * COLS] = jnp.dot(
                    rows_ref[...],
                    gru_ref[:, g * width + j * COLS : g * width + (j + 1) * COLS],
                    preferred_element_type=jnp.float32,
                ).astype(made_ref.dtype)
        first = pltpu.make_async_copy(rows_ref, previous_ref.at[here], sems.at[0])
        second = pltpu.make_async_copy(made_ref, gates_ref.at[here], sems.at[1])
        first.start()
        second.start()
        first.wait()
        second.wait()
        return carry

    lax.fori_loop(0, steps, block, 0)
    third.wait()


def message_kernel(
    place_ref,
    rows_ref,
    feat_ref,
    w1_hbm,
    b1_ref,
    w2_hbm,
    b2_ref,
    out_ref,
    w1_ref,
    w2_ref,
    tiles_ref,
    inputs_ref,
    hidden_ref,
    sent_ref,
    sem,
    sems,
):
    events = feat_ref.shape[0]
    hid, width = w2_ref.shape
    group = 16
    loads = []
    for source, target in ((w1_hbm, w1_ref), (w2_hbm, w2_ref)):
        load = pltpu.make_async_copy(source, target, sems.at[len(loads)])
        load.start()
        loads.append(load)
    for half in range(2):

        def fetch(i, c):
            for a in range(group):
                e = i * group + a
                tiles_ref[pl.ds(pl.multiple_of(e * SUB, SUB), SUB), :] = rows_ref[place_ref[half, e]].astype(
                    jnp.float32
                )
            return c

        lax.fori_loop(0, events // group, fetch, 0)
        inputs_ref[:, half * width : (half + 1) * width] = to_matrix(tiles_ref, 0, events)
    inputs_ref[:, 2 * width :] = feat_ref[...]
    loads[0].wait()
    for j in range(hid // COLS):
        cols = slice(j * COLS, (j + 1) * COLS)
        h = jnp.dot(inputs_ref[...], w1_ref[:, cols], preferred_element_type=jnp.float32) + b1_ref[:, cols]
        hidden_ref[:, cols] = jnp.maximum(h, 0.0).astype(jnp.bfloat16)
    loads[1].wait()
    for j in range(width // COLS):
        cols = slice(j * COLS, (j + 1) * COLS)
        m = jnp.dot(hidden_ref[...], w2_ref[:, cols], preferred_element_type=jnp.float32) + b2_ref[:, cols]
        for c in range(COLS // LANES):
            tiles_ref[pl.ds(j * (COLS // LANES) + c, events, stride=SUB), :] = m[:, c * LANES : (c + 1) * LANES]

    def send(i, c):
        for a in range(group):
            e = i * group + a
            sent_ref[place_ref[1, e]] = tiles_ref[pl.ds(pl.multiple_of(e * SUB, SUB), SUB), :].astype(jnp.bfloat16)
        return c

    lax.fori_loop(0, events // group, send, 0)
    leave = pltpu.make_async_copy(sent_ref, out_ref, sem)
    leave.start()
    leave.wait()


def update_kernel(
    slot_ref,
    index_ref,
    count_ref,
    size_ref,
    incoming_ref,
    of_ref,
    kept_hbm,
    previous_hbm,
    gates_hbm,
    gru_hbm,
    bias_ref,
    out_ref,
    final_ref,
    previous_ref,
    gates_ref,
    gru_ref,
    even_ref,
    odd_ref,
    aggregate_ref,
    pick_ref,
    load_sems,
    sems,
):
    width = final_ref.shape[1]
    taken = size_ref[0]
    nodes = size_ref[1]
    steps = jnp.maximum(pl.cdiv(nodes, TILE), 1)
    half = width // 2
    first_tile = pl.ds(0, TILE)
    halves = []
    for h in range(2):
        loads = [(gates_hbm.at[first_tile, pl.ds(h * 3 * half, 3 * half)], gates_ref.at[:, pl.ds(h * 3 * half, 3 * half)])]
        for g in range(3):
            cols = pl.ds(g * width + h * half, half)
            loads.append((gru_hbm.at[:, cols], gru_ref.at[:, cols]))
        if h == 0:
            loads.append((previous_hbm.at[first_tile], previous_ref))
        else:
            loads.append((kept_hbm, final_ref))
        halves.append([pltpu.make_async_copy(a, b, load_sems.at[h, i]) for i, (a, b) in enumerate(loads)])
    for copy in halves[0] + halves[1]:
        copy.start()

    def clear(t, c):
        here = pl.ds(pl.multiple_of(t * TILE * SUB, TILE * SUB), TILE * SUB)
        even_ref[here, :] = jnp.zeros((TILE * SUB, LANES), jnp.float32)
        odd_ref[here, :] = jnp.zeros((TILE * SUB, LANES), jnp.float32)
        return c

    lax.fori_loop(0, steps, clear, 0)

    def add(i, c):
        for a in range(UNROLL):
            into = odd_ref if a % 2 else even_ref
            here = pl.ds(pl.multiple_of(index_ref[i * UNROLL + a] * SUB, SUB), SUB)
            into[here, :] += incoming_ref[slot_ref[i * UNROLL + a]].astype(jnp.float32)
        return c

    lax.fori_loop(0, pl.cdiv(taken, UNROLL), add, 0)
    def mean(i, c):
        for a in range(UNROLL):
            u = i * UNROLL + a
            here = pl.ds(pl.multiple_of(u * SUB, SUB), SUB)
            even_ref[here, :] = (even_ref[here, :] + odd_ref[here, :]) / count_ref[u].astype(jnp.float32)
        return c

    lax.fori_loop(0, pl.cdiv(nodes, UNROLL), mean, 0)

    def prepare(t):
        aggregate_ref[...] = to_matrix(even_ref, pl.multiple_of(t * TILE, TILE), TILE)
        lane = lax.broadcasted_iota(jnp.int32, (of_ref.shape[0], TILE), 1) + t * TILE
        pick_ref[...] = (of_ref[...] == lane).astype(jnp.float32).astype(jnp.bfloat16)

    def renew(j):
        pre = []
        for g in range(3):
            cols = slice(g * width + j * COLS, g * width + (j + 1) * COLS)
            hid = gates_ref[:, (j * 3 + g) * COLS : (j * 3 + g + 1) * COLS].astype(jnp.float32)
            into = jnp.dot(aggregate_ref[...], gru_ref[:, cols], preferred_element_type=jnp.float32) + bias_ref[:, cols]
            pre.append((into, hid))
        reset = jax.nn.sigmoid(pre[0][0] + pre[0][1])
        update = jax.nn.sigmoid(pre[1][0] + pre[1][1])
        candidate = jnp.tanh(pre[2][0] + reset * pre[2][1])
        previous = previous_ref[:, j * COLS : (j + 1) * COLS].astype(jnp.float32)
        return ((1.0 - update) * candidate + update * previous).astype(jnp.bfloat16)

    def place(j, renewed):
        cols = slice(j * COLS, (j + 1) * COLS)
        for i in range(final_ref.shape[0] // BAND):
            rows = slice(i * BAND, (i + 1) * BAND)
            found = jnp.dot(pick_ref[rows, :], renewed, preferred_element_type=jnp.float32)
            final_ref[rows, cols] = found.astype(jnp.bfloat16) + final_ref[rows, cols]

    per = half // COLS
    prepare(0)
    for copy in halves[0]:
        copy.wait()
    made = [renew(j) for j in range(per)]
    for copy in halves[1]:
        copy.wait()
    sends = [
        pltpu.make_async_copy(
            final_ref.at[:, pl.ds(h * half, half)], out_ref.at[:, pl.ds(h * half, half)], sems.at[h]
        )
        for h in range(2)
    ]
    for j in range(per):
        place(j, made[j])

    @pl.when(steps == 1)
    def _():
        sends[0].start()

    for j in range(per, 2 * per):
        place(j, renew(j))

    @pl.when(steps > 1)
    def _():
        def block(t, c):
            here = pl.ds(pl.multiple_of(t * TILE, TILE), TILE)
            again = [
                pltpu.make_async_copy(gates_hbm.at[here], gates_ref, load_sems.at[0, 0]),
                pltpu.make_async_copy(previous_hbm.at[here], previous_ref, load_sems.at[0, 1]),
            ]
            for copy in again:
                copy.start()
            prepare(t)
            for copy in again:
                copy.wait()
            for j in range(2 * per):
                place(j, renew(j))
            return c

        lax.fori_loop(1, steps, block, 0)
        sends[0].start()

    sends[1].start()
    for send in sends:
        send.wait()


def on_device(
    memory,
    ends_owner,
    ends_row,
    event_mask,
    edge_feat,
    msg_w1,
    msg_b1,
    msg_w2,
    msg_b2,
    gru_in,
    gru_hid,
    gru_bias,
):
    devices = lax.axis_size(AXES)
    events = ends_owner.shape[0]
    node_rows, width = memory.shape
    hid = msg_w2.shape[0]
    capacity = 5 * events // (2 * devices)
    slots = devices * capacity
    padded = pl.cdiv(slots, TILE) * TILE
    cells = width // LANES
    f32, bf16, i32 = jnp.float32, jnp.bfloat16, jnp.int32
    shape = jax.ShapeDtypeStruct

    ids, place = pl.pallas_call(
        lambda *refs: plan_kernel(capacity, *refs),
        out_shape=(shape((devices, LANES), i32), shape((2, events), i32)),
        in_specs=[VM, VM, VM],
        out_specs=(VM, VM),
        compiler_params=pltpu.CompilerParams(vmem_limit_bytes=WHOLE),
        name="plan",
    )(ends_owner.T, ends_row.T, event_mask.reshape(1, events))

    arrived = lax.all_to_all(
        ids.reshape(devices, 1, LANES), AXES, split_axis=0, concat_axis=0, tiled=True
    ).reshape(devices, LANES)
    tiles = memory.reshape(node_rows, cells, LANES)

    answers, codes = pl.pallas_call(
        lambda *refs: answer_kernel(capacity, *refs),
        out_shape=(shape((slots, cells, LANES), bf16), shape((SUB, devices), i32)),
        in_specs=[VM, HBM],
        out_specs=(HBM, VM),
        scratch_shapes=[
            pltpu.VMEM((node_rows, cells, LANES), bf16),
            pltpu.VMEM((SUB, devices), i32),
            pltpu.SMEM((SUB, devices), i32),
            pltpu.VMEM((slots, cells, LANES), bf16),
            pltpu.SemaphoreType.DMA,
            pltpu.SemaphoreType.DMA,
            pltpu.SemaphoreType.DMA((4,)),
        ],
        compiler_params=pltpu.CompilerParams(vmem_limit_bytes=ANSWER),
        name="answer",
    )(arrived, tiles)
    returned = lax.all_to_all(
        answers.reshape(devices, capacity, cells, LANES), AXES, split_axis=0, concat_axis=0, tiled=True
    ).reshape(slots, cells, LANES)

    slot, index, count, node, of, size = pl.pallas_call(
        lambda *refs: compact_kernel(capacity, padded, *refs),
        out_shape=(
            shape((1024,), i32),
            shape((1024,), i32),
            shape((1024,), i32),
            shape((1024,), i32),
            shape((node_rows,), i32),
            shape((8,), i32),
        ),
        in_specs=[VM],
        out_specs=(SM, SM, SM, SM, SM, SM),
        scratch_shapes=[pltpu.SMEM((SUB, devices), i32), pltpu.SemaphoreType.DMA],
        compiler_params=pltpu.CompilerParams(vmem_limit_bytes=MOST),
        cost_estimate=pl.CostEstimate(flops=4_000_000_000, bytes_accessed=20_000_000, transcendentals=0),
        name="compact",
    )(codes)

    of = of.reshape(node_rows, 1)
    previous, gates, kept = pl.pallas_call(
        hidden_gates_kernel,
        out_shape=(
            shape((padded, width), bf16),
            shape((padded, 3 * width), GATES),
            shape((node_rows, width), bf16),
        ),
        in_specs=[SM, SM, VM, VM, VM, VM],
        out_specs=(HBM, HBM, HBM),
        scratch_shapes=[
            pltpu.VMEM((TILE * SUB, LANES), f32),
            pltpu.VMEM((TILE, width), bf16),
            pltpu.VMEM((TILE, 3 * width), GATES),
            pltpu.VMEM((node_rows, width), bf16),
            pltpu.SemaphoreType.DMA((3,)),
        ],
        compiler_params=pltpu.CompilerParams(vmem_limit_bytes=WHOLE),
        cost_estimate=pl.CostEstimate(flops=4_000_000_000, bytes_accessed=20_000_000, transcendentals=0),
        name="hidden_gates",
    )(node, size, tiles, gru_hid, memory, of)

    returned, size = lax.optimization_barrier((returned, size))
    outgoing = pl.pallas_call(
        message_kernel,
        out_shape=shape((slots, cells, LANES), bf16),
        in_specs=[SM, VM, VM, HBM, VM, HBM, VM],
        out_specs=HBM,
        scratch_shapes=[
            pltpu.VMEM(msg_w1.shape, bf16),
            pltpu.VMEM(msg_w2.shape, bf16),
            pltpu.VMEM((events * SUB, LANES), f32),
            pltpu.VMEM((events, msg_w1.shape[0]), bf16),
            pltpu.VMEM((events, hid), bf16),
            pltpu.VMEM((slots, cells, LANES), bf16),
            pltpu.SemaphoreType.DMA,
            pltpu.SemaphoreType.DMA((2,)),
        ],
        compiler_params=pltpu.CompilerParams(vmem_limit_bytes=MOST),
        name="message",
    )(place, returned, edge_feat, msg_w1, msg_b1.reshape(1, hid), msg_w2, msg_b2.reshape(1, width))
    incoming = lax.all_to_all(
        outgoing.reshape(devices, capacity, cells, LANES), AXES, split_axis=0, concat_axis=0, tiled=True
    ).reshape(slots, cells, LANES)

    return pl.pallas_call(
        update_kernel,
        out_shape=shape((node_rows, width), bf16),
        in_specs=[SM, SM, SM, SM, VM, VM, HBM, HBM, HBM, HBM, VM],
        out_specs=HBM,
        scratch_shapes=[
            pltpu.VMEM((node_rows, width), bf16),
            pltpu.VMEM((TILE, width), bf16),
            pltpu.VMEM((TILE, 3 * width), GATES),
            pltpu.VMEM((width, 3 * width), bf16),
            pltpu.VMEM(((padded + 1) * SUB, LANES), f32),
            pltpu.VMEM(((padded + 1) * SUB, LANES), f32),
            pltpu.VMEM((TILE, width), bf16),
            pltpu.VMEM((node_rows, TILE), bf16),
            pltpu.SemaphoreType.DMA((2, 5)),
            pltpu.SemaphoreType.DMA((2,)),
        ],
        compiler_params=pltpu.CompilerParams(vmem_limit_bytes=MOST),
        name="update",
    )(
        slot,
        index,
        count,
        size,
        incoming,
        of,
        kept,
        previous,
        gates,
        gru_in,
        gru_bias.reshape(1, 3 * width),
    )


def solution(mesh):
    row = P(AXES, None)
    return jax.shard_map(
        on_device,
        mesh=mesh,
        in_specs=(row, row, row, P(AXES), row, P(), P(), P(), P(), P(), P(), P()),
        out_specs=row,
        check_vma=False,
    )
```

```python
import jax
import jax.numpy as jnp
from jax import lax
from jax.experimental import pallas as pl
from jax.experimental.pallas import tpu as pltpu
from jax.sharding import PartitionSpec as P

AXES = ("node", "tm")
LANES = 128
SUB = 8
ACTIVE = 1024
TILE = 256
COLS = 256
GATES = jnp.bfloat16
UNROLL = 16
BAND = 512
MIB = 1 << 20
WHOLE = 58 * MIB
MOST = 51 * MIB
ANSWER = 51968 * 1024

VM = pl.BlockSpec(memory_space=pltpu.VMEM)
SM = pl.BlockSpec(memory_space=pltpu.SMEM)
HBM = pl.BlockSpec(memory_space=pltpu.HBM)


def plan_kernel(capacity, owner_ref, row_ref, mask_ref, ids_ref, place_ref):
    devices = ids_ref.shape[0]
    events = owner_ref.shape[1]
    ends = 2 * events
    owner = jnp.concatenate([owner_ref[0:1, :], owner_ref[1:2, :]], axis=1)
    code = jnp.concatenate([row_ref[0:1, :], row_ref[1:2, :] + ACTIVE * mask_ref[...]], axis=1)
    named = lax.broadcasted_iota(jnp.int32, (devices, ends), 0) == owner
    named_b = named.astype(jnp.float32).astype(jnp.bfloat16)
    block = (LANES, LANES)
    before = lax.broadcasted_iota(jnp.int32, block, 0) < lax.broadcasted_iota(jnp.int32, block, 1)
    table = jnp.concatenate([before.astype(jnp.float32), jnp.ones(block, jnp.float32)], axis=1).astype(jnp.bfloat16)
    total = jnp.zeros((devices, LANES), jnp.float32)
    counts = []
    for i in range(ends // LANES):
        both = jnp.dot(named_b[:, i * LANES : (i + 1) * LANES], table, preferred_element_type=jnp.float32)
        counts.append(both[:, :LANES] + total)
        total = total + both[:, LANES:]
    count = jnp.concatenate(counts, axis=1)
    position = jnp.sum(jnp.where(named, count, 0.0), axis=0, keepdims=True).astype(jnp.int32)
    place = owner * capacity + position
    place_ref[0:1, :] = place[:, :events]
    place_ref[1:2, :] = place[:, events:]
    here = lax.broadcasted_iota(jnp.int32, (LANES, ends), 0) == position
    low = jnp.where(here, (code & 31).astype(jnp.float32), 0.0).astype(jnp.bfloat16)
    high = jnp.where(here, (code >> 5).astype(jnp.float32), 0.0).astype(jnp.bfloat16)
    contract = (((1,), (1,)), ((), ()))
    low_sum = lax.dot_general(named_b, low, contract, preferred_element_type=jnp.float32)
    high_sum = lax.dot_general(named_b, high, contract, preferred_element_type=jnp.float32)
    ids_ref[...] = (low_sum + 32.0 * high_sum).astype(jnp.int32)


def answer_kernel(
    capacity,
    ids_ref,
    memory_hbm,
    out_ref,
    codes_ref,
    memory_ref,
    turned_ref,
    wanted_ref,
    rows_ref,
    memory_sem,
    load_sem,
    sems,
):
    devices = ids_ref.shape[0]
    memory_load = pltpu.make_async_copy(memory_hbm, memory_ref, memory_sem)
    memory_load.start()
    turned = jnp.transpose(ids_ref[...])[:SUB, :]
    codes_ref[...] = turned
    turned_ref[...] = turned
    load = pltpu.make_async_copy(turned_ref, wanted_ref, load_sem)
    load.start()
    load.wait()
    memory_load.wait()
    group = 8
    chunks = sems.shape[0]
    part = devices // chunks
    sends = []
    for q in range(chunks):

        def step(i, carry):
            for a in range(group):
                p = q * part + i * group + a
                for k in range(capacity):
                    rows_ref[p * capacity + k] = memory_ref[wanted_ref[k, p] & (ACTIVE - 1)]
            return carry

        lax.fori_loop(0, part // group, step, 0)
        here = pl.ds(q * part * capacity, part * capacity)
        send = pltpu.make_async_copy(rows_ref.at[here], out_ref.at[here], sems.at[q])
        send.start()
        sends.append(send)
    for send in sends:
        send.wait()


def compact_kernel(
    capacity, spare_row, codes_ref, slot_ref, index_ref, count_ref, node_ref, of_ref, size_ref, ids_ref, load_sem
):
    devices = ids_ref.shape[1]
    rows = of_ref.shape[0]
    load = pltpu.make_async_copy(codes_ref, ids_ref, load_sem)
    load.start()
    load.wait()

    def clear(i, carry):
        for a in range(16):
            of_ref[i * 16 + a] = -1
        return carry

    lax.fori_loop(0, rows // 16, clear, 0)

    def step(p, carry):
        taken, nodes = carry
        for k in range(capacity):
            code = ids_ref[k, p]
            active = code >= ACTIVE
            node = code & (ACTIVE - 1)
            known = of_ref[node]
            fresh = active & (known < 0)
            index = jnp.where(known < 0, nodes, known)
            of_ref[node] = jnp.where(active, index, known)
            slot_ref[taken] = p * capacity + k
            index_ref[taken] = index
            old = count_ref[index]
            was = jnp.where(known < 0, 0, old)
            count_ref[index] = jnp.where(active, was + 1, was)
            node_ref[index] = jnp.where(fresh, node, jnp.where(known < 0, 0, node_ref[index]))
            taken = taken + active.astype(jnp.int32)
            nodes = nodes + fresh.astype(jnp.int32)
        return taken, nodes

    taken, nodes = lax.fori_loop(0, devices, step, (jnp.int32(0), jnp.int32(0)))
    size_ref[0] = taken
    size_ref[1] = nodes
    for a in range(UNROLL):
        slot_ref[taken + a] = 0
        index_ref[taken + a] = spare_row
        count_ref[nodes + a] = 1


def to_matrix(tiles_ref, start, rows):
    parts = [tiles_ref[pl.ds(start * SUB + c, rows, stride=SUB), :].astype(jnp.bfloat16) for c in range(SUB)]
    return jnp.concatenate(parts, axis=1)


def hidden_gates_kernel(
    node_ref,
    size_ref,
    memory_ref,
    gru_ref,
    plain_ref,
    of_ref,
    previous_ref,
    gates_ref,
    kept_ref,
    tiles_ref,
    rows_ref,
    made_ref,
    left_ref,
    sems,
):
    left_ref[...] = jnp.where(of_ref[...] < 0, plain_ref[...].astype(jnp.float32), 0.0).astype(jnp.bfloat16)
    third = pltpu.make_async_copy(left_ref, kept_ref, sems.at[2])
    third.start()
    steps = jnp.maximum(pl.cdiv(size_ref[1], TILE), 1)
    width = rows_ref.shape[1]

    def block(t, carry):
        def copy(i, c):
            for a in range(16):
                u = i * 16 + a
                row = node_ref[t * TILE + u] & (ACTIVE - 1)
                tiles_ref[pl.ds(pl.multiple_of(u * SUB, SUB), SUB), :] = memory_ref[row].astype(jnp.float32)
            return c

        lax.fori_loop(0, TILE // 16, copy, 0)
        here = pl.ds(pl.multiple_of(t * TILE, TILE), TILE)
        rows_ref[...] = to_matrix(tiles_ref, 0, TILE)
        for j in range(width // COLS):
            for g in range(3):
                made_ref[:, (j * 3 + g) * COLS : (j * 3 + g + 1) * COLS] = jnp.dot(
                    rows_ref[...],
                    gru_ref[:, g * width + j * COLS : g * width + (j + 1) * COLS],
                    preferred_element_type=jnp.float32,
                ).astype(made_ref.dtype)
        first = pltpu.make_async_copy(rows_ref, previous_ref.at[here], sems.at[0])
        second = pltpu.make_async_copy(made_ref, gates_ref.at[here], sems.at[1])
        first.start()
        second.start()
        first.wait()
        second.wait()
        return carry

    lax.fori_loop(0, steps, block, 0)
    third.wait()


def fold_kernel(w2_ref, b2_ref, gru_ref, bias_ref, folded_ref, shift_ref):
    folded_ref[...] = jnp.dot(w2_ref[...], gru_ref[...], preferred_element_type=jnp.float32).astype(jnp.bfloat16)
    rest = jnp.broadcast_to(b2_ref[...], (SUB, b2_ref.shape[1]))
    shift = bias_ref[...]
    for i in range(3):
        term = rest.astype(jnp.bfloat16)
        shift = shift + jnp.dot(term, gru_ref[...], preferred_element_type=jnp.float32)[0:1, :]
        rest = rest - term.astype(jnp.float32)
    shift_ref[...] = shift


def message_kernel(
    place_ref,
    rows_ref,
    feat_ref,
    w1_hbm,
    b1_ref,
    out_ref,
    w1_ref,
    tiles_ref,
    inputs_ref,
    partial_ref,
    sent_ref,
    sem,
    sems,
):
    events = feat_ref.shape[0]
    depth, hid = w1_ref.shape
    width = (depth - feat_ref.shape[1]) // 2
    group = 16
    loads = []
    for i, rows in enumerate((pl.ds(0, width), pl.ds(width, depth - width))):
        load = pltpu.make_async_copy(w1_hbm.at[rows], w1_ref.at[rows], sems.at[i])
        load.start()
        loads.append(load)
    for half in range(2):

        def fetch(i, c):
            for a in range(group):
                e = i * group + a
                tiles_ref[pl.ds(pl.multiple_of(e * SUB, SUB), SUB), :] = rows_ref[place_ref[half, e]].astype(
                    jnp.float32
                )
            return c

        lax.fori_loop(0, events // group, fetch, 0)
        inputs_ref[:, half * width : (half + 1) * width] = to_matrix(tiles_ref, 0, events)
    inputs_ref[:, 2 * width :] = feat_ref[...]
    loads[0].wait()
    for j in range(hid // COLS):
        cols = slice(j * COLS, (j + 1) * COLS)
        partial_ref[:, cols] = (
            jnp.dot(inputs_ref[:, :width], w1_ref[:width, cols], preferred_element_type=jnp.float32) + b1_ref[:, cols]
        )
    loads[1].wait()
    for j in range(hid // COLS):
        cols = slice(j * COLS, (j + 1) * COLS)
        h = partial_ref[:, cols] + jnp.dot(
            inputs_ref[:, width:], w1_ref[width:, cols], preferred_element_type=jnp.float32
        )
        h = jnp.maximum(h, 0.0)
        for c in range(COLS // LANES):
            tiles_ref[pl.ds(j * (COLS // LANES) + c, events, stride=SUB), :] = h[:, c * LANES : (c + 1) * LANES]

    def send(i, c):
        for a in range(group):
            e = i * group + a
            sent_ref[place_ref[1, e]] = tiles_ref[pl.ds(pl.multiple_of(e * SUB, SUB), SUB), :].astype(jnp.bfloat16)
        return c

    lax.fori_loop(0, events // group, send, 0)
    leave = pltpu.make_async_copy(sent_ref, out_ref, sem)
    leave.start()
    leave.wait()


def update_kernel(
    slot_ref,
    index_ref,
    count_ref,
    size_ref,
    incoming_ref,
    of_ref,
    kept_hbm,
    previous_hbm,
    gates_hbm,
    gates_in_hbm,
    candidate_in_hbm,
    gates_bias_ref,
    candidate_bias_ref,
    out_ref,
    final_ref,
    previous_ref,
    gates_ref,
    gru_ref,
    even_ref,
    odd_ref,
    aggregate_ref,
    pick_ref,
    load_sems,
    sems,
):
    width = final_ref.shape[1]
    taken = size_ref[0]
    nodes = size_ref[1]
    steps = jnp.maximum(pl.cdiv(nodes, TILE), 1)
    half = width // 2
    first_tile = pl.ds(0, TILE)
    halves = []
    for h in range(2):
        loads = [(gates_hbm.at[first_tile, pl.ds(h * 3 * half, 3 * half)], gates_ref.at[:, pl.ds(h * 3 * half, 3 * half)])]
        for g in range(3):
            cols = pl.ds(g * width + h * half, half)
            source = gates_in_hbm.at[:, cols] if g < 2 else candidate_in_hbm.at[:, pl.ds(h * half, half)]
            loads.append((source, gru_ref.at[:, cols]))
        if h == 0:
            loads.append((previous_hbm.at[first_tile], previous_ref))
        else:
            loads.append((kept_hbm, final_ref))
        halves.append([pltpu.make_async_copy(a, b, load_sems.at[h, i]) for i, (a, b) in enumerate(loads)])
    for copy in halves[0] + halves[1]:
        copy.start()

    def clear(t, c):
        here = pl.ds(pl.multiple_of(t * TILE * SUB, TILE * SUB), TILE * SUB)
        even_ref[here, :] = jnp.zeros((TILE * SUB, LANES), jnp.float32)
        odd_ref[here, :] = jnp.zeros((TILE * SUB, LANES), jnp.float32)
        return c

    lax.fori_loop(0, steps, clear, 0)

    def add(i, c):
        for a in range(UNROLL):
            into = odd_ref if a % 2 else even_ref
            here = pl.ds(pl.multiple_of(index_ref[i * UNROLL + a] * SUB, SUB), SUB)
            into[here, :] += incoming_ref[slot_ref[i * UNROLL + a]].astype(jnp.float32)
        return c

    lax.fori_loop(0, pl.cdiv(taken, UNROLL), add, 0)
    def mean(i, c):
        for a in range(UNROLL):
            u = i * UNROLL + a
            here = pl.ds(pl.multiple_of(u * SUB, SUB), SUB)
            even_ref[here, :] = (even_ref[here, :] + odd_ref[here, :]) / count_ref[u].astype(jnp.float32)
        return c

    lax.fori_loop(0, pl.cdiv(nodes, UNROLL), mean, 0)

    def prepare(t):
        aggregate_ref[...] = to_matrix(even_ref, pl.multiple_of(t * TILE, TILE), TILE)
        lane = lax.broadcasted_iota(jnp.int32, (of_ref.shape[0], TILE), 1) + t * TILE
        pick_ref[...] = (of_ref[...] == lane).astype(jnp.float32).astype(jnp.bfloat16)

    def renew(j):
        pre = []
        for g in range(3):
            cols = slice(g * width + j * COLS, g * width + (j + 1) * COLS)
            hid = gates_ref[:, (j * 3 + g) * COLS : (j * 3 + g + 1) * COLS].astype(jnp.float32)
            bias = gates_bias_ref[:, cols] if g < 2 else candidate_bias_ref[:, j * COLS : (j + 1) * COLS]
            into = jnp.dot(aggregate_ref[...], gru_ref[:, cols], preferred_element_type=jnp.float32) + bias
            pre.append((into, hid))
        reset = jax.nn.sigmoid(pre[0][0] + pre[0][1])
        update = jax.nn.sigmoid(pre[1][0] + pre[1][1])
        candidate = jnp.tanh(pre[2][0] + reset * pre[2][1])
        previous = previous_ref[:, j * COLS : (j + 1) * COLS].astype(jnp.float32)
        return ((1.0 - update) * candidate + update * previous).astype(jnp.bfloat16)

    def place(j, renewed):
        cols = slice(j * COLS, (j + 1) * COLS)
        for i in range(final_ref.shape[0] // BAND):
            rows = slice(i * BAND, (i + 1) * BAND)
            found = jnp.dot(pick_ref[rows, :], renewed, preferred_element_type=jnp.float32)
            final_ref[rows, cols] = found.astype(jnp.bfloat16) + final_ref[rows, cols]

    per = half // COLS
    prepare(0)
    for copy in halves[0]:
        copy.wait()
    made = [renew(j) for j in range(per)]
    for copy in halves[1]:
        copy.wait()
    sends = [
        pltpu.make_async_copy(
            final_ref.at[:, pl.ds(h * half, half)], out_ref.at[:, pl.ds(h * half, half)], sems.at[h]
        )
        for h in range(2)
    ]
    for j in range(per):
        place(j, made[j])

    @pl.when(steps == 1)
    def _():
        sends[0].start()

    for j in range(per, 2 * per):
        place(j, renew(j))

    @pl.when(steps > 1)
    def _():
        def block(t, c):
            here = pl.ds(pl.multiple_of(t * TILE, TILE), TILE)
            again = [
                pltpu.make_async_copy(gates_hbm.at[here], gates_ref, load_sems.at[0, 0]),
                pltpu.make_async_copy(previous_hbm.at[here], previous_ref, load_sems.at[0, 1]),
            ]
            for copy in again:
                copy.start()
            prepare(t)
            for copy in again:
                copy.wait()
            for j in range(2 * per):
                place(j, renew(j))
            return c

        lax.fori_loop(1, steps, block, 0)
        sends[0].start()

    sends[1].start()
    for send in sends:
        send.wait()


def on_device(
    memory,
    ends_owner,
    ends_row,
    event_mask,
    edge_feat,
    msg_w1,
    msg_b1,
    msg_w2,
    msg_b2,
    gru_in,
    gru_hid,
    gru_bias,
):
    devices = lax.axis_size(AXES)
    events = ends_owner.shape[0]
    node_rows, width = memory.shape
    hid = msg_w2.shape[0]
    capacity = 5 * events // (2 * devices)
    slots = devices * capacity
    padded = pl.cdiv(slots, TILE) * TILE
    cells = width // LANES
    f32, bf16, i32 = jnp.float32, jnp.bfloat16, jnp.int32
    shape = jax.ShapeDtypeStruct

    ids, place = pl.pallas_call(
        lambda *refs: plan_kernel(capacity, *refs),
        out_shape=(shape((devices, LANES), i32), shape((2, events), i32)),
        in_specs=[VM, VM, VM],
        out_specs=(VM, VM),
        compiler_params=pltpu.CompilerParams(vmem_limit_bytes=WHOLE),
        name="plan",
    )(ends_owner.T, ends_row.T, event_mask.reshape(1, events))

    arrived = lax.all_to_all(
        ids.reshape(devices, 1, LANES), AXES, split_axis=0, concat_axis=0, tiled=True
    ).reshape(devices, LANES)
    tiles = memory.reshape(node_rows, cells, LANES)

    answers, codes = pl.pallas_call(
        lambda *refs: answer_kernel(capacity, *refs),
        out_shape=(shape((slots, cells, LANES), bf16), shape((SUB, devices), i32)),
        in_specs=[VM, HBM],
        out_specs=(HBM, VM),
        scratch_shapes=[
            pltpu.VMEM((node_rows, cells, LANES), bf16),
            pltpu.VMEM((SUB, devices), i32),
            pltpu.SMEM((SUB, devices), i32),
            pltpu.VMEM((slots, cells, LANES), bf16),
            pltpu.SemaphoreType.DMA,
            pltpu.SemaphoreType.DMA,
            pltpu.SemaphoreType.DMA((4,)),
        ],
        compiler_params=pltpu.CompilerParams(vmem_limit_bytes=ANSWER),
        name="answer",
    )(arrived, tiles)
    returned = lax.all_to_all(
        answers.reshape(devices, capacity, cells, LANES), AXES, split_axis=0, concat_axis=0, tiled=True
    ).reshape(slots, cells, LANES)

    slot, index, count, node, of, size = pl.pallas_call(
        lambda *refs: compact_kernel(capacity, padded, *refs),
        out_shape=(
            shape((1024,), i32),
            shape((1024,), i32),
            shape((1024,), i32),
            shape((1024,), i32),
            shape((node_rows,), i32),
            shape((8,), i32),
        ),
        in_specs=[VM],
        out_specs=(SM, SM, SM, SM, SM, SM),
        scratch_shapes=[pltpu.SMEM((SUB, devices), i32), pltpu.SemaphoreType.DMA],
        compiler_params=pltpu.CompilerParams(vmem_limit_bytes=MOST),
        cost_estimate=pl.CostEstimate(flops=4_000_000_000, bytes_accessed=20_000_000, transcendentals=0),
        name="compact",
    )(codes)

    of = of.reshape(node_rows, 1)
    previous, gates, kept = pl.pallas_call(
        hidden_gates_kernel,
        out_shape=(
            shape((padded, width), bf16),
            shape((padded, 3 * width), GATES),
            shape((node_rows, width), bf16),
        ),
        in_specs=[SM, SM, VM, VM, VM, VM],
        out_specs=(HBM, HBM, HBM),
        scratch_shapes=[
            pltpu.VMEM((TILE * SUB, LANES), f32),
            pltpu.VMEM((TILE, width), bf16),
            pltpu.VMEM((TILE, 3 * width), GATES),
            pltpu.VMEM((node_rows, width), bf16),
            pltpu.SemaphoreType.DMA((3,)),
        ],
        compiler_params=pltpu.CompilerParams(vmem_limit_bytes=WHOLE),
        cost_estimate=pl.CostEstimate(flops=4_000_000_000, bytes_accessed=20_000_000, transcendentals=0),
        name="hidden_gates",
    )(node, size, tiles, gru_hid, memory, of)

    def fold(first, last):
        step = 512
        offset = first // step
        return pl.pallas_call(
            fold_kernel,
            out_shape=(shape((hid, last - first), bf16), shape((1, last - first), f32)),
            grid=((last - first) // step,),
            in_specs=[
                pl.BlockSpec((hid, width), lambda i: (0, 0)),
                pl.BlockSpec((1, width), lambda i: (0, 0)),
                pl.BlockSpec((width, step), lambda i: (0, i + offset)),
                pl.BlockSpec((1, step), lambda i: (0, i + offset)),
            ],
            out_specs=(pl.BlockSpec((hid, step), lambda i: (0, i)), pl.BlockSpec((1, step), lambda i: (0, i))),
            compiler_params=pltpu.CompilerParams(vmem_limit_bytes=WHOLE),
            cost_estimate=pl.CostEstimate(
                flops=2 * hid * width * (last - first), bytes_accessed=4 * width * (last - first), transcendentals=0
            ),
            name="fold",
        )(msg_w2, msg_b2.reshape(1, width), gru_in, gru_bias.reshape(1, 3 * width))

    gates_in, gates_bias = fold(0, 2 * width)
    returned, size, gates_in = lax.optimization_barrier((returned, size, gates_in))
    outgoing = pl.pallas_call(
        message_kernel,
        out_shape=shape((slots, cells, LANES), bf16),
        in_specs=[SM, VM, VM, HBM, VM],
        out_specs=HBM,
        scratch_shapes=[
            pltpu.VMEM(msg_w1.shape, bf16),
            pltpu.VMEM((events * SUB, LANES), f32),
            pltpu.VMEM((events, msg_w1.shape[0]), bf16),
            pltpu.VMEM((events, hid), f32),
            pltpu.VMEM((slots, cells, LANES), bf16),
            pltpu.SemaphoreType.DMA,
            pltpu.SemaphoreType.DMA((2,)),
        ],
        compiler_params=pltpu.CompilerParams(vmem_limit_bytes=MOST),
        name="message",
    )(place, returned, edge_feat, msg_w1, msg_b1.reshape(1, hid))
    candidate_in, candidate_bias = fold(2 * width, 3 * width)
    incoming = lax.all_to_all(
        outgoing.reshape(devices, capacity, cells, LANES), AXES, split_axis=0, concat_axis=0, tiled=True
    ).reshape(slots, cells, LANES)

    return pl.pallas_call(
        update_kernel,
        out_shape=shape((node_rows, width), bf16),
        in_specs=[SM, SM, SM, SM, VM, VM, HBM, HBM, HBM, HBM, HBM, VM, VM],
        out_specs=HBM,
        scratch_shapes=[
            pltpu.VMEM((node_rows, width), bf16),
            pltpu.VMEM((TILE, width), bf16),
            pltpu.VMEM((TILE, 3 * width), GATES),
            pltpu.VMEM((width, 3 * width), bf16),
            pltpu.VMEM(((padded + 1) * SUB, LANES), f32),
            pltpu.VMEM(((padded + 1) * SUB, LANES), f32),
            pltpu.VMEM((TILE, width), bf16),
            pltpu.VMEM((node_rows, TILE), bf16),
            pltpu.SemaphoreType.DMA((2, 5)),
            pltpu.SemaphoreType.DMA((2,)),
        ],
        compiler_params=pltpu.CompilerParams(vmem_limit_bytes=MOST),
        name="update",
    )(
        slot,
        index,
        count,
        size,
        incoming,
        of,
        kept,
        previous,
        gates,
        gates_in,
        candidate_in,
        gates_bias,
        candidate_bias,
    )


def solution(mesh):
    row = P(AXES, None)
    return jax.shard_map(
        on_device,
        mesh=mesh,
        in_specs=(row, row, row, P(AXES), row, P(), P(), P(), P(), P(), P(), P()),
        out_specs=row,
        check_vma=False,
    )
```

```python
import jax
import jax.numpy as jnp
from jax import lax
from jax.experimental import pallas as pl
from jax.experimental.pallas import tpu as pltpu
from jax.sharding import PartitionSpec as P

AXES = ("node", "tm")
LANES = 128
SUB = 8
ACTIVE = 1024
TILE = 256
COLS = 256
GATES = jnp.bfloat16
UNROLL = 16
BAND = 512
MIB = 1 << 20
WHOLE = 58 * MIB
MOST = 51 * MIB
ANSWER = 51968 * 1024

VM = pl.BlockSpec(memory_space=pltpu.VMEM)
SM = pl.BlockSpec(memory_space=pltpu.SMEM)
HBM = pl.BlockSpec(memory_space=pltpu.HBM)


def plan_kernel(capacity, owner_ref, row_ref, mask_ref, ids_ref, place_ref):
    devices = ids_ref.shape[0]
    events = owner_ref.shape[1]
    ends = 2 * events
    owner = jnp.concatenate([owner_ref[0:1, :], owner_ref[1:2, :]], axis=1)
    code = jnp.concatenate([row_ref[0:1, :], row_ref[1:2, :] + ACTIVE * mask_ref[...]], axis=1)
    named = lax.broadcasted_iota(jnp.int32, (devices, ends), 0) == owner
    named_b = named.astype(jnp.float32).astype(jnp.bfloat16)
    block = (LANES, LANES)
    before = lax.broadcasted_iota(jnp.int32, block, 0) < lax.broadcasted_iota(jnp.int32, block, 1)
    table = jnp.concatenate([before.astype(jnp.float32), jnp.ones(block, jnp.float32)], axis=1).astype(jnp.bfloat16)
    total = jnp.zeros((devices, LANES), jnp.float32)
    counts = []
    for i in range(ends // LANES):
        both = jnp.dot(named_b[:, i * LANES : (i + 1) * LANES], table, preferred_element_type=jnp.float32)
        counts.append(both[:, :LANES] + total)
        total = total + both[:, LANES:]
    count = jnp.concatenate(counts, axis=1)
    position = jnp.sum(jnp.where(named, count, 0.0), axis=0, keepdims=True).astype(jnp.int32)
    place = owner * capacity + position
    place_ref[0:1, :] = place[:, :events]
    place_ref[1:2, :] = place[:, events:]
    here = lax.broadcasted_iota(jnp.int32, (LANES, ends), 0) == position
    low = jnp.where(here, (code & 31).astype(jnp.float32), 0.0).astype(jnp.bfloat16)
    high = jnp.where(here, (code >> 5).astype(jnp.float32), 0.0).astype(jnp.bfloat16)
    contract = (((1,), (1,)), ((), ()))
    low_sum = lax.dot_general(named_b, low, contract, preferred_element_type=jnp.float32)
    high_sum = lax.dot_general(named_b, high, contract, preferred_element_type=jnp.float32)
    ids_ref[...] = (low_sum + 32.0 * high_sum).astype(jnp.int32)


def answer_kernel(
    capacity,
    ids_ref,
    memory_hbm,
    out_ref,
    codes_ref,
    memory_ref,
    turned_ref,
    wanted_ref,
    rows_ref,
    memory_sem,
    load_sem,
    sems,
):
    devices = ids_ref.shape[0]
    memory_load = pltpu.make_async_copy(memory_hbm, memory_ref, memory_sem)
    memory_load.start()
    turned = jnp.transpose(ids_ref[...])[:SUB, :]
    turned_ref[...] = turned
    load = pltpu.make_async_copy(turned_ref, wanted_ref, load_sem)
    load.start()
    load.wait()
    keep = pltpu.make_async_copy(turned_ref, codes_ref, load_sem)
    keep.start()
    memory_load.wait()
    group = 8
    chunks = sems.shape[0]
    part = devices // chunks
    sends = []
    for q in range(chunks):

        def step(i, carry):
            for a in range(group):
                p = q * part + i * group + a
                for k in range(capacity):
                    rows_ref[p * capacity + k] = memory_ref[wanted_ref[k, p] & (ACTIVE - 1)]
            return carry

        lax.fori_loop(0, part // group, step, 0)
        here = pl.ds(q * part * capacity, part * capacity)
        send = pltpu.make_async_copy(rows_ref.at[here], out_ref.at[here], sems.at[q])
        send.start()
        sends.append(send)
    keep.wait()
    for send in sends:
        send.wait()


def compact_kernel(
    capacity, spare_row, codes_ref, slot_ref, index_ref, count_ref, node_ref, of_ref, size_ref, ids_ref, load_sem
):
    devices = ids_ref.shape[1]
    rows = of_ref.shape[0]
    load = pltpu.make_async_copy(codes_ref, ids_ref, load_sem)
    load.start()
    load.wait()

    def clear(i, carry):
        for a in range(16):
            of_ref[i * 16 + a] = -1
        return carry

    lax.fori_loop(0, rows // 16, clear, 0)

    def choose(p, taken):
        for k in range(capacity):
            code = ids_ref[k, p]
            slot_ref[taken] = p * capacity + k
            index_ref[taken] = code & (ACTIVE - 1)
            taken = taken + (code >= ACTIVE).astype(jnp.int32)
        return taken

    taken = lax.fori_loop(0, devices, choose, jnp.int32(0), unroll=2)

    def number(i, nodes):
        node = index_ref[i]
        known = of_ref[node]
        fresh = known < 0
        index = jnp.where(fresh, nodes, known)
        of_ref[node] = index
        index_ref[i] = index
        node_ref[index] = node
        count_ref[index] = jnp.where(fresh, 0, count_ref[index]) + 1
        return nodes + fresh.astype(jnp.int32)

    nodes = lax.fori_loop(0, taken, number, jnp.int32(0))
    size_ref[0] = taken
    size_ref[1] = nodes
    for a in range(UNROLL):
        slot_ref[taken + a] = 0
        index_ref[taken + a] = spare_row
        count_ref[nodes + a] = 1


def to_matrix(tiles_ref, start, rows):
    parts = [tiles_ref[pl.ds(start * SUB + c, rows, stride=SUB), :].astype(jnp.bfloat16) for c in range(SUB)]
    return jnp.concatenate(parts, axis=1)


def hidden_gates_kernel(
    node_ref,
    size_ref,
    memory_hbm,
    gru_hbm,
    plain_hbm,
    of_ref,
    previous_ref,
    gates_ref,
    kept_ref,
    memory_ref,
    gru_ref,
    plain_ref,
    tiles_ref,
    rows_ref,
    made_ref,
    left_ref,
    sems,
):
    loads = []
    for source, target in ((memory_hbm, memory_ref), (plain_hbm, plain_ref), (gru_hbm, gru_ref)):
        load = pltpu.make_async_copy(source, target, sems.at[3 + len(loads)])
        load.start()
        loads.append(load)
    loads[0].wait()
    loads[1].wait()
    left_ref[...] = jnp.where(of_ref[...] < 0, plain_ref[...].astype(jnp.float32), 0.0).astype(jnp.bfloat16)
    third = pltpu.make_async_copy(left_ref, kept_ref, sems.at[2])
    third.start()
    loads[2].wait()
    steps = jnp.maximum(pl.cdiv(size_ref[1], TILE), 1)
    width = rows_ref.shape[1]

    def block(t, carry):
        def copy(i, c):
            for a in range(16):
                u = i * 16 + a
                row = node_ref[t * TILE + u] & (ACTIVE - 1)
                tiles_ref[pl.ds(pl.multiple_of(u * SUB, SUB), SUB), :] = memory_ref[row].astype(jnp.float32)
            return c

        lax.fori_loop(0, TILE // 16, copy, 0)
        here = pl.ds(pl.multiple_of(t * TILE, TILE), TILE)
        rows_ref[...] = to_matrix(tiles_ref, 0, TILE)
        for j in range(width // COLS):
            for g in range(3):
                made_ref[:, (j * 3 + g) * COLS : (j * 3 + g + 1) * COLS] = jnp.dot(
                    rows_ref[...],
                    gru_ref[:, g * width + j * COLS : g * width + (j + 1) * COLS],
                    preferred_element_type=jnp.float32,
                ).astype(made_ref.dtype)
        first = pltpu.make_async_copy(rows_ref, previous_ref.at[here], sems.at[0])
        second = pltpu.make_async_copy(made_ref, gates_ref.at[here], sems.at[1])
        first.start()
        second.start()
        first.wait()
        second.wait()
        return carry

    lax.fori_loop(0, steps, block, 0)
    third.wait()


def fold_kernel(w2_ref, b2_ref, gru_ref, bias_ref, folded_ref, shift_ref, left_ref):
    hid = w2_ref.shape[0]

    @pl.when(pl.program_id(0) == 0)
    def _():
        left_ref[:hid, :] = w2_ref[...]
        first = b2_ref[...].astype(jnp.bfloat16).astype(jnp.float32)
        rest = b2_ref[...] - first
        second = rest.astype(jnp.bfloat16).astype(jnp.float32)
        rows = lax.broadcasted_iota(jnp.int32, (2 * SUB, b2_ref.shape[1]), 0)
        terms = jnp.where(rows == 0, first, jnp.where(rows == 1, second, jnp.where(rows == 2, rest - second, 0.0)))
        left_ref[hid:, :] = terms.astype(jnp.bfloat16)

    both = jnp.dot(left_ref[...], gru_ref[...], preferred_element_type=jnp.float32)
    folded_ref[...] = both[:hid, :].astype(jnp.bfloat16)
    shift_ref[...] = bias_ref[...] + jnp.sum(both[hid:, :], axis=0, keepdims=True)


def message_kernel(
    place_ref,
    rows_ref,
    feat_ref,
    w1_hbm,
    b1_ref,
    out_ref,
    w1_ref,
    tiles_ref,
    inputs_ref,
    partial_ref,
    sent_ref,
    sem,
    sems,
):
    events = feat_ref.shape[0]
    depth, hid = w1_ref.shape
    width = (depth - feat_ref.shape[1]) // 2
    group = 16
    loads = []
    for i, rows in enumerate((pl.ds(0, width), pl.ds(width, depth - width))):
        load = pltpu.make_async_copy(w1_hbm.at[rows], w1_ref.at[rows], sems.at[i])
        load.start()
        loads.append(load)
    for half in range(2):

        def fetch(i, c):
            for a in range(group):
                e = i * group + a
                tiles_ref[pl.ds(pl.multiple_of(e * SUB, SUB), SUB), :] = rows_ref[place_ref[half, e]].astype(
                    jnp.float32
                )
            return c

        lax.fori_loop(0, events // group, fetch, 0)
        inputs_ref[:, half * width : (half + 1) * width] = to_matrix(tiles_ref, 0, events)
    inputs_ref[:, 2 * width :] = feat_ref[...]
    loads[0].wait()
    for j in range(hid // COLS):
        cols = slice(j * COLS, (j + 1) * COLS)
        partial_ref[:, cols] = (
            jnp.dot(inputs_ref[:, :width], w1_ref[:width, cols], preferred_element_type=jnp.float32) + b1_ref[:, cols]
        )
    loads[1].wait()
    for j in range(hid // COLS):
        cols = slice(j * COLS, (j + 1) * COLS)
        h = partial_ref[:, cols] + jnp.dot(
            inputs_ref[:, width:], w1_ref[width:, cols], preferred_element_type=jnp.float32
        )
        h = jnp.maximum(h, 0.0)
        for c in range(COLS // LANES):
            tiles_ref[pl.ds(j * (COLS // LANES) + c, events, stride=SUB), :] = h[:, c * LANES : (c + 1) * LANES]

    def send(i, c):
        for a in range(group):
            e = i * group + a
            sent_ref[place_ref[1, e]] = tiles_ref[pl.ds(pl.multiple_of(e * SUB, SUB), SUB), :].astype(jnp.bfloat16)
        return c

    lax.fori_loop(0, events // group, send, 0)
    leave = pltpu.make_async_copy(sent_ref, out_ref, sem)
    leave.start()
    leave.wait()


def update_kernel(
    slot_ref,
    index_ref,
    count_ref,
    size_ref,
    incoming_ref,
    of_ref,
    kept_hbm,
    previous_hbm,
    gates_hbm,
    left_in_hbm,
    right_in_hbm,
    left_bias_ref,
    right_bias_ref,
    out_ref,
    final_ref,
    previous_ref,
    gates_ref,
    gru_ref,
    even_ref,
    odd_ref,
    aggregate_ref,
    pick_ref,
    load_sems,
    sems,
):
    width = final_ref.shape[1]
    taken = size_ref[0]
    nodes = size_ref[1]
    steps = jnp.maximum(pl.cdiv(nodes, TILE), 1)
    half = width // 2
    split = left_in_hbm.shape[1]
    first_tile = pl.ds(0, TILE)
    halves = []
    for h in range(2):
        loads = [(gates_hbm.at[first_tile, pl.ds(h * 3 * half, 3 * half)], gates_ref.at[:, pl.ds(h * 3 * half, 3 * half)])]
        for g in range(3):
            first = g * width + h * half
            part = (left_in_hbm, right_in_hbm)[first // split]
            loads.append((part.at[:, pl.ds(first % split, half)], gru_ref.at[:, pl.ds(first, half)]))
        if h == 0:
            loads.append((previous_hbm.at[first_tile], previous_ref))
        else:
            loads.append((kept_hbm, final_ref))
        halves.append([pltpu.make_async_copy(a, b, load_sems.at[h, i]) for i, (a, b) in enumerate(loads)])
    for copy in halves[0] + halves[1]:
        copy.start()

    def clear(t, c):
        here = pl.ds(pl.multiple_of(t * TILE * SUB, TILE * SUB), TILE * SUB)
        even_ref[here, :] = jnp.zeros((TILE * SUB, LANES), jnp.float32)
        odd_ref[here, :] = jnp.zeros((TILE * SUB, LANES), jnp.float32)
        return c

    lax.fori_loop(0, steps, clear, 0)

    def add(i, c):
        for a in range(UNROLL):
            into = odd_ref if a % 2 else even_ref
            here = pl.ds(pl.multiple_of(index_ref[i * UNROLL + a] * SUB, SUB), SUB)
            into[here, :] += incoming_ref[slot_ref[i * UNROLL + a]].astype(jnp.float32)
        return c

    lax.fori_loop(0, pl.cdiv(taken, UNROLL), add, 0)
    def mean(i, c):
        for a in range(UNROLL):
            u = i * UNROLL + a
            here = pl.ds(pl.multiple_of(u * SUB, SUB), SUB)
            even_ref[here, :] = (even_ref[here, :] + odd_ref[here, :]) / count_ref[u].astype(jnp.float32)
        return c

    lax.fori_loop(0, pl.cdiv(nodes, UNROLL), mean, 0)

    def prepare(t):
        aggregate_ref[...] = to_matrix(even_ref, pl.multiple_of(t * TILE, TILE), TILE)
        lane = lax.broadcasted_iota(jnp.int32, (of_ref.shape[0], TILE), 1) + t * TILE
        pick_ref[...] = (of_ref[...] == lane).astype(jnp.float32).astype(jnp.bfloat16)

    def renew(j):
        pre = []
        for g in range(3):
            cols = slice(g * width + j * COLS, g * width + (j + 1) * COLS)
            hid = gates_ref[:, (j * 3 + g) * COLS : (j * 3 + g + 1) * COLS].astype(jnp.float32)
            first = g * width + j * COLS
            bias = (left_bias_ref, right_bias_ref)[first // split][:, first % split : first % split + COLS]
            into = jnp.dot(aggregate_ref[...], gru_ref[:, cols], preferred_element_type=jnp.float32) + bias
            pre.append((into, hid))
        reset = jax.nn.sigmoid(pre[0][0] + pre[0][1])
        update = jax.nn.sigmoid(pre[1][0] + pre[1][1])
        candidate = jnp.tanh(pre[2][0] + reset * pre[2][1])
        previous = previous_ref[:, j * COLS : (j + 1) * COLS].astype(jnp.float32)
        return ((1.0 - update) * candidate + update * previous).astype(jnp.bfloat16)

    def place(j, renewed):
        cols = slice(j * COLS, (j + 1) * COLS)
        for i in range(final_ref.shape[0] // BAND):
            rows = slice(i * BAND, (i + 1) * BAND)
            found = jnp.dot(pick_ref[rows, :], renewed, preferred_element_type=jnp.float32)
            final_ref[rows, cols] = found.astype(jnp.bfloat16) + final_ref[rows, cols]

    per = half // COLS
    prepare(0)
    for copy in halves[0]:
        copy.wait()
    made = [renew(j) for j in range(per)]
    for copy in halves[1]:
        copy.wait()
    sends = [
        pltpu.make_async_copy(
            final_ref.at[:, pl.ds(h * half, half)], out_ref.at[:, pl.ds(h * half, half)], sems.at[h]
        )
        for h in range(2)
    ]
    for j in range(per):
        place(j, made[j])

    @pl.when(steps == 1)
    def _():
        sends[0].start()

    for j in range(per, 2 * per):
        place(j, renew(j))

    @pl.when(steps > 1)
    def _():
        def block(t, c):
            here = pl.ds(pl.multiple_of(t * TILE, TILE), TILE)
            again = [
                pltpu.make_async_copy(gates_hbm.at[here], gates_ref, load_sems.at[0, 0]),
                pltpu.make_async_copy(previous_hbm.at[here], previous_ref, load_sems.at[0, 1]),
            ]
            for copy in again:
                copy.start()
            prepare(t)
            for copy in again:
                copy.wait()
            for j in range(2 * per):
                place(j, renew(j))
            return c

        lax.fori_loop(1, steps, block, 0)
        sends[0].start()

    sends[1].start()
    for send in sends:
        send.wait()


def on_device(
    memory,
    ends_owner,
    ends_row,
    event_mask,
    edge_feat,
    msg_w1,
    msg_b1,
    msg_w2,
    msg_b2,
    gru_in,
    gru_hid,
    gru_bias,
):
    devices = lax.axis_size(AXES)
    events = ends_owner.shape[0]
    node_rows, width = memory.shape
    hid = msg_w2.shape[0]
    capacity = 5 * events // (2 * devices)
    slots = devices * capacity
    padded = pl.cdiv(slots, TILE) * TILE
    cells = width // LANES
    f32, bf16, i32 = jnp.float32, jnp.bfloat16, jnp.int32
    shape = jax.ShapeDtypeStruct

    ids, place = pl.pallas_call(
        lambda *refs: plan_kernel(capacity, *refs),
        out_shape=(shape((devices, LANES), i32), shape((2, events), i32)),
        in_specs=[VM, VM, VM],
        out_specs=(VM, VM),
        compiler_params=pltpu.CompilerParams(vmem_limit_bytes=WHOLE),
        name="plan",
    )(ends_owner.T, ends_row.T, event_mask.reshape(1, events))

    arrived = lax.all_to_all(
        ids.reshape(devices, 1, LANES), AXES, split_axis=0, concat_axis=0, tiled=True
    ).reshape(devices, LANES)
    tiles = memory.reshape(node_rows, cells, LANES)

    answers, codes = pl.pallas_call(
        lambda *refs: answer_kernel(capacity, *refs),
        out_shape=(shape((slots, cells, LANES), bf16), shape((SUB, devices), i32)),
        in_specs=[VM, HBM],
        out_specs=(HBM, HBM),
        scratch_shapes=[
            pltpu.VMEM((node_rows, cells, LANES), bf16),
            pltpu.VMEM((SUB, devices), i32),
            pltpu.SMEM((SUB, devices), i32),
            pltpu.VMEM((slots, cells, LANES), bf16),
            pltpu.SemaphoreType.DMA,
            pltpu.SemaphoreType.DMA,
            pltpu.SemaphoreType.DMA((4,)),
        ],
        compiler_params=pltpu.CompilerParams(vmem_limit_bytes=ANSWER),
        name="answer",
    )(arrived, tiles)
    returned = lax.all_to_all(
        answers.reshape(devices, capacity, cells, LANES), AXES, split_axis=0, concat_axis=0, tiled=True
    ).reshape(slots, cells, LANES)

    slot, index, count, node, of, size = pl.pallas_call(
        lambda *refs: compact_kernel(capacity, padded, *refs),
        out_shape=(
            shape((1024,), i32),
            shape((1024,), i32),
            shape((1024,), i32),
            shape((1024,), i32),
            shape((node_rows,), i32),
            shape((8,), i32),
        ),
        in_specs=[VM],
        out_specs=(SM, SM, SM, SM, SM, SM),
        scratch_shapes=[pltpu.SMEM((SUB, devices), i32), pltpu.SemaphoreType.DMA],
        compiler_params=pltpu.CompilerParams(vmem_limit_bytes=MOST),
        cost_estimate=pl.CostEstimate(flops=4_000_000_000, bytes_accessed=20_000_000, transcendentals=0),
        name="compact",
    )(codes)

    of = of.reshape(node_rows, 1)
    previous, gates, kept = pl.pallas_call(
        hidden_gates_kernel,
        out_shape=(
            shape((padded, width), bf16),
            shape((padded, 3 * width), GATES),
            shape((node_rows, width), bf16),
        ),
        in_specs=[SM, SM, HBM, HBM, HBM, VM],
        out_specs=(HBM, HBM, HBM),
        scratch_shapes=[
            pltpu.VMEM((node_rows, cells, LANES), bf16),
            pltpu.VMEM((width, 3 * width), bf16),
            pltpu.VMEM((node_rows, width), bf16),
            pltpu.VMEM((TILE * SUB, LANES), f32),
            pltpu.VMEM((TILE, width), bf16),
            pltpu.VMEM((TILE, 3 * width), GATES),
            pltpu.VMEM((node_rows, width), bf16),
            pltpu.SemaphoreType.DMA((6,)),
        ],
        compiler_params=pltpu.CompilerParams(vmem_limit_bytes=WHOLE),
        cost_estimate=pl.CostEstimate(flops=4_000_000_000, bytes_accessed=20_000_000, transcendentals=0),
        name="hidden_gates",
    )(node, size, tiles, gru_hid, memory, of)

    def fold(first, last):
        step = 512
        offset = first // step
        return pl.pallas_call(
            fold_kernel,
            out_shape=(shape((hid, last - first), bf16), shape((1, last - first), f32)),
            grid=((last - first) // step,),
            in_specs=[
                pl.BlockSpec((hid, width), lambda i: (0, 0)),
                pl.BlockSpec((1, width), lambda i: (0, 0)),
                pl.BlockSpec((width, step), lambda i: (0, i + offset)),
                pl.BlockSpec((1, step), lambda i: (0, i + offset)),
            ],
            out_specs=(pl.BlockSpec((hid, step), lambda i: (0, i)), pl.BlockSpec((1, step), lambda i: (0, i))),
            scratch_shapes=[pltpu.VMEM((hid + 2 * SUB, width), bf16)],
            compiler_params=pltpu.CompilerParams(vmem_limit_bytes=WHOLE),
            cost_estimate=pl.CostEstimate(
                flops=2 * hid * width * (last - first), bytes_accessed=4 * width * (last - first), transcendentals=0
            ),
            name="fold",
        )(msg_w2, msg_b2.reshape(1, width), gru_in, gru_bias.reshape(1, 3 * width))

    split = 3 * width // 2
    left_in, left_bias = fold(0, split)
    returned, size, left_in = lax.optimization_barrier((returned, size, left_in))
    outgoing = pl.pallas_call(
        message_kernel,
        out_shape=shape((slots, cells, LANES), bf16),
        in_specs=[SM, VM, VM, HBM, VM],
        out_specs=HBM,
        scratch_shapes=[
            pltpu.VMEM(msg_w1.shape, bf16),
            pltpu.VMEM((events * SUB, LANES), f32),
            pltpu.VMEM((events, msg_w1.shape[0]), bf16),
            pltpu.VMEM((events, hid), f32),
            pltpu.VMEM((slots, cells, LANES), bf16),
            pltpu.SemaphoreType.DMA,
            pltpu.SemaphoreType.DMA((2,)),
        ],
        compiler_params=pltpu.CompilerParams(vmem_limit_bytes=MOST),
        name="message",
    )(place, returned, edge_feat, msg_w1, msg_b1.reshape(1, hid))
    right_in, right_bias = fold(split, 3 * width)
    incoming = lax.all_to_all(
        outgoing.reshape(devices, capacity, cells, LANES), AXES, split_axis=0, concat_axis=0, tiled=True
    ).reshape(slots, cells, LANES)

    return pl.pallas_call(
        update_kernel,
        out_shape=shape((node_rows, width), bf16),
        in_specs=[SM, SM, SM, SM, VM, VM, HBM, HBM, HBM, HBM, HBM, VM, VM],
        out_specs=HBM,
        scratch_shapes=[
            pltpu.VMEM((node_rows, width), bf16),
            pltpu.VMEM((TILE, width), bf16),
            pltpu.VMEM((TILE, 3 * width), GATES),
            pltpu.VMEM((width, 3 * width), bf16),
            pltpu.VMEM(((padded + 1) * SUB, LANES), f32),
            pltpu.VMEM(((padded + 1) * SUB, LANES), f32),
            pltpu.VMEM((TILE, width), bf16),
            pltpu.VMEM((node_rows, TILE), bf16),
            pltpu.SemaphoreType.DMA((2, 5)),
            pltpu.SemaphoreType.DMA((2,)),
        ],
        compiler_params=pltpu.CompilerParams(vmem_limit_bytes=MOST),
        name="update",
    )(
        slot,
        index,
        count,
        size,
        incoming,
        of,
        kept,
        previous,
        gates,
        left_in,
        right_in,
        left_bias,
        right_bias,
    )


def solution(mesh):
    row = P(AXES, None)
    return jax.shard_map(
        on_device,
        mesh=mesh,
        in_specs=(row, row, row, P(AXES), row, P(), P(), P(), P(), P(), P(), P()),
        out_specs=row,
        check_vma=False,
    )
```

```python
import jax
import jax.numpy as jnp
from jax import lax
from jax.experimental import pallas as pl
from jax.experimental.pallas import tpu as pltpu
from jax.sharding import PartitionSpec as P

AXES = ("node", "tm")
LANES = 128
SUB = 8
ACTIVE = 1024
TILE = 256
COLS = 256
GATES = jnp.bfloat16
UNROLL = 16
BAND = 512
MIB = 1 << 20
WHOLE = 58 * MIB
MOST = 51 * MIB
ANSWER = 51968 * 1024

VM = pl.BlockSpec(memory_space=pltpu.VMEM)
SM = pl.BlockSpec(memory_space=pltpu.SMEM)
HBM = pl.BlockSpec(memory_space=pltpu.HBM)


def plan_kernel(capacity, owner_ref, row_ref, mask_ref, ids_ref, place_ref):
    devices = ids_ref.shape[0]
    events = owner_ref.shape[1]
    ends = 2 * events
    owner = jnp.concatenate([owner_ref[0:1, :], owner_ref[1:2, :]], axis=1)
    code = jnp.concatenate([row_ref[0:1, :], row_ref[1:2, :] + ACTIVE * mask_ref[...]], axis=1)
    named = lax.broadcasted_iota(jnp.int32, (devices, ends), 0) == owner
    named_b = named.astype(jnp.float32).astype(jnp.bfloat16)
    block = (LANES, LANES)
    before = lax.broadcasted_iota(jnp.int32, block, 0) < lax.broadcasted_iota(jnp.int32, block, 1)
    table = jnp.concatenate([before.astype(jnp.float32), jnp.ones(block, jnp.float32)], axis=1).astype(jnp.bfloat16)
    total = jnp.zeros((devices, LANES), jnp.float32)
    counts = []
    for i in range(ends // LANES):
        both = jnp.dot(named_b[:, i * LANES : (i + 1) * LANES], table, preferred_element_type=jnp.float32)
        counts.append(both[:, :LANES] + total)
        total = total + both[:, LANES:]
    count = jnp.concatenate(counts, axis=1)
    position = jnp.sum(jnp.where(named, count, 0.0), axis=0, keepdims=True).astype(jnp.int32)
    place = owner * capacity + position
    place_ref[0:1, :] = place[:, :events]
    place_ref[1:2, :] = place[:, events:]
    here = lax.broadcasted_iota(jnp.int32, (LANES, ends), 0) == position
    low = jnp.where(here, (code & 31).astype(jnp.float32), 0.0).astype(jnp.bfloat16)
    high = jnp.where(here, (code >> 5).astype(jnp.float32), 0.0).astype(jnp.bfloat16)
    contract = (((1,), (1,)), ((), ()))
    low_sum = lax.dot_general(named_b, low, contract, preferred_element_type=jnp.float32)
    high_sum = lax.dot_general(named_b, high, contract, preferred_element_type=jnp.float32)
    ids_ref[...] = (low_sum + 32.0 * high_sum).astype(jnp.int32)


def answer_kernel(
    capacity,
    ids_ref,
    memory_hbm,
    out_ref,
    codes_ref,
    memory_ref,
    turned_ref,
    asked_ref,
    wanted_ref,
    rows_ref,
    memory_sem,
    load_sem,
    sems,
):
    devices = ids_ref.shape[0]
    memory_load = pltpu.make_async_copy(memory_hbm, memory_ref, memory_sem)
    memory_load.start()
    turned = jnp.transpose(ids_ref[...])[:SUB, :]
    turned_ref[...] = turned
    asked_ref[...] = turned & (ACTIVE - 1)
    load = pltpu.make_async_copy(asked_ref, wanted_ref, load_sem)
    load.start()
    load.wait()
    keep = pltpu.make_async_copy(turned_ref, codes_ref, load_sem)
    keep.start()
    memory_load.wait()
    group = 8
    chunks = sems.shape[0]
    part = devices // chunks
    sends = []
    for q in range(chunks):

        def step(i, carry):
            for a in range(group):
                p = q * part + i * group + a
                for k in range(capacity):
                    rows_ref[p * capacity + k] = memory_ref[wanted_ref[k, p]]
            return carry

        lax.fori_loop(0, part // group, step, 0, unroll=True)
        here = pl.ds(q * part * capacity, part * capacity)
        send = pltpu.make_async_copy(rows_ref.at[here], out_ref.at[here], sems.at[q])
        send.start()
        sends.append(send)
    keep.wait()
    for send in sends:
        send.wait()


def compact_kernel(
    capacity, spare_row, codes_ref, slot_ref, index_ref, count_ref, node_ref, of_ref, size_ref, ids_ref, load_sem
):
    devices = ids_ref.shape[1]
    rows = of_ref.shape[0]
    load = pltpu.make_async_copy(codes_ref, ids_ref, load_sem)
    load.start()
    load.wait()

    def clear(i, carry):
        for a in range(16):
            of_ref[i * 16 + a] = -1
        return carry

    lax.fori_loop(0, rows // 16, clear, 0)

    def choose(p, taken):
        for k in range(capacity):
            code = ids_ref[k, p]
            slot_ref[taken] = p * capacity + k
            index_ref[taken] = code & (ACTIVE - 1)
            taken = taken + (code >= ACTIVE).astype(jnp.int32)
        return taken

    taken = lax.fori_loop(0, devices, choose, jnp.int32(0), unroll=2)

    def number(i, nodes):
        node = index_ref[i]
        known = of_ref[node]
        fresh = known < 0
        index = jnp.where(fresh, nodes, known)
        of_ref[node] = index
        index_ref[i] = index
        node_ref[index] = node
        count_ref[index] = jnp.where(fresh, 0, count_ref[index]) + 1
        return nodes + fresh.astype(jnp.int32)

    nodes = lax.fori_loop(0, taken, number, jnp.int32(0))
    size_ref[0] = taken
    size_ref[1] = nodes
    for a in range(UNROLL):
        slot_ref[taken + a] = 0
        index_ref[taken + a] = spare_row
        count_ref[nodes + a] = 1


def to_matrix(tiles_ref, start, rows):
    parts = [tiles_ref[pl.ds(start * SUB + c, rows, stride=SUB), :].astype(jnp.bfloat16) for c in range(SUB)]
    return jnp.concatenate(parts, axis=1)


def hidden_gates_kernel(
    node_ref,
    size_ref,
    memory_hbm,
    gru_hbm,
    plain_hbm,
    of_ref,
    previous_ref,
    gates_ref,
    kept_ref,
    memory_ref,
    gru_ref,
    plain_ref,
    tiles_ref,
    rows_ref,
    made_ref,
    left_ref,
    sems,
):
    loads = []
    for source, target in ((memory_hbm, memory_ref), (plain_hbm, plain_ref), (gru_hbm, gru_ref)):
        load = pltpu.make_async_copy(source, target, sems.at[3 + len(loads)])
        load.start()
        loads.append(load)
    loads[0].wait()
    loads[1].wait()
    left_ref[...] = jnp.where(of_ref[...] < 0, plain_ref[...].astype(jnp.float32), 0.0).astype(jnp.bfloat16)
    third = pltpu.make_async_copy(left_ref, kept_ref, sems.at[2])
    third.start()
    loads[2].wait()
    steps = jnp.maximum(pl.cdiv(size_ref[1], TILE), 1)
    width = rows_ref.shape[1]

    def block(t, carry):
        def copy(i, c):
            for a in range(16):
                u = i * 16 + a
                row = node_ref[t * TILE + u] & (ACTIVE - 1)
                tiles_ref[pl.ds(pl.multiple_of(u * SUB, SUB), SUB), :] = memory_ref[row].astype(jnp.float32)
            return c

        lax.fori_loop(0, TILE // 16, copy, 0)
        here = pl.ds(pl.multiple_of(t * TILE, TILE), TILE)
        rows_ref[...] = to_matrix(tiles_ref, 0, TILE)
        for j in range(width // COLS):
            for g in range(3):
                made_ref[:, (j * 3 + g) * COLS : (j * 3 + g + 1) * COLS] = jnp.dot(
                    rows_ref[...],
                    gru_ref[:, g * width + j * COLS : g * width + (j + 1) * COLS],
                    preferred_element_type=jnp.float32,
                ).astype(made_ref.dtype)
        first = pltpu.make_async_copy(rows_ref, previous_ref.at[here], sems.at[0])
        second = pltpu.make_async_copy(made_ref, gates_ref.at[here], sems.at[1])
        first.start()
        second.start()
        first.wait()
        second.wait()
        return carry

    lax.fori_loop(0, steps, block, 0)
    third.wait()


def fold_kernel(w2_ref, b2_ref, gru_ref, bias_ref, folded_ref, shift_ref, left_ref):
    hid = w2_ref.shape[0]

    @pl.when(pl.program_id(0) == 0)
    def _():
        left_ref[:hid, :] = w2_ref[...]
        first = b2_ref[...].astype(jnp.bfloat16).astype(jnp.float32)
        rest = b2_ref[...] - first
        second = rest.astype(jnp.bfloat16).astype(jnp.float32)
        rows = lax.broadcasted_iota(jnp.int32, (2 * SUB, b2_ref.shape[1]), 0)
        terms = jnp.where(rows == 0, first, jnp.where(rows == 1, second, jnp.where(rows == 2, rest - second, 0.0)))
        left_ref[hid:, :] = terms.astype(jnp.bfloat16)

    both = jnp.dot(left_ref[...], gru_ref[...], preferred_element_type=jnp.float32)
    folded_ref[...] = both[:hid, :].astype(jnp.bfloat16)
    shift_ref[...] = bias_ref[...] + jnp.sum(both[hid:, :], axis=0, keepdims=True)


def message_kernel(
    place_ref,
    rows_ref,
    feat_ref,
    w1_hbm,
    b1_ref,
    out_ref,
    w1_ref,
    tiles_ref,
    inputs_ref,
    partial_ref,
    got_ref,
    sent_ref,
    sem,
    sems,
):
    events = feat_ref.shape[0]
    depth, hid = w1_ref.shape
    width = (depth - feat_ref.shape[1]) // 2
    group = 16
    loads = []
    for i, rows in enumerate((pl.ds(0, width), pl.ds(width, depth - width))):
        load = pltpu.make_async_copy(w1_hbm.at[rows], w1_ref.at[rows], sems.at[i])
        load.start()
        loads.append(load)
    for half in range(2):

        def fetch(i, c):
            for a in range(group):
                e = i * group + a
                got_ref[e] = rows_ref[place_ref[half, e]]
            return c

        lax.fori_loop(0, events // group, fetch, 0, unroll=True)
        tiles_ref[...] = got_ref[...].astype(jnp.float32).reshape(events * SUB, LANES)
        inputs_ref[:, half * width : (half + 1) * width] = to_matrix(tiles_ref, 0, events)
    inputs_ref[:, 2 * width :] = feat_ref[...]
    loads[0].wait()
    for j in range(hid // COLS):
        cols = slice(j * COLS, (j + 1) * COLS)
        partial_ref[:, cols] = (
            jnp.dot(inputs_ref[:, :width], w1_ref[:width, cols], preferred_element_type=jnp.float32) + b1_ref[:, cols]
        )
    loads[1].wait()
    for j in range(hid // COLS):
        cols = slice(j * COLS, (j + 1) * COLS)
        h = partial_ref[:, cols] + jnp.dot(
            inputs_ref[:, width:], w1_ref[width:, cols], preferred_element_type=jnp.float32
        )
        h = jnp.maximum(h, 0.0)
        for c in range(COLS // LANES):
            tiles_ref[pl.ds(j * (COLS // LANES) + c, events, stride=SUB), :] = h[:, c * LANES : (c + 1) * LANES]

    def send(i, c):
        for a in range(group):
            e = i * group + a
            sent_ref[place_ref[1, e]] = got_ref[e]
        return c

    got_ref[...] = tiles_ref[...].reshape(events, SUB, LANES).astype(jnp.bfloat16)
    lax.fori_loop(0, events // group, send, 0, unroll=True)
    leave = pltpu.make_async_copy(sent_ref, out_ref, sem)
    leave.start()
    leave.wait()


def update_kernel(
    slot_ref,
    index_ref,
    count_ref,
    size_ref,
    incoming_ref,
    of_ref,
    kept_hbm,
    previous_hbm,
    gates_hbm,
    left_in_hbm,
    right_in_hbm,
    left_bias_ref,
    right_bias_ref,
    out_ref,
    final_ref,
    previous_ref,
    gates_ref,
    gru_ref,
    even_ref,
    odd_ref,
    aggregate_ref,
    pick_ref,
    load_sems,
    sems,
):
    width = final_ref.shape[1]
    taken = size_ref[0]
    nodes = size_ref[1]
    steps = jnp.maximum(pl.cdiv(nodes, TILE), 1)
    half = width // 2
    split = left_in_hbm.shape[1]
    first_tile = pl.ds(0, TILE)
    halves = []
    for h in range(2):
        loads = [(gates_hbm.at[first_tile, pl.ds(h * 3 * half, 3 * half)], gates_ref.at[:, pl.ds(h * 3 * half, 3 * half)])]
        for g in range(3):
            first = g * width + h * half
            part = (left_in_hbm, right_in_hbm)[first // split]
            loads.append((part.at[:, pl.ds(first % split, half)], gru_ref.at[:, pl.ds(first, half)]))
        if h == 0:
            loads.append((previous_hbm.at[first_tile], previous_ref))
        else:
            loads.append((kept_hbm, final_ref))
        halves.append([pltpu.make_async_copy(a, b, load_sems.at[h, i]) for i, (a, b) in enumerate(loads)])
    for copy in halves[0] + halves[1]:
        copy.start()

    def clear(t, c):
        here = pl.ds(pl.multiple_of(t * TILE * SUB, TILE * SUB), TILE * SUB)
        even_ref[here, :] = jnp.zeros((TILE * SUB, LANES), jnp.float32)
        odd_ref[here, :] = jnp.zeros((TILE * SUB, LANES), jnp.float32)
        return c

    lax.fori_loop(0, steps, clear, 0)

    def add(i, c):
        for a in range(UNROLL):
            into = odd_ref if a % 2 else even_ref
            here = pl.ds(pl.multiple_of(index_ref[i * UNROLL + a] * SUB, SUB), SUB)
            into[here, :] += incoming_ref[slot_ref[i * UNROLL + a]].astype(jnp.float32)
        return c

    lax.fori_loop(0, pl.cdiv(taken, UNROLL), add, 0)
    def mean(i, c):
        for a in range(UNROLL):
            u = i * UNROLL + a
            here = pl.ds(pl.multiple_of(u * SUB, SUB), SUB)
            even_ref[here, :] = (even_ref[here, :] + odd_ref[here, :]) / count_ref[u].astype(jnp.float32)
        return c

    lax.fori_loop(0, pl.cdiv(nodes, UNROLL), mean, 0)

    def prepare(t):
        aggregate_ref[...] = to_matrix(even_ref, pl.multiple_of(t * TILE, TILE), TILE)
        lane = lax.broadcasted_iota(jnp.int32, (of_ref.shape[0], TILE), 1) + t * TILE
        pick_ref[...] = (of_ref[...] == lane).astype(jnp.float32).astype(jnp.bfloat16)

    def renew(j):
        pre = []
        for g in range(3):
            cols = slice(g * width + j * COLS, g * width + (j + 1) * COLS)
            hid = gates_ref[:, (j * 3 + g) * COLS : (j * 3 + g + 1) * COLS].astype(jnp.float32)
            first = g * width + j * COLS
            bias = (left_bias_ref, right_bias_ref)[first // split][:, first % split : first % split + COLS]
            into = jnp.dot(aggregate_ref[...], gru_ref[:, cols], preferred_element_type=jnp.float32) + bias
            pre.append((into, hid))
        reset = jax.nn.sigmoid(pre[0][0] + pre[0][1])
        update = jax.nn.sigmoid(pre[1][0] + pre[1][1])
        candidate = jnp.tanh(pre[2][0] + reset * pre[2][1])
        previous = previous_ref[:, j * COLS : (j + 1) * COLS].astype(jnp.float32)
        return ((1.0 - update) * candidate + update * previous).astype(jnp.bfloat16)

    def place(j, renewed):
        cols = slice(j * COLS, (j + 1) * COLS)
        for i in range(final_ref.shape[0] // BAND):
            rows = slice(i * BAND, (i + 1) * BAND)
            found = jnp.dot(pick_ref[rows, :], renewed, preferred_element_type=jnp.float32)
            final_ref[rows, cols] = found.astype(jnp.bfloat16) + final_ref[rows, cols]

    per = half // COLS
    prepare(0)
    for copy in halves[0]:
        copy.wait()
    made = [renew(j) for j in range(per)]
    for copy in halves[1]:
        copy.wait()
    sends = [
        pltpu.make_async_copy(
            final_ref.at[:, pl.ds(h * half, half)], out_ref.at[:, pl.ds(h * half, half)], sems.at[h]
        )
        for h in range(2)
    ]
    for j in range(per):
        place(j, made[j])

    @pl.when(steps == 1)
    def _():
        sends[0].start()

    for j in range(per, 2 * per):
        place(j, renew(j))

    @pl.when(steps > 1)
    def _():
        def block(t, c):
            here = pl.ds(pl.multiple_of(t * TILE, TILE), TILE)
            again = [
                pltpu.make_async_copy(gates_hbm.at[here], gates_ref, load_sems.at[0, 0]),
                pltpu.make_async_copy(previous_hbm.at[here], previous_ref, load_sems.at[0, 1]),
            ]
            for copy in again:
                copy.start()
            prepare(t)
            for copy in again:
                copy.wait()
            for j in range(2 * per):
                place(j, renew(j))
            return c

        lax.fori_loop(1, steps, block, 0)
        sends[0].start()

    sends[1].start()
    for send in sends:
        send.wait()


def on_device(
    memory,
    ends_owner,
    ends_row,
    event_mask,
    edge_feat,
    msg_w1,
    msg_b1,
    msg_w2,
    msg_b2,
    gru_in,
    gru_hid,
    gru_bias,
):
    devices = lax.axis_size(AXES)
    events = ends_owner.shape[0]
    node_rows, width = memory.shape
    hid = msg_w2.shape[0]
    capacity = 5 * events // (2 * devices)
    slots = devices * capacity
    padded = pl.cdiv(slots, TILE) * TILE
    cells = width // LANES
    f32, bf16, i32 = jnp.float32, jnp.bfloat16, jnp.int32
    shape = jax.ShapeDtypeStruct

    ids, place = pl.pallas_call(
        lambda *refs: plan_kernel(capacity, *refs),
        out_shape=(shape((devices, LANES), i32), shape((2, events), i32)),
        in_specs=[VM, VM, VM],
        out_specs=(VM, VM),
        compiler_params=pltpu.CompilerParams(vmem_limit_bytes=WHOLE),
        name="plan",
    )(ends_owner.T, ends_row.T, event_mask.reshape(1, events))

    arrived = lax.all_to_all(
        ids.reshape(devices, 1, LANES), AXES, split_axis=0, concat_axis=0, tiled=True
    ).reshape(devices, LANES)
    tiles = memory.reshape(node_rows, cells, LANES)

    answers, codes = pl.pallas_call(
        lambda *refs: answer_kernel(capacity, *refs),
        out_shape=(shape((slots, cells, LANES), bf16), shape((SUB, devices), i32)),
        in_specs=[VM, HBM],
        out_specs=(HBM, HBM),
        scratch_shapes=[
            pltpu.VMEM((node_rows, cells, LANES), bf16),
            pltpu.VMEM((SUB, devices), i32),
            pltpu.VMEM((SUB, devices), i32),
            pltpu.SMEM((SUB, devices), i32),
            pltpu.VMEM((slots, cells, LANES), bf16),
            pltpu.SemaphoreType.DMA,
            pltpu.SemaphoreType.DMA,
            pltpu.SemaphoreType.DMA((4,)),
        ],
        compiler_params=pltpu.CompilerParams(vmem_limit_bytes=ANSWER),
        name="answer",
    )(arrived, tiles)
    returned = lax.all_to_all(
        answers.reshape(devices, capacity, cells, LANES), AXES, split_axis=0, concat_axis=0, tiled=True
    ).reshape(slots, cells, LANES)

    slot, index, count, node, of, size = pl.pallas_call(
        lambda *refs: compact_kernel(capacity, padded, *refs),
        out_shape=(
            shape((1024,), i32),
            shape((1024,), i32),
            shape((1024,), i32),
            shape((1024,), i32),
            shape((node_rows,), i32),
            shape((8,), i32),
        ),
        in_specs=[VM],
        out_specs=(SM, SM, SM, SM, SM, SM),
        scratch_shapes=[pltpu.SMEM((SUB, devices), i32), pltpu.SemaphoreType.DMA],
        compiler_params=pltpu.CompilerParams(vmem_limit_bytes=MOST),
        cost_estimate=pl.CostEstimate(flops=4_000_000_000, bytes_accessed=20_000_000, transcendentals=0),
        name="compact",
    )(codes)

    of = of.reshape(node_rows, 1)
    previous, gates, kept = pl.pallas_call(
        hidden_gates_kernel,
        out_shape=(
            shape((padded, width), bf16),
            shape((padded, 3 * width), GATES),
            shape((node_rows, width), bf16),
        ),
        in_specs=[SM, SM, HBM, HBM, HBM, VM],
        out_specs=(HBM, HBM, HBM),
        scratch_shapes=[
            pltpu.VMEM((node_rows, cells, LANES), bf16),
            pltpu.VMEM((width, 3 * width), bf16),
            pltpu.VMEM((node_rows, width), bf16),
            pltpu.VMEM((TILE * SUB, LANES), f32),
            pltpu.VMEM((TILE, width), bf16),
            pltpu.VMEM((TILE, 3 * width), GATES),
            pltpu.VMEM((node_rows, width), bf16),
            pltpu.SemaphoreType.DMA((6,)),
        ],
        compiler_params=pltpu.CompilerParams(vmem_limit_bytes=WHOLE),
        cost_estimate=pl.CostEstimate(flops=4_000_000_000, bytes_accessed=20_000_000, transcendentals=0),
        name="hidden_gates",
    )(node, size, tiles, gru_hid, memory, of)

    def fold(first, last):
        step = 512
        offset = first // step
        return pl.pallas_call(
            fold_kernel,
            out_shape=(shape((hid, last - first), bf16), shape((1, last - first), f32)),
            grid=((last - first) // step,),
            in_specs=[
                pl.BlockSpec((hid, width), lambda i: (0, 0)),
                pl.BlockSpec((1, width), lambda i: (0, 0)),
                pl.BlockSpec((width, step), lambda i: (0, i + offset)),
                pl.BlockSpec((1, step), lambda i: (0, i + offset)),
            ],
            out_specs=(pl.BlockSpec((hid, step), lambda i: (0, i)), pl.BlockSpec((1, step), lambda i: (0, i))),
            scratch_shapes=[pltpu.VMEM((hid + 2 * SUB, width), bf16)],
            compiler_params=pltpu.CompilerParams(vmem_limit_bytes=WHOLE),
            cost_estimate=pl.CostEstimate(
                flops=2 * hid * width * (last - first), bytes_accessed=4 * width * (last - first), transcendentals=0
            ),
            name="fold",
        )(msg_w2, msg_b2.reshape(1, width), gru_in, gru_bias.reshape(1, 3 * width))

    split = 3 * width // 2
    left_in, left_bias = fold(0, split)
    returned, size, left_in = lax.optimization_barrier((returned, size, left_in))
    outgoing = pl.pallas_call(
        message_kernel,
        out_shape=shape((slots, cells, LANES), bf16),
        in_specs=[SM, VM, VM, HBM, VM],
        out_specs=HBM,
        scratch_shapes=[
            pltpu.VMEM(msg_w1.shape, bf16),
            pltpu.VMEM((events * SUB, LANES), f32),
            pltpu.VMEM((events, msg_w1.shape[0]), bf16),
            pltpu.VMEM((events, hid), f32),
            pltpu.VMEM((events, cells, LANES), bf16),
            pltpu.VMEM((slots, cells, LANES), bf16),
            pltpu.SemaphoreType.DMA,
            pltpu.SemaphoreType.DMA((2,)),
        ],
        compiler_params=pltpu.CompilerParams(vmem_limit_bytes=MOST),
        name="message",
    )(place, returned, edge_feat, msg_w1, msg_b1.reshape(1, hid))
    right_in, right_bias = fold(split, 3 * width)
    incoming = lax.all_to_all(
        outgoing.reshape(devices, capacity, cells, LANES), AXES, split_axis=0, concat_axis=0, tiled=True
    ).reshape(slots, cells, LANES)

    return pl.pallas_call(
        update_kernel,
        out_shape=shape((node_rows, width), bf16),
        in_specs=[SM, SM, SM, SM, VM, VM, HBM, HBM, HBM, HBM, HBM, VM, VM],
        out_specs=HBM,
        scratch_shapes=[
            pltpu.VMEM((node_rows, width), bf16),
            pltpu.VMEM((TILE, width), bf16),
            pltpu.VMEM((TILE, 3 * width), GATES),
            pltpu.VMEM((width, 3 * width), bf16),
            pltpu.VMEM(((padded + 1) * SUB, LANES), f32),
            pltpu.VMEM(((padded + 1) * SUB, LANES), f32),
            pltpu.VMEM((TILE, width), bf16),
            pltpu.VMEM((node_rows, TILE), bf16),
            pltpu.SemaphoreType.DMA((2, 5)),
            pltpu.SemaphoreType.DMA((2,)),
        ],
        compiler_params=pltpu.CompilerParams(vmem_limit_bytes=MOST),
        name="update",
    )(
        slot,
        index,
        count,
        size,
        incoming,
        of,
        kept,
        previous,
        gates,
        left_in,
        right_in,
        left_bias,
        right_bias,
    )


def solution(mesh):
    row = P(AXES, None)
    return jax.shard_map(
        on_device,
        mesh=mesh,
        in_specs=(row, row, row, P(AXES), row, P(), P(), P(), P(), P(), P(), P()),
        out_specs=row,
        check_vma=False,
    )
```

```python
import jax
import jax.numpy as jnp
from jax import lax
from jax.experimental import pallas as pl
from jax.experimental.pallas import tpu as pltpu
from jax.sharding import PartitionSpec as P

AXES = ("node", "tm")
LANES = 128
SUB = 8
ACTIVE = 1024
TILE = 256
COLS = 256
GATES = jnp.bfloat16
UNROLL = 16
BAND = 512
MIB = 1 << 20
WHOLE = 58 * MIB
MOST = 51 * MIB
ANSWER = 51968 * 1024

VM = pl.BlockSpec(memory_space=pltpu.VMEM)
SM = pl.BlockSpec(memory_space=pltpu.SMEM)
HBM = pl.BlockSpec(memory_space=pltpu.HBM)


def plan_kernel(capacity, owner_ref, row_ref, mask_ref, ids_ref, place_ref):
    devices = ids_ref.shape[0]
    events = owner_ref.shape[1]
    ends = 2 * events
    owner = jnp.concatenate([owner_ref[0:1, :], owner_ref[1:2, :]], axis=1)
    code = jnp.concatenate([row_ref[0:1, :], row_ref[1:2, :] + ACTIVE * mask_ref[...]], axis=1)
    named = lax.broadcasted_iota(jnp.int32, (devices, ends), 0) == owner
    named_b = named.astype(jnp.float32).astype(jnp.bfloat16)
    block = (LANES, LANES)
    before = lax.broadcasted_iota(jnp.int32, block, 0) < lax.broadcasted_iota(jnp.int32, block, 1)
    table = jnp.concatenate([before.astype(jnp.float32), jnp.ones(block, jnp.float32)], axis=1).astype(jnp.bfloat16)
    total = jnp.zeros((devices, LANES), jnp.float32)
    counts = []
    for i in range(ends // LANES):
        both = jnp.dot(named_b[:, i * LANES : (i + 1) * LANES], table, preferred_element_type=jnp.float32)
        counts.append(both[:, :LANES] + total)
        total = total + both[:, LANES:]
    count = jnp.concatenate(counts, axis=1)
    position = jnp.sum(jnp.where(named, count, 0.0), axis=0, keepdims=True).astype(jnp.int32)
    place = owner * capacity + position
    place_ref[0:1, :] = place[:, :events]
    place_ref[1:2, :] = place[:, events:]
    here = lax.broadcasted_iota(jnp.int32, (LANES, ends), 0) == position
    low = jnp.where(here, (code & 31).astype(jnp.float32), 0.0).astype(jnp.bfloat16)
    high = jnp.where(here, (code >> 5).astype(jnp.float32), 0.0).astype(jnp.bfloat16)
    contract = (((1,), (1,)), ((), ()))
    low_sum = lax.dot_general(named_b, low, contract, preferred_element_type=jnp.float32)
    high_sum = lax.dot_general(named_b, high, contract, preferred_element_type=jnp.float32)
    ids_ref[...] = (low_sum + 32.0 * high_sum).astype(jnp.int32)


def answer_kernel(
    capacity,
    ids_ref,
    memory_hbm,
    out_ref,
    codes_ref,
    memory_ref,
    turned_ref,
    asked_ref,
    wanted_ref,
    rows_ref,
    memory_sem,
    load_sem,
    sems,
):
    devices = ids_ref.shape[0]
    memory_load = pltpu.make_async_copy(memory_hbm, memory_ref, memory_sem)
    memory_load.start()
    turned = jnp.transpose(ids_ref[...])[:SUB, :]
    turned_ref[...] = turned
    asked_ref[...] = turned & (ACTIVE - 1)
    load = pltpu.make_async_copy(asked_ref, wanted_ref, load_sem)
    load.start()
    load.wait()
    keep = pltpu.make_async_copy(turned_ref, codes_ref, load_sem)
    keep.start()
    memory_load.wait()
    group = 8
    chunks = sems.shape[0]
    part = devices // chunks
    sends = []
    for q in range(chunks):

        def step(i, carry):
            for a in range(group):
                p = q * part + i * group + a
                for k in range(capacity):
                    rows_ref[p * capacity + k] = memory_ref[wanted_ref[k, p]]
            return carry

        lax.fori_loop(0, part // group, step, 0, unroll=True)
        here = pl.ds(q * part * capacity, part * capacity)
        send = pltpu.make_async_copy(rows_ref.at[here], out_ref.at[here], sems.at[q])
        send.start()
        sends.append(send)
    keep.wait()
    for send in sends:
        send.wait()


def compact_kernel(
    capacity, spare_row, codes_ref, slot_ref, index_ref, count_ref, node_ref, of_ref, size_ref, ids_ref, load_sem
):
    devices = ids_ref.shape[1]
    rows = of_ref.shape[0]
    load = pltpu.make_async_copy(codes_ref, ids_ref, load_sem)
    load.start()
    load.wait()

    def clear(i, carry):
        for a in range(16):
            of_ref[i * 16 + a] = -1
        return carry

    lax.fori_loop(0, rows // 16, clear, 0)

    def choose(p, taken):
        for k in range(capacity):
            code = ids_ref[k, p]
            slot_ref[taken] = p * capacity + k
            index_ref[taken] = code & (ACTIVE - 1)
            taken = taken + (code >= ACTIVE).astype(jnp.int32)
        return taken

    taken = lax.fori_loop(0, devices, choose, jnp.int32(0), unroll=2)

    def number(i, nodes):
        node = index_ref[i]
        known = of_ref[node]
        fresh = known < 0
        index = jnp.where(fresh, nodes, known)
        of_ref[node] = index
        index_ref[i] = index
        node_ref[index] = node
        count_ref[index] = jnp.where(fresh, 0, count_ref[index]) + 1
        return nodes + fresh.astype(jnp.int32)

    nodes = lax.fori_loop(0, taken, number, jnp.int32(0))
    size_ref[0] = taken
    size_ref[1] = nodes
    for a in range(UNROLL):
        slot_ref[taken + a] = 0
        index_ref[taken + a] = spare_row
        count_ref[nodes + a] = 1


def to_matrix(tiles_ref, start, rows):
    parts = [tiles_ref[pl.ds(start * SUB + c, rows, stride=SUB), :].astype(jnp.bfloat16) for c in range(SUB)]
    return jnp.concatenate(parts, axis=1)


def hidden_gates_kernel(
    node_ref,
    size_ref,
    memory_ref,
    gru_ref,
    plain_ref,
    of_ref,
    previous_ref,
    gates_ref,
    kept_ref,
    tiles_ref,
    rows_ref,
    made_ref,
    left_ref,
    sems,
):
    left_ref[...] = jnp.where(of_ref[...] < 0, plain_ref[...].astype(jnp.float32), 0.0).astype(jnp.bfloat16)
    third = pltpu.make_async_copy(left_ref, kept_ref, sems.at[2])
    third.start()
    steps = jnp.maximum(pl.cdiv(size_ref[1], TILE), 1)
    width = rows_ref.shape[1]

    def block(t, carry):
        def copy(i, c):
            for a in range(16):
                u = i * 16 + a
                row = node_ref[t * TILE + u] & (ACTIVE - 1)
                tiles_ref[pl.ds(pl.multiple_of(u * SUB, SUB), SUB), :] = memory_ref[row].astype(jnp.float32)
            return c

        lax.fori_loop(0, TILE // 16, copy, 0)
        here = pl.ds(pl.multiple_of(t * TILE, TILE), TILE)
        rows_ref[...] = to_matrix(tiles_ref, 0, TILE)
        for j in range(width // COLS):
            for g in range(3):
                made_ref[:, (j * 3 + g) * COLS : (j * 3 + g + 1) * COLS] = jnp.dot(
                    rows_ref[...],
                    gru_ref[:, g * width + j * COLS : g * width + (j + 1) * COLS],
                    preferred_element_type=jnp.float32,
                ).astype(made_ref.dtype)
        first = pltpu.make_async_copy(rows_ref, previous_ref.at[here], sems.at[0])
        second = pltpu.make_async_copy(made_ref, gates_ref.at[here], sems.at[1])
        first.start()
        second.start()
        first.wait()
        second.wait()
        return carry

    lax.fori_loop(0, steps, block, 0)
    third.wait()


def fold_kernel(w2_ref, b2_ref, gru_ref, bias_ref, folded_ref, shift_ref, left_ref):
    hid = w2_ref.shape[0]

    @pl.when(pl.program_id(0) == 0)
    def _():
        left_ref[:hid, :] = w2_ref[...]
        first = b2_ref[...].astype(jnp.bfloat16).astype(jnp.float32)
        rest = b2_ref[...] - first
        second = rest.astype(jnp.bfloat16).astype(jnp.float32)
        rows = lax.broadcasted_iota(jnp.int32, (2 * SUB, b2_ref.shape[1]), 0)
        terms = jnp.where(rows == 0, first, jnp.where(rows == 1, second, jnp.where(rows == 2, rest - second, 0.0)))
        left_ref[hid:, :] = terms.astype(jnp.bfloat16)

    both = jnp.dot(left_ref[...], gru_ref[...], preferred_element_type=jnp.float32)
    folded_ref[...] = both[:hid, :].astype(jnp.bfloat16)
    shift_ref[...] = bias_ref[...] + jnp.sum(both[hid:, :], axis=0, keepdims=True)


def message_kernel(
    place_ref,
    rows_ref,
    feat_ref,
    w1_hbm,
    b1_ref,
    out_ref,
    w1_ref,
    tiles_ref,
    inputs_ref,
    partial_ref,
    got_ref,
    sent_ref,
    sem,
    sems,
):
    events = feat_ref.shape[0]
    depth, hid = w1_ref.shape
    width = (depth - feat_ref.shape[1]) // 2
    group = 16
    loads = []
    for i, rows in enumerate((pl.ds(0, width), pl.ds(width, depth - width))):
        load = pltpu.make_async_copy(w1_hbm.at[rows], w1_ref.at[rows], sems.at[i])
        load.start()
        loads.append(load)
    for half in range(2):

        def fetch(i, c):
            for a in range(group):
                e = i * group + a
                got_ref[e] = rows_ref[place_ref[half, e]]
            return c

        lax.fori_loop(0, events // group, fetch, 0, unroll=True)
        tiles_ref[...] = got_ref[...].astype(jnp.float32).reshape(events * SUB, LANES)
        inputs_ref[:, half * width : (half + 1) * width] = to_matrix(tiles_ref, 0, events)
    inputs_ref[:, 2 * width :] = feat_ref[...]
    loads[0].wait()
    for j in range(hid // COLS):
        cols = slice(j * COLS, (j + 1) * COLS)
        partial_ref[:, cols] = (
            jnp.dot(inputs_ref[:, :width], w1_ref[:width, cols], preferred_element_type=jnp.float32) + b1_ref[:, cols]
        )
    loads[1].wait()
    for j in range(hid // COLS):
        cols = slice(j * COLS, (j + 1) * COLS)
        h = partial_ref[:, cols] + jnp.dot(
            inputs_ref[:, width:], w1_ref[width:, cols], preferred_element_type=jnp.float32
        )
        h = jnp.maximum(h, 0.0)
        for c in range(COLS // LANES):
            tiles_ref[pl.ds(j * (COLS // LANES) + c, events, stride=SUB), :] = h[:, c * LANES : (c + 1) * LANES]

    def send(i, c):
        for a in range(group):
            e = i * group + a
            sent_ref[place_ref[1, e]] = got_ref[e]
        return c

    got_ref[...] = tiles_ref[...].reshape(events, SUB, LANES).astype(jnp.bfloat16)
    lax.fori_loop(0, events // group, send, 0, unroll=True)
    leave = pltpu.make_async_copy(sent_ref, out_ref, sem)
    leave.start()
    leave.wait()


def update_kernel(
    slot_ref,
    index_ref,
    count_ref,
    size_ref,
    incoming_ref,
    of_ref,
    kept_hbm,
    previous_hbm,
    gates_hbm,
    left_in_hbm,
    right_in_hbm,
    left_bias_ref,
    right_bias_ref,
    out_ref,
    final_ref,
    previous_ref,
    gates_ref,
    gru_ref,
    even_ref,
    odd_ref,
    aggregate_ref,
    pick_ref,
    load_sems,
    sems,
):
    width = final_ref.shape[1]
    taken = size_ref[0]
    nodes = size_ref[1]
    steps = jnp.maximum(pl.cdiv(nodes, TILE), 1)
    half = width // 2
    split = left_in_hbm.shape[1]
    first_tile = pl.ds(0, TILE)
    halves = []
    for h in range(2):
        loads = [(gates_hbm.at[first_tile, pl.ds(h * 3 * half, 3 * half)], gates_ref.at[:, pl.ds(h * 3 * half, 3 * half)])]
        for g in range(3):
            first = g * width + h * half
            part, at = (left_in_hbm, first) if first < split else (right_in_hbm, first - split)
            loads.append((part.at[:, pl.ds(at, half)], gru_ref.at[:, pl.ds(first, half)]))
        if h == 0:
            loads.append((previous_hbm.at[first_tile], previous_ref))
        else:
            loads.append((kept_hbm, final_ref))
        halves.append([pltpu.make_async_copy(a, b, load_sems.at[h, i]) for i, (a, b) in enumerate(loads)])
    for copy in halves[0] + halves[1]:
        copy.start()

    def clear(t, c):
        here = pl.ds(pl.multiple_of(t * TILE * SUB, TILE * SUB), TILE * SUB)
        even_ref[here, :] = jnp.zeros((TILE * SUB, LANES), jnp.float32)
        odd_ref[here, :] = jnp.zeros((TILE * SUB, LANES), jnp.float32)
        return c

    lax.fori_loop(0, steps, clear, 0)

    def add(i, c):
        for a in range(UNROLL):
            into = odd_ref if a % 2 else even_ref
            here = pl.ds(pl.multiple_of(index_ref[i * UNROLL + a] * SUB, SUB), SUB)
            into[here, :] += incoming_ref[slot_ref[i * UNROLL + a]].astype(jnp.float32)
        return c

    lax.fori_loop(0, pl.cdiv(taken, UNROLL), add, 0)
    def mean(i, c):
        for a in range(UNROLL):
            u = i * UNROLL + a
            here = pl.ds(pl.multiple_of(u * SUB, SUB), SUB)
            even_ref[here, :] = (even_ref[here, :] + odd_ref[here, :]) / count_ref[u].astype(jnp.float32)
        return c

    lax.fori_loop(0, pl.cdiv(nodes, UNROLL), mean, 0)

    def prepare(t):
        aggregate_ref[...] = to_matrix(even_ref, pl.multiple_of(t * TILE, TILE), TILE)
        lane = lax.broadcasted_iota(jnp.int32, (of_ref.shape[0], TILE), 1) + t * TILE
        pick_ref[...] = (of_ref[...] == lane).astype(jnp.float32).astype(jnp.bfloat16)

    def renew(j):
        pre = []
        for g in range(3):
            cols = slice(g * width + j * COLS, g * width + (j + 1) * COLS)
            hid = gates_ref[:, (j * 3 + g) * COLS : (j * 3 + g + 1) * COLS].astype(jnp.float32)
            first = g * width + j * COLS
            part, at = (left_bias_ref, first) if first < split else (right_bias_ref, first - split)
            bias = part[:, at : at + COLS]
            into = jnp.dot(aggregate_ref[...], gru_ref[:, cols], preferred_element_type=jnp.float32) + bias
            pre.append((into, hid))
        reset = jax.nn.sigmoid(pre[0][0] + pre[0][1])
        update = jax.nn.sigmoid(pre[1][0] + pre[1][1])
        candidate = jnp.tanh(pre[2][0] + reset * pre[2][1])
        previous = previous_ref[:, j * COLS : (j + 1) * COLS].astype(jnp.float32)
        return ((1.0 - update) * candidate + update * previous).astype(jnp.bfloat16)

    def place(j, renewed):
        cols = slice(j * COLS, (j + 1) * COLS)
        for i in range(final_ref.shape[0] // BAND):
            rows = slice(i * BAND, (i + 1) * BAND)
            found = jnp.dot(pick_ref[rows, :], renewed, preferred_element_type=jnp.float32)
            final_ref[rows, cols] = found.astype(jnp.bfloat16) + final_ref[rows, cols]

    per = half // COLS
    prepare(0)
    for copy in halves[0]:
        copy.wait()
    made = [renew(j) for j in range(per)]
    for copy in halves[1]:
        copy.wait()
    sends = [
        pltpu.make_async_copy(
            final_ref.at[:, pl.ds(h * half, half)], out_ref.at[:, pl.ds(h * half, half)], sems.at[h]
        )
        for h in range(2)
    ]
    for j in range(per):
        place(j, made[j])

    @pl.when(steps == 1)
    def _():
        sends[0].start()

    for j in range(per, 2 * per):
        place(j, renew(j))

    @pl.when(steps > 1)
    def _():
        def block(t, c):
            here = pl.ds(pl.multiple_of(t * TILE, TILE), TILE)
            again = [
                pltpu.make_async_copy(gates_hbm.at[here], gates_ref, load_sems.at[0, 0]),
                pltpu.make_async_copy(previous_hbm.at[here], previous_ref, load_sems.at[0, 1]),
            ]
            for copy in again:
                copy.start()
            prepare(t)
            for copy in again:
                copy.wait()
            for j in range(2 * per):
                place(j, renew(j))
            return c

        lax.fori_loop(1, steps, block, 0)
        sends[0].start()

    sends[1].start()
    for send in sends:
        send.wait()


def on_device(
    memory,
    ends_owner,
    ends_row,
    event_mask,
    edge_feat,
    msg_w1,
    msg_b1,
    msg_w2,
    msg_b2,
    gru_in,
    gru_hid,
    gru_bias,
):
    devices = lax.axis_size(AXES)
    events = ends_owner.shape[0]
    node_rows, width = memory.shape
    hid = msg_w2.shape[0]
    capacity = 5 * events // (2 * devices)
    slots = devices * capacity
    padded = pl.cdiv(slots, TILE) * TILE
    cells = width // LANES
    f32, bf16, i32 = jnp.float32, jnp.bfloat16, jnp.int32
    shape = jax.ShapeDtypeStruct

    ids, place = pl.pallas_call(
        lambda *refs: plan_kernel(capacity, *refs),
        out_shape=(shape((devices, LANES), i32), shape((2, events), i32)),
        in_specs=[VM, VM, VM],
        out_specs=(VM, VM),
        compiler_params=pltpu.CompilerParams(vmem_limit_bytes=WHOLE),
        name="plan",
    )(ends_owner.T, ends_row.T, event_mask.reshape(1, events))

    arrived = lax.all_to_all(
        ids.reshape(devices, 1, LANES), AXES, split_axis=0, concat_axis=0, tiled=True
    ).reshape(devices, LANES)
    tiles = memory.reshape(node_rows, cells, LANES)

    answers, codes = pl.pallas_call(
        lambda *refs: answer_kernel(capacity, *refs),
        out_shape=(shape((slots, cells, LANES), bf16), shape((SUB, devices), i32)),
        in_specs=[VM, HBM],
        out_specs=(HBM, HBM),
        scratch_shapes=[
            pltpu.VMEM((node_rows, cells, LANES), bf16),
            pltpu.VMEM((SUB, devices), i32),
            pltpu.VMEM((SUB, devices), i32),
            pltpu.SMEM((SUB, devices), i32),
            pltpu.VMEM((slots, cells, LANES), bf16),
            pltpu.SemaphoreType.DMA,
            pltpu.SemaphoreType.DMA,
            pltpu.SemaphoreType.DMA((4,)),
        ],
        compiler_params=pltpu.CompilerParams(vmem_limit_bytes=ANSWER),
        name="answer",
    )(arrived, tiles)
    returned = lax.all_to_all(
        answers.reshape(devices, capacity, cells, LANES), AXES, split_axis=0, concat_axis=0, tiled=True
    ).reshape(slots, cells, LANES)

    slot, index, count, node, of, size = pl.pallas_call(
        lambda *refs: compact_kernel(capacity, padded, *refs),
        out_shape=(
            shape((1024,), i32),
            shape((1024,), i32),
            shape((1024,), i32),
            shape((1024,), i32),
            shape((node_rows,), i32),
            shape((8,), i32),
        ),
        in_specs=[VM],
        out_specs=(SM, SM, SM, SM, SM, SM),
        scratch_shapes=[pltpu.SMEM((SUB, devices), i32), pltpu.SemaphoreType.DMA],
        compiler_params=pltpu.CompilerParams(vmem_limit_bytes=MOST),
        cost_estimate=pl.CostEstimate(flops=4_000_000_000, bytes_accessed=20_000_000, transcendentals=0),
        name="compact",
    )(codes)

    of = of.reshape(node_rows, 1)
    previous, gates, kept = pl.pallas_call(
        hidden_gates_kernel,
        out_shape=(
            shape((padded, width), bf16),
            shape((padded, 3 * width), GATES),
            shape((node_rows, width), bf16),
        ),
        in_specs=[SM, SM, VM, VM, VM, VM],
        out_specs=(HBM, HBM, HBM),
        scratch_shapes=[
            pltpu.VMEM((TILE * SUB, LANES), f32),
            pltpu.VMEM((TILE, width), bf16),
            pltpu.VMEM((TILE, 3 * width), GATES),
            pltpu.VMEM((node_rows, width), bf16),
            pltpu.SemaphoreType.DMA((3,)),
        ],
        compiler_params=pltpu.CompilerParams(vmem_limit_bytes=WHOLE),
        cost_estimate=pl.CostEstimate(flops=4_000_000_000, bytes_accessed=20_000_000, transcendentals=0),
        name="hidden_gates",
    )(node, size, tiles, gru_hid, memory, of)

    def fold(first, last):
        step = 512
        offset = first // step
        return pl.pallas_call(
            fold_kernel,
            out_shape=(shape((hid, last - first), bf16), shape((1, last - first), f32)),
            grid=((last - first) // step,),
            in_specs=[
                pl.BlockSpec((hid, width), lambda i: (0, 0)),
                pl.BlockSpec((1, width), lambda i: (0, 0)),
                pl.BlockSpec((width, step), lambda i: (0, i + offset)),
                pl.BlockSpec((1, step), lambda i: (0, i + offset)),
            ],
            out_specs=(pl.BlockSpec((hid, step), lambda i: (0, i)), pl.BlockSpec((1, step), lambda i: (0, i))),
            scratch_shapes=[pltpu.VMEM((hid + 2 * SUB, width), bf16)],
            compiler_params=pltpu.CompilerParams(vmem_limit_bytes=WHOLE),
            cost_estimate=pl.CostEstimate(
                flops=2 * hid * width * (last - first), bytes_accessed=4 * width * (last - first), transcendentals=0
            ),
            name="fold",
        )(msg_w2, msg_b2.reshape(1, width), gru_in, gru_bias.reshape(1, 3 * width))

    split = width
    left_in, left_bias = fold(0, split)
    returned, size, left_in = lax.optimization_barrier((returned, size, left_in))
    outgoing = pl.pallas_call(
        message_kernel,
        out_shape=shape((slots, cells, LANES), bf16),
        in_specs=[SM, VM, VM, HBM, VM],
        out_specs=HBM,
        scratch_shapes=[
            pltpu.VMEM(msg_w1.shape, bf16),
            pltpu.VMEM((events * SUB, LANES), f32),
            pltpu.VMEM((events, msg_w1.shape[0]), bf16),
            pltpu.VMEM((events, hid), f32),
            pltpu.VMEM((events, cells, LANES), bf16),
            pltpu.VMEM((slots, cells, LANES), bf16),
            pltpu.SemaphoreType.DMA,
            pltpu.SemaphoreType.DMA((2,)),
        ],
        compiler_params=pltpu.CompilerParams(vmem_limit_bytes=MOST),
        name="message",
    )(place, returned, edge_feat, msg_w1, msg_b1.reshape(1, hid))
    right_in, right_bias = fold(split, 3 * width)
    incoming = lax.all_to_all(
        outgoing.reshape(devices, capacity, cells, LANES), AXES, split_axis=0, concat_axis=0, tiled=True
    ).reshape(slots, cells, LANES)

    return pl.pallas_call(
        update_kernel,
        out_shape=shape((node_rows, width), bf16),
        in_specs=[SM, SM, SM, SM, VM, VM, HBM, HBM, HBM, HBM, HBM, VM, VM],
        out_specs=HBM,
        scratch_shapes=[
            pltpu.VMEM((node_rows, width), bf16),
            pltpu.VMEM((TILE, width), bf16),
            pltpu.VMEM((TILE, 3 * width), GATES),
            pltpu.VMEM((width, 3 * width), bf16),
            pltpu.VMEM(((padded + 1) * SUB, LANES), f32),
            pltpu.VMEM(((padded + 1) * SUB, LANES), f32),
            pltpu.VMEM((TILE, width), bf16),
            pltpu.VMEM((node_rows, TILE), bf16),
            pltpu.SemaphoreType.DMA((2, 5)),
            pltpu.SemaphoreType.DMA((2,)),
        ],
        compiler_params=pltpu.CompilerParams(vmem_limit_bytes=MOST),
        name="update",
    )(
        slot,
        index,
        count,
        size,
        incoming,
        of,
        kept,
        previous,
        gates,
        left_in,
        right_in,
        left_bias,
        right_bias,
    )


def solution(mesh):
    row = P(AXES, None)
    return jax.shard_map(
        on_device,
        mesh=mesh,
        in_specs=(row, row, row, P(AXES), row, P(), P(), P(), P(), P(), P(), P()),
        out_specs=row,
        check_vma=False,
    )
```

```python
import jax
import jax.numpy as jnp
from jax import lax
from jax.experimental import pallas as pl
from jax.experimental.pallas import tpu as pltpu
from jax.sharding import PartitionSpec as P

AXES = ("node", "tm")
LANES = 128
SUB = 8
ACTIVE = 1024
TILE = 256
COLS = 256
GATES = jnp.bfloat16
UNROLL = 16
BAND = 512
MIB = 1 << 20
WHOLE = 58 * MIB
MOST = 51 * MIB
MESSAGE = 48 * MIB
ANSWER = 48 * MIB

VM = pl.BlockSpec(memory_space=pltpu.VMEM)
SM = pl.BlockSpec(memory_space=pltpu.SMEM)
HBM = pl.BlockSpec(memory_space=pltpu.HBM)


def plan_kernel(capacity, owner_ref, row_ref, mask_ref, ids_ref, place_ref):
    devices = ids_ref.shape[0]
    events = owner_ref.shape[1]
    ends = 2 * events
    owner = jnp.concatenate([owner_ref[0:1, :], owner_ref[1:2, :]], axis=1)
    code = jnp.concatenate([row_ref[0:1, :], row_ref[1:2, :] + ACTIVE * mask_ref[...]], axis=1)
    named = lax.broadcasted_iota(jnp.int32, (devices, ends), 0) == owner
    named_b = named.astype(jnp.float32).astype(jnp.bfloat16)
    block = (LANES, LANES)
    before = lax.broadcasted_iota(jnp.int32, block, 0) < lax.broadcasted_iota(jnp.int32, block, 1)
    table = jnp.concatenate([before.astype(jnp.float32), jnp.ones(block, jnp.float32)], axis=1).astype(jnp.bfloat16)
    total = jnp.zeros((devices, LANES), jnp.float32)
    counts = []
    for i in range(ends // LANES):
        both = jnp.dot(named_b[:, i * LANES : (i + 1) * LANES], table, preferred_element_type=jnp.float32)
        counts.append(both[:, :LANES] + total)
        total = total + both[:, LANES:]
    count = jnp.concatenate(counts, axis=1)
    position = jnp.sum(jnp.where(named, count, 0.0), axis=0, keepdims=True).astype(jnp.int32)
    place = owner * capacity + position
    place_ref[0:1, :] = place[:, :events]
    place_ref[1:2, :] = place[:, events:]
    here = lax.broadcasted_iota(jnp.int32, (LANES, ends), 0) == position
    low = jnp.where(here, (code & 31).astype(jnp.float32), 0.0).astype(jnp.bfloat16)
    high = jnp.where(here, (code >> 5).astype(jnp.float32), 0.0).astype(jnp.bfloat16)
    contract = (((1,), (1,)), ((), ()))
    low_sum = lax.dot_general(named_b, low, contract, preferred_element_type=jnp.float32)
    high_sum = lax.dot_general(named_b, high, contract, preferred_element_type=jnp.float32)
    ids_ref[...] = (low_sum + 32.0 * high_sum).astype(jnp.int32)


def answer_kernel(
    capacity,
    ids_ref,
    memory_ref,
    out_ref,
    codes_ref,
    turned_ref,
    asked_ref,
    wanted_ref,
    rows_ref,
    load_sem,
    sems,
):
    devices = ids_ref.shape[0]
    turned = jnp.transpose(ids_ref[...])[:SUB, :]
    turned_ref[...] = turned
    asked_ref[...] = turned & (ACTIVE - 1)
    load = pltpu.make_async_copy(asked_ref, wanted_ref, load_sem)
    load.start()
    load.wait()
    keep = pltpu.make_async_copy(turned_ref, codes_ref, load_sem)
    keep.start()
    group = 8
    chunks = sems.shape[0]
    part = devices // chunks
    sends = []
    for q in range(chunks):

        def step(i, carry):
            for a in range(group):
                p = q * part + i * group + a
                for k in range(capacity):
                    rows_ref[p * capacity + k] = memory_ref[wanted_ref[k, p]]
            return carry

        lax.fori_loop(0, part // group, step, 0, unroll=True)
        here = pl.ds(q * part * capacity, part * capacity)
        send = pltpu.make_async_copy(rows_ref.at[here], out_ref.at[here], sems.at[q])
        send.start()
        sends.append(send)
    keep.wait()
    for send in sends:
        send.wait()


def compact_kernel(
    capacity, spare_row, codes_ref, slot_ref, index_ref, count_ref, node_ref, of_ref, size_ref, ids_ref, load_sem
):
    devices = ids_ref.shape[1]
    rows = of_ref.shape[0]
    load = pltpu.make_async_copy(codes_ref, ids_ref, load_sem)
    load.start()
    load.wait()

    def clear(i, carry):
        for a in range(16):
            of_ref[i * 16 + a] = -1
        return carry

    lax.fori_loop(0, rows // 16, clear, 0)

    def choose(p, taken):
        for k in range(capacity):
            code = ids_ref[k, p]
            slot_ref[taken] = p * capacity + k
            index_ref[taken] = code & (ACTIVE - 1)
            taken = taken + (code >= ACTIVE).astype(jnp.int32)
        return taken

    taken = lax.fori_loop(0, devices, choose, jnp.int32(0), unroll=2)

    def number(i, nodes):
        node = index_ref[i]
        known = of_ref[node]
        fresh = known < 0
        index = jnp.where(fresh, nodes, known)
        of_ref[node] = index
        index_ref[i] = index
        node_ref[index] = node
        count_ref[index] = jnp.where(fresh, 0, count_ref[index]) + 1
        return nodes + fresh.astype(jnp.int32)

    nodes = lax.fori_loop(0, taken, number, jnp.int32(0))
    size_ref[0] = taken
    size_ref[1] = nodes
    for a in range(UNROLL):
        slot_ref[taken + a] = 0
        index_ref[taken + a] = spare_row
        count_ref[nodes + a] = 1


def to_matrix(tiles_ref, start, rows):
    parts = [tiles_ref[pl.ds(start * SUB + c, rows, stride=SUB), :].astype(jnp.bfloat16) for c in range(SUB)]
    return jnp.concatenate(parts, axis=1)


def hidden_gates_kernel(
    node_ref,
    size_ref,
    memory_ref,
    gru_ref,
    plain_ref,
    of_ref,
    previous_ref,
    gates_ref,
    kept_ref,
    tiles_ref,
    rows_ref,
    made_ref,
    left_ref,
    sems,
):
    left_ref[...] = jnp.where(of_ref[...] < 0, plain_ref[...].astype(jnp.float32), 0.0).astype(jnp.bfloat16)
    third = pltpu.make_async_copy(left_ref, kept_ref, sems.at[2])
    third.start()
    steps = jnp.maximum(pl.cdiv(size_ref[1], TILE), 1)
    width = rows_ref.shape[1]

    def block(t, carry):
        def copy(i, c):
            for a in range(16):
                u = i * 16 + a
                row = node_ref[t * TILE + u] & (ACTIVE - 1)
                tiles_ref[pl.ds(pl.multiple_of(u * SUB, SUB), SUB), :] = memory_ref[row].astype(jnp.float32)
            return c

        lax.fori_loop(0, TILE // 16, copy, 0)
        here = pl.ds(pl.multiple_of(t * TILE, TILE), TILE)
        rows_ref[...] = to_matrix(tiles_ref, 0, TILE)
        for j in range(width // COLS):
            for g in range(3):
                made_ref[:, (j * 3 + g) * COLS : (j * 3 + g + 1) * COLS] = jnp.dot(
                    rows_ref[...],
                    gru_ref[:, g * width + j * COLS : g * width + (j + 1) * COLS],
                    preferred_element_type=jnp.float32,
                ).astype(made_ref.dtype)
        first = pltpu.make_async_copy(rows_ref, previous_ref.at[here], sems.at[0])
        second = pltpu.make_async_copy(made_ref, gates_ref.at[here], sems.at[1])
        first.start()
        second.start()
        first.wait()
        second.wait()
        return carry

    lax.fori_loop(0, steps, block, 0)
    third.wait()


def fold_kernel(w2_ref, b2_ref, gru_ref, bias_ref, folded_ref, shift_ref, left_ref):
    hid = w2_ref.shape[0]

    @pl.when(pl.program_id(0) == 0)
    def _():
        left_ref[:hid, :] = w2_ref[...]
        first = b2_ref[...].astype(jnp.bfloat16).astype(jnp.float32)
        rest = b2_ref[...] - first
        second = rest.astype(jnp.bfloat16).astype(jnp.float32)
        rows = lax.broadcasted_iota(jnp.int32, (2 * SUB, b2_ref.shape[1]), 0)
        terms = jnp.where(rows == 0, first, jnp.where(rows == 1, second, jnp.where(rows == 2, rest - second, 0.0)))
        left_ref[hid:, :] = terms.astype(jnp.bfloat16)

    both = jnp.dot(left_ref[...], gru_ref[...], preferred_element_type=jnp.float32)
    folded_ref[...] = both[:hid, :].astype(jnp.bfloat16)
    shift_ref[...] = bias_ref[...] + jnp.sum(both[hid:, :], axis=0, keepdims=True)


def message_kernel(
    place_ref,
    rows_ref,
    feat_ref,
    w1_first_ref,
    w1_hbm,
    b1_ref,
    out_ref,
    w1_ref,
    tiles_ref,
    inputs_ref,
    partial_ref,
    got_ref,
    sent_ref,
    sem,
):
    events = feat_ref.shape[0]
    width, hid = w1_first_ref.shape
    group = 16
    load = pltpu.make_async_copy(w1_hbm.at[pl.ds(width, w1_ref.shape[0])], w1_ref, sem)
    load.start()
    for half in range(2):

        def fetch(i, c):
            for a in range(group):
                e = i * group + a
                got_ref[e] = rows_ref[place_ref[half, e]]
            return c

        lax.fori_loop(0, events // group, fetch, 0, unroll=True)
        tiles_ref[...] = got_ref[...].astype(jnp.float32).reshape(events * SUB, LANES)
        inputs_ref[:, half * width : (half + 1) * width] = to_matrix(tiles_ref, 0, events)
    inputs_ref[:, 2 * width :] = feat_ref[...]
    for j in range(hid // COLS):
        cols = slice(j * COLS, (j + 1) * COLS)
        partial_ref[:, cols] = (
            jnp.dot(inputs_ref[:, :width], w1_first_ref[:, cols], preferred_element_type=jnp.float32) + b1_ref[:, cols]
        )
    load.wait()
    for j in range(hid // COLS):
        cols = slice(j * COLS, (j + 1) * COLS)
        h = partial_ref[:, cols] + jnp.dot(
            inputs_ref[:, width:], w1_ref[:, cols], preferred_element_type=jnp.float32
        )
        h = jnp.maximum(h, 0.0)
        for c in range(COLS // LANES):
            tiles_ref[pl.ds(j * (COLS // LANES) + c, events, stride=SUB), :] = h[:, c * LANES : (c + 1) * LANES]

    def send(i, c):
        for a in range(group):
            e = i * group + a
            sent_ref[place_ref[1, e]] = got_ref[e]
        return c

    got_ref[...] = tiles_ref[...].reshape(events, SUB, LANES).astype(jnp.bfloat16)
    lax.fori_loop(0, events // group, send, 0, unroll=True)
    leave = pltpu.make_async_copy(sent_ref, out_ref, sem)
    leave.start()
    leave.wait()


def update_kernel(
    slot_ref,
    index_ref,
    count_ref,
    size_ref,
    incoming_ref,
    of_ref,
    kept_hbm,
    previous_hbm,
    gates_hbm,
    left_in_hbm,
    right_in_hbm,
    left_bias_ref,
    right_bias_ref,
    out_ref,
    final_ref,
    previous_ref,
    gates_ref,
    gru_ref,
    even_ref,
    odd_ref,
    aggregate_ref,
    pick_ref,
    load_sems,
    sems,
):
    width = final_ref.shape[1]
    taken = size_ref[0]
    nodes = size_ref[1]
    steps = jnp.maximum(pl.cdiv(nodes, TILE), 1)
    half = width // 2
    split = left_in_hbm.shape[1]
    first_tile = pl.ds(0, TILE)
    halves = []
    for h in range(2):
        loads = [(gates_hbm.at[first_tile, pl.ds(h * 3 * half, 3 * half)], gates_ref.at[:, pl.ds(h * 3 * half, 3 * half)])]
        for g in range(3):
            first = g * width + h * half
            part, at = (left_in_hbm, first) if first < split else (right_in_hbm, first - split)
            loads.append((part.at[:, pl.ds(at, half)], gru_ref.at[:, pl.ds(first, half)]))
        if h == 0:
            loads.append((previous_hbm.at[first_tile], previous_ref))
        else:
            loads.append((kept_hbm, final_ref))
        halves.append([pltpu.make_async_copy(a, b, load_sems.at[h, i]) for i, (a, b) in enumerate(loads)])
    for copy in halves[0] + halves[1]:
        copy.start()

    def clear(t, c):
        here = pl.ds(pl.multiple_of(t * TILE * SUB, TILE * SUB), TILE * SUB)
        even_ref[here, :] = jnp.zeros((TILE * SUB, LANES), jnp.float32)
        odd_ref[here, :] = jnp.zeros((TILE * SUB, LANES), jnp.float32)
        return c

    lax.fori_loop(0, steps, clear, 0)

    def add(i, c):
        for a in range(UNROLL):
            into = odd_ref if a % 2 else even_ref
            here = pl.ds(pl.multiple_of(index_ref[i * UNROLL + a] * SUB, SUB), SUB)
            into[here, :] += incoming_ref[slot_ref[i * UNROLL + a]].astype(jnp.float32)
        return c

    lax.fori_loop(0, pl.cdiv(taken, UNROLL), add, 0)
    def mean(i, c):
        for a in range(UNROLL):
            u = i * UNROLL + a
            here = pl.ds(pl.multiple_of(u * SUB, SUB), SUB)
            even_ref[here, :] = (even_ref[here, :] + odd_ref[here, :]) / count_ref[u].astype(jnp.float32)
        return c

    lax.fori_loop(0, pl.cdiv(nodes, UNROLL), mean, 0)

    def prepare(t):
        aggregate_ref[...] = to_matrix(even_ref, pl.multiple_of(t * TILE, TILE), TILE)
        lane = lax.broadcasted_iota(jnp.int32, (of_ref.shape[0], TILE), 1) + t * TILE
        pick_ref[...] = (of_ref[...] == lane).astype(jnp.float32).astype(jnp.bfloat16)

    def renew(j):
        pre = []
        for g in range(3):
            cols = slice(g * width + j * COLS, g * width + (j + 1) * COLS)
            hid = gates_ref[:, (j * 3 + g) * COLS : (j * 3 + g + 1) * COLS].astype(jnp.float32)
            first = g * width + j * COLS
            part, at = (left_bias_ref, first) if first < split else (right_bias_ref, first - split)
            bias = part[:, at : at + COLS]
            into = jnp.dot(aggregate_ref[...], gru_ref[:, cols], preferred_element_type=jnp.float32) + bias
            pre.append((into, hid))
        reset = jax.nn.sigmoid(pre[0][0] + pre[0][1])
        update = jax.nn.sigmoid(pre[1][0] + pre[1][1])
        candidate = jnp.tanh(pre[2][0] + reset * pre[2][1])
        previous = previous_ref[:, j * COLS : (j + 1) * COLS].astype(jnp.float32)
        return ((1.0 - update) * candidate + update * previous).astype(jnp.bfloat16)

    def place(j, renewed):
        cols = slice(j * COLS, (j + 1) * COLS)
        for i in range(final_ref.shape[0] // BAND):
            rows = slice(i * BAND, (i + 1) * BAND)
            found = jnp.dot(pick_ref[rows, :], renewed, preferred_element_type=jnp.float32)
            final_ref[rows, cols] = found.astype(jnp.bfloat16) + final_ref[rows, cols]

    per = half // COLS
    prepare(0)
    for copy in halves[0]:
        copy.wait()
    made = [renew(j) for j in range(per)]
    for copy in halves[1]:
        copy.wait()
    sends = [
        pltpu.make_async_copy(
            final_ref.at[:, pl.ds(h * half, half)], out_ref.at[:, pl.ds(h * half, half)], sems.at[h]
        )
        for h in range(2)
    ]
    for j in range(per):
        place(j, made[j])

    @pl.when(steps == 1)
    def _():
        sends[0].start()

    for j in range(per, 2 * per):
        place(j, renew(j))

    @pl.when(steps > 1)
    def _():
        def block(t, c):
            here = pl.ds(pl.multiple_of(t * TILE, TILE), TILE)
            again = [
                pltpu.make_async_copy(gates_hbm.at[here], gates_ref, load_sems.at[0, 0]),
                pltpu.make_async_copy(previous_hbm.at[here], previous_ref, load_sems.at[0, 1]),
            ]
            for copy in again:
                copy.start()
            prepare(t)
            for copy in again:
                copy.wait()
            for j in range(2 * per):
                place(j, renew(j))
            return c

        lax.fori_loop(1, steps, block, 0)
        sends[0].start()

    sends[1].start()
    for send in sends:
        send.wait()


def on_device(
    memory,
    ends_owner,
    ends_row,
    event_mask,
    edge_feat,
    msg_w1,
    msg_b1,
    msg_w2,
    msg_b2,
    gru_in,
    gru_hid,
    gru_bias,
):
    devices = lax.axis_size(AXES)
    events = ends_owner.shape[0]
    node_rows, width = memory.shape
    hid = msg_w2.shape[0]
    capacity = 5 * events // (2 * devices)
    slots = devices * capacity
    padded = pl.cdiv(slots, TILE) * TILE
    cells = width // LANES
    f32, bf16, i32 = jnp.float32, jnp.bfloat16, jnp.int32
    shape = jax.ShapeDtypeStruct

    ids, place = pl.pallas_call(
        lambda *refs: plan_kernel(capacity, *refs),
        out_shape=(shape((devices, LANES), i32), shape((2, events), i32)),
        in_specs=[VM, VM, VM],
        out_specs=(VM, VM),
        compiler_params=pltpu.CompilerParams(vmem_limit_bytes=WHOLE),
        name="plan",
    )(ends_owner.T, ends_row.T, event_mask.reshape(1, events))

    arrived = lax.all_to_all(
        ids.reshape(devices, 1, LANES), AXES, split_axis=0, concat_axis=0, tiled=True
    ).reshape(devices, LANES)
    tiles = memory.reshape(node_rows, cells, LANES)

    answers, codes = pl.pallas_call(
        lambda *refs: answer_kernel(capacity, *refs),
        out_shape=(pltpu.HBM((slots, cells, LANES), bf16), pltpu.HBM((SUB, devices), i32)),
        in_specs=[VM, VM],
        out_specs=(HBM, HBM),
        scratch_shapes=[
            pltpu.VMEM((SUB, devices), i32),
            pltpu.VMEM((SUB, devices), i32),
            pltpu.SMEM((SUB, devices), i32),
            pltpu.VMEM((slots, cells, LANES), bf16),
            pltpu.SemaphoreType.DMA,
            pltpu.SemaphoreType.DMA((4,)),
        ],
        compiler_params=pltpu.CompilerParams(vmem_limit_bytes=ANSWER),
        name="answer",
    )(arrived, tiles)
    returned = lax.all_to_all(
        answers.reshape(devices, capacity, cells, LANES), AXES, split_axis=0, concat_axis=0, tiled=True
    ).reshape(slots, cells, LANES)

    slot, index, count, node, of, size = pl.pallas_call(
        lambda *refs: compact_kernel(capacity, padded, *refs),
        out_shape=(
            shape((1024,), i32),
            shape((1024,), i32),
            shape((1024,), i32),
            shape((1024,), i32),
            shape((node_rows,), i32),
            shape((8,), i32),
        ),
        in_specs=[VM],
        out_specs=(SM, SM, SM, SM, SM, SM),
        scratch_shapes=[pltpu.SMEM((SUB, devices), i32), pltpu.SemaphoreType.DMA],
        compiler_params=pltpu.CompilerParams(vmem_limit_bytes=MOST),
        cost_estimate=pl.CostEstimate(flops=4_000_000_000, bytes_accessed=20_000_000, transcendentals=0),
        name="compact",
    )(codes)

    of = of.reshape(node_rows, 1)
    previous, gates, kept = pl.pallas_call(
        hidden_gates_kernel,
        out_shape=(
            shape((padded, width), bf16),
            shape((padded, 3 * width), GATES),
            shape((node_rows, width), bf16),
        ),
        in_specs=[SM, SM, VM, VM, VM, VM],
        out_specs=(HBM, HBM, HBM),
        scratch_shapes=[
            pltpu.VMEM((TILE * SUB, LANES), f32),
            pltpu.VMEM((TILE, width), bf16),
            pltpu.VMEM((TILE, 3 * width), GATES),
            pltpu.VMEM((node_rows, width), bf16),
            pltpu.SemaphoreType.DMA((3,)),
        ],
        compiler_params=pltpu.CompilerParams(vmem_limit_bytes=WHOLE),
        cost_estimate=pl.CostEstimate(flops=4_000_000_000, bytes_accessed=20_000_000, transcendentals=0),
        name="hidden_gates",
    )(node, size, tiles, gru_hid, memory, of)

    def fold(first, last):
        step = 512
        offset = first // step
        return pl.pallas_call(
            fold_kernel,
            out_shape=(shape((hid, last - first), bf16), shape((1, last - first), f32)),
            grid=((last - first) // step,),
            in_specs=[
                pl.BlockSpec((hid, width), lambda i: (0, 0)),
                pl.BlockSpec((1, width), lambda i: (0, 0)),
                pl.BlockSpec((width, step), lambda i: (0, i + offset)),
                pl.BlockSpec((1, step), lambda i: (0, i + offset)),
            ],
            out_specs=(pl.BlockSpec((hid, step), lambda i: (0, i)), pl.BlockSpec((1, step), lambda i: (0, i))),
            scratch_shapes=[pltpu.VMEM((hid + 2 * SUB, width), bf16)],
            compiler_params=pltpu.CompilerParams(vmem_limit_bytes=WHOLE),
            cost_estimate=pl.CostEstimate(
                flops=2 * hid * width * (last - first), bytes_accessed=4 * width * (last - first), transcendentals=0
            ),
            name="fold",
        )(msg_w2, msg_b2.reshape(1, width), gru_in, gru_bias.reshape(1, 3 * width))

    split = width
    left_in, left_bias = fold(0, split)
    returned, size, left_in = lax.optimization_barrier((returned, size, left_in))
    outgoing = pl.pallas_call(
        message_kernel,
        out_shape=pltpu.HBM((slots, cells, LANES), bf16),
        in_specs=[SM, VM, VM, VM, HBM, VM],
        out_specs=HBM,
        scratch_shapes=[
            pltpu.VMEM((msg_w1.shape[0] - width, hid), bf16),
            pltpu.VMEM((events * SUB, LANES), f32),
            pltpu.VMEM((events, msg_w1.shape[0]), bf16),
            pltpu.VMEM((events, hid), f32),
            pltpu.VMEM((events, cells, LANES), bf16),
            pltpu.VMEM((slots, cells, LANES), bf16),
            pltpu.SemaphoreType.DMA,
        ],
        compiler_params=pltpu.CompilerParams(vmem_limit_bytes=MESSAGE),
        name="message",
    )(place, returned, edge_feat, msg_w1[:width], msg_w1, msg_b1.reshape(1, hid))
    right_in, right_bias = fold(split, 3 * width)
    incoming = lax.all_to_all(
        outgoing.reshape(devices, capacity, cells, LANES), AXES, split_axis=0, concat_axis=0, tiled=True
    ).reshape(slots, cells, LANES)

    return pl.pallas_call(
        update_kernel,
        out_shape=shape((node_rows, width), bf16),
        in_specs=[SM, SM, SM, SM, VM, VM, HBM, HBM, HBM, HBM, HBM, VM, VM],
        out_specs=HBM,
        scratch_shapes=[
            pltpu.VMEM((node_rows, width), bf16),
            pltpu.VMEM((TILE, width), bf16),
            pltpu.VMEM((TILE, 3 * width), GATES),
            pltpu.VMEM((width, 3 * width), bf16),
            pltpu.VMEM(((padded + 1) * SUB, LANES), f32),
            pltpu.VMEM(((padded + 1) * SUB, LANES), f32),
            pltpu.VMEM((TILE, width), bf16),
            pltpu.VMEM((node_rows, TILE), bf16),
            pltpu.SemaphoreType.DMA((2, 5)),
            pltpu.SemaphoreType.DMA((2,)),
        ],
        compiler_params=pltpu.CompilerParams(vmem_limit_bytes=MOST),
        name="update",
    )(
        slot,
        index,
        count,
        size,
        incoming,
        of,
        kept,
        previous,
        gates,
        left_in,
        right_in,
        left_bias,
        right_bias,
    )


def solution(mesh):
    row = P(AXES, None)
    return jax.shard_map(
        on_device,
        mesh=mesh,
        in_specs=(row, row, row, P(AXES), row, P(), P(), P(), P(), P(), P(), P()),
        out_specs=row,
        check_vma=False,
    )
```

```python
import jax
import jax.numpy as jnp
from jax import lax
from jax.experimental import pallas as pl
from jax.experimental.pallas import tpu as pltpu
from jax.sharding import PartitionSpec as P

AXES = ("node", "tm")
LANES = 128
SUB = 8
ACTIVE = 1024
TILE = 256
COLS = 256
GATES = jnp.bfloat16
UNROLL = 16
BAND = 512
MIB = 1 << 20
WHOLE = 58 * MIB
MOST = 51 * MIB
MESSAGE = 48 * MIB
SMALL = 48 * MIB
ANSWER = 48 * MIB

VM = pl.BlockSpec(memory_space=pltpu.VMEM)
SM = pl.BlockSpec(memory_space=pltpu.SMEM)
HBM = pl.BlockSpec(memory_space=pltpu.HBM)


def plan_kernel(capacity, owner_ref, row_ref, mask_ref, ids_ref, place_ref):
    devices = ids_ref.shape[0]
    events = owner_ref.shape[1]
    ends = 2 * events
    owner = jnp.concatenate([owner_ref[0:1, :], owner_ref[1:2, :]], axis=1)
    code = jnp.concatenate([row_ref[0:1, :], row_ref[1:2, :] + ACTIVE * mask_ref[...]], axis=1)
    named = lax.broadcasted_iota(jnp.int32, (devices, ends), 0) == owner
    named_b = named.astype(jnp.float32).astype(jnp.bfloat16)
    block = (LANES, LANES)
    before = lax.broadcasted_iota(jnp.int32, block, 0) < lax.broadcasted_iota(jnp.int32, block, 1)
    table = jnp.concatenate([before.astype(jnp.float32), jnp.ones(block, jnp.float32)], axis=1).astype(jnp.bfloat16)
    total = jnp.zeros((devices, LANES), jnp.float32)
    counts = []
    for i in range(ends // LANES):
        both = jnp.dot(named_b[:, i * LANES : (i + 1) * LANES], table, preferred_element_type=jnp.float32)
        counts.append(both[:, :LANES] + total)
        total = total + both[:, LANES:]
    count = jnp.concatenate(counts, axis=1)
    position = jnp.sum(jnp.where(named, count, 0.0), axis=0, keepdims=True).astype(jnp.int32)
    place = owner * capacity + position
    place_ref[0:1, :] = place[:, :events]
    place_ref[1:2, :] = place[:, events:]
    here = lax.broadcasted_iota(jnp.int32, (LANES, ends), 0) == position
    low = jnp.where(here, (code & 31).astype(jnp.float32), 0.0).astype(jnp.bfloat16)
    high = jnp.where(here, (code >> 5).astype(jnp.float32), 0.0).astype(jnp.bfloat16)
    contract = (((1,), (1,)), ((), ()))
    low_sum = lax.dot_general(named_b, low, contract, preferred_element_type=jnp.float32)
    high_sum = lax.dot_general(named_b, high, contract, preferred_element_type=jnp.float32)
    ids_ref[...] = (low_sum + 32.0 * high_sum).astype(jnp.int32)


def answer_kernel(
    capacity,
    ids_ref,
    memory_ref,
    out_ref,
    codes_ref,
    turned_ref,
    asked_ref,
    wanted_ref,
    rows_ref,
    load_sem,
    sems,
):
    devices = ids_ref.shape[0]
    turned = jnp.transpose(ids_ref[...])[:SUB, :]
    turned_ref[...] = turned
    asked_ref[...] = turned & (ACTIVE - 1)
    load = pltpu.make_async_copy(asked_ref, wanted_ref, load_sem)
    load.start()
    load.wait()
    keep = pltpu.make_async_copy(turned_ref, codes_ref, load_sem)
    keep.start()
    group = 8
    chunks = sems.shape[0]
    part = devices // chunks
    sends = []
    for q in range(chunks):

        def step(i, carry):
            for a in range(group):
                p = q * part + i * group + a
                for k in range(capacity):
                    rows_ref[p * capacity + k] = memory_ref[wanted_ref[k, p]]
            return carry

        lax.fori_loop(0, part // group, step, 0, unroll=True)
        here = pl.ds(q * part * capacity, part * capacity)
        send = pltpu.make_async_copy(rows_ref.at[here], out_ref.at[here], sems.at[q])
        send.start()
        sends.append(send)
    keep.wait()
    for send in sends:
        send.wait()


def compact_kernel(
    capacity, spare_row, codes_ref, slot_ref, index_ref, count_ref, node_ref, of_ref, size_ref, ids_ref, load_sem
):
    devices = ids_ref.shape[1]
    rows = of_ref.shape[0]
    load = pltpu.make_async_copy(codes_ref, ids_ref, load_sem)
    load.start()
    load.wait()

    def clear(i, carry):
        for a in range(16):
            of_ref[i * 16 + a] = -1
        return carry

    lax.fori_loop(0, rows // 16, clear, 0)

    def choose(p, taken):
        for k in range(capacity):
            code = ids_ref[k, p]
            slot_ref[taken] = p * capacity + k
            index_ref[taken] = code & (ACTIVE - 1)
            taken = taken + (code >= ACTIVE).astype(jnp.int32)
        return taken

    taken = lax.fori_loop(0, devices, choose, jnp.int32(0), unroll=2)

    def number(i, nodes):
        node = index_ref[i]
        known = of_ref[node]
        fresh = known < 0
        index = jnp.where(fresh, nodes, known)
        of_ref[node] = index
        index_ref[i] = index
        node_ref[index] = node
        count_ref[index] = jnp.where(fresh, 0, count_ref[index]) + 1
        return nodes + fresh.astype(jnp.int32)

    nodes = lax.fori_loop(0, taken, number, jnp.int32(0))
    size_ref[0] = taken
    size_ref[1] = nodes
    for a in range(UNROLL):
        slot_ref[taken + a] = 0
        index_ref[taken + a] = spare_row
        count_ref[nodes + a] = 1


def to_matrix(tiles_ref, start, rows):
    parts = [tiles_ref[pl.ds(start * SUB + c, rows, stride=SUB), :].astype(jnp.bfloat16) for c in range(SUB)]
    return jnp.concatenate(parts, axis=1)


def hidden_gates_kernel(
    node_ref,
    size_ref,
    memory_ref,
    gru_ref,
    plain_ref,
    of_ref,
    previous_ref,
    gates_ref,
    kept_ref,
    tiles_ref,
    rows_ref,
    made_ref,
    left_ref,
    sems,
):
    left_ref[...] = jnp.where(of_ref[...] < 0, plain_ref[...].astype(jnp.float32), 0.0).astype(jnp.bfloat16)
    third = pltpu.make_async_copy(left_ref, kept_ref, sems.at[2])
    third.start()
    steps = jnp.maximum(pl.cdiv(size_ref[1], TILE), 1)
    width = rows_ref.shape[1]

    def block(t, carry):
        def copy(i, c):
            for a in range(16):
                u = i * 16 + a
                row = node_ref[t * TILE + u] & (ACTIVE - 1)
                tiles_ref[pl.ds(pl.multiple_of(u * SUB, SUB), SUB), :] = memory_ref[row].astype(jnp.float32)
            return c

        lax.fori_loop(0, TILE // 16, copy, 0)
        here = pl.ds(pl.multiple_of(t * TILE, TILE), TILE)
        rows_ref[...] = to_matrix(tiles_ref, 0, TILE)
        for j in range(width // COLS):
            for g in range(3):
                made_ref[:, (j * 3 + g) * COLS : (j * 3 + g + 1) * COLS] = jnp.dot(
                    rows_ref[...],
                    gru_ref[:, g * width + j * COLS : g * width + (j + 1) * COLS],
                    preferred_element_type=jnp.float32,
                ).astype(made_ref.dtype)
        first = pltpu.make_async_copy(rows_ref, previous_ref.at[here], sems.at[0])
        second = pltpu.make_async_copy(made_ref, gates_ref.at[here], sems.at[1])
        first.start()
        second.start()
        first.wait()
        second.wait()
        return carry

    lax.fori_loop(0, steps, block, 0)
    third.wait()


def fold_kernel(w2_ref, b2_ref, gru_ref, bias_ref, folded_ref, shift_ref, left_ref):
    hid = w2_ref.shape[0]

    @pl.when(pl.program_id(0) == 0)
    def _():
        left_ref[:hid, :] = w2_ref[...]
        first = b2_ref[...].astype(jnp.bfloat16).astype(jnp.float32)
        rest = b2_ref[...] - first
        second = rest.astype(jnp.bfloat16).astype(jnp.float32)
        rows = lax.broadcasted_iota(jnp.int32, (2 * SUB, b2_ref.shape[1]), 0)
        terms = jnp.where(rows == 0, first, jnp.where(rows == 1, second, jnp.where(rows == 2, rest - second, 0.0)))
        left_ref[hid:, :] = terms.astype(jnp.bfloat16)

    both = jnp.dot(left_ref[...], gru_ref[...], preferred_element_type=jnp.float32)
    folded_ref[...] = both[:hid, :].astype(jnp.bfloat16)
    shift_ref[...] = bias_ref[...] + jnp.sum(both[hid:, :], axis=0, keepdims=True)


def message_kernel(
    place_ref,
    rows_ref,
    feat_ref,
    w1_first_ref,
    w1_hbm,
    b1_ref,
    out_ref,
    w1_ref,
    tiles_ref,
    inputs_ref,
    partial_ref,
    got_ref,
    sent_ref,
    sem,
):
    events = feat_ref.shape[0]
    width, hid = w1_first_ref.shape
    group = 16
    load = pltpu.make_async_copy(w1_hbm.at[pl.ds(width, w1_ref.shape[0])], w1_ref, sem)
    load.start()
    for half in range(2):

        def fetch(i, c):
            for a in range(group):
                e = i * group + a
                got_ref[e] = rows_ref[place_ref[half, e]]
            return c

        lax.fori_loop(0, events // group, fetch, 0, unroll=True)
        tiles_ref[...] = got_ref[...].astype(jnp.float32).reshape(events * SUB, LANES)
        inputs_ref[:, half * width : (half + 1) * width] = to_matrix(tiles_ref, 0, events)
    inputs_ref[:, 2 * width :] = feat_ref[...]
    for j in range(hid // COLS):
        cols = slice(j * COLS, (j + 1) * COLS)
        partial_ref[:, cols] = (
            jnp.dot(inputs_ref[:, :width], w1_first_ref[:, cols], preferred_element_type=jnp.float32) + b1_ref[:, cols]
        )
    load.wait()
    for j in range(hid // COLS):
        cols = slice(j * COLS, (j + 1) * COLS)
        h = partial_ref[:, cols] + jnp.dot(
            inputs_ref[:, width:], w1_ref[:, cols], preferred_element_type=jnp.float32
        )
        h = jnp.maximum(h, 0.0)
        for c in range(COLS // LANES):
            tiles_ref[pl.ds(j * (COLS // LANES) + c, events, stride=SUB), :] = h[:, c * LANES : (c + 1) * LANES]

    def send(i, c):
        for a in range(group):
            e = i * group + a
            sent_ref[place_ref[1, e]] = got_ref[e]
        return c

    got_ref[...] = tiles_ref[...].reshape(events, SUB, LANES).astype(jnp.bfloat16)
    lax.fori_loop(0, events // group, send, 0, unroll=True)
    leave = pltpu.make_async_copy(sent_ref, out_ref, sem)
    leave.start()
    leave.wait()


def update_kernel(
    slot_ref,
    index_ref,
    count_ref,
    size_ref,
    incoming_ref,
    of_ref,
    kept_hbm,
    previous_hbm,
    gates_hbm,
    left_in_ref,
    right_in_hbm,
    left_bias_ref,
    right_bias_ref,
    out_ref,
    final_ref,
    previous_ref,
    gates_ref,
    gru_ref,
    even_ref,
    odd_ref,
    aggregate_ref,
    pick_ref,
    load_sems,
    sems,
):
    width = final_ref.shape[1]
    taken = size_ref[0]
    nodes = size_ref[1]
    steps = jnp.maximum(pl.cdiv(nodes, TILE), 1)
    half = width // 2
    split = left_in_ref.shape[1]
    first_tile = pl.ds(0, TILE)
    halves = []
    for h in range(2):
        loads = [(gates_hbm.at[first_tile, pl.ds(h * 3 * half, 3 * half)], gates_ref.at[:, pl.ds(h * 3 * half, 3 * half)])]
        for g in range(1, 3):
            cols = pl.ds(g * width + h * half - split, half)
            loads.append((right_in_hbm.at[:, cols], gru_ref.at[:, cols]))
        if h == 0:
            loads.append((previous_hbm.at[first_tile], previous_ref))
        else:
            loads.append((kept_hbm, final_ref))
        halves.append([pltpu.make_async_copy(a, b, load_sems.at[h, i]) for i, (a, b) in enumerate(loads)])
    for copy in halves[0] + halves[1]:
        copy.start()

    def clear(t, c):
        here = pl.ds(pl.multiple_of(t * TILE * SUB, TILE * SUB), TILE * SUB)
        even_ref[here, :] = jnp.zeros((TILE * SUB, LANES), jnp.float32)
        odd_ref[here, :] = jnp.zeros((TILE * SUB, LANES), jnp.float32)
        return c

    lax.fori_loop(0, steps, clear, 0)

    def add(i, c):
        for a in range(UNROLL):
            into = odd_ref if a % 2 else even_ref
            here = pl.ds(pl.multiple_of(index_ref[i * UNROLL + a] * SUB, SUB), SUB)
            into[here, :] += incoming_ref[slot_ref[i * UNROLL + a]].astype(jnp.float32)
        return c

    lax.fori_loop(0, pl.cdiv(taken, UNROLL), add, 0)
    def mean(i, c):
        for a in range(UNROLL):
            u = i * UNROLL + a
            here = pl.ds(pl.multiple_of(u * SUB, SUB), SUB)
            even_ref[here, :] = (even_ref[here, :] + odd_ref[here, :]) / count_ref[u].astype(jnp.float32)
        return c

    lax.fori_loop(0, pl.cdiv(nodes, UNROLL), mean, 0)

    def prepare(t):
        aggregate_ref[...] = to_matrix(even_ref, pl.multiple_of(t * TILE, TILE), TILE)
        lane = lax.broadcasted_iota(jnp.int32, (of_ref.shape[0], TILE), 1) + t * TILE
        pick_ref[...] = (of_ref[...] == lane).astype(jnp.float32).astype(jnp.bfloat16)

    def renew(j):
        pre = []
        for g in range(3):
            hid = gates_ref[:, (j * 3 + g) * COLS : (j * 3 + g + 1) * COLS].astype(jnp.float32)
            first = g * width + j * COLS
            part, at = (left_bias_ref, first) if first < split else (right_bias_ref, first - split)
            bias = part[:, at : at + COLS]
            weight = (left_in_ref if first < split else gru_ref)[:, at : at + COLS]
            into = jnp.dot(aggregate_ref[...], weight, preferred_element_type=jnp.float32) + bias
            pre.append((into, hid))
        reset = jax.nn.sigmoid(pre[0][0] + pre[0][1])
        update = jax.nn.sigmoid(pre[1][0] + pre[1][1])
        candidate = jnp.tanh(pre[2][0] + reset * pre[2][1])
        previous = previous_ref[:, j * COLS : (j + 1) * COLS].astype(jnp.float32)
        return ((1.0 - update) * candidate + update * previous).astype(jnp.bfloat16)

    def place(j, renewed):
        cols = slice(j * COLS, (j + 1) * COLS)
        for i in range(final_ref.shape[0] // BAND):
            rows = slice(i * BAND, (i + 1) * BAND)
            found = jnp.dot(pick_ref[rows, :], renewed, preferred_element_type=jnp.float32)
            final_ref[rows, cols] = found.astype(jnp.bfloat16) + final_ref[rows, cols]

    per = half // COLS
    prepare(0)
    for copy in halves[0]:
        copy.wait()
    made = [renew(j) for j in range(per)]
    for copy in halves[1]:
        copy.wait()
    sends = [
        pltpu.make_async_copy(
            final_ref.at[:, pl.ds(h * half, half)], out_ref.at[:, pl.ds(h * half, half)], sems.at[h]
        )
        for h in range(2)
    ]
    for j in range(per):
        place(j, made[j])

    @pl.when(steps == 1)
    def _():
        sends[0].start()

    for j in range(per, 2 * per):
        place(j, renew(j))

    @pl.when(steps > 1)
    def _():
        def block(t, c):
            here = pl.ds(pl.multiple_of(t * TILE, TILE), TILE)
            again = [
                pltpu.make_async_copy(gates_hbm.at[here], gates_ref, load_sems.at[0, 0]),
                pltpu.make_async_copy(previous_hbm.at[here], previous_ref, load_sems.at[0, 1]),
            ]
            for copy in again:
                copy.start()
            prepare(t)
            for copy in again:
                copy.wait()
            for j in range(2 * per):
                place(j, renew(j))
            return c

        lax.fori_loop(1, steps, block, 0)
        sends[0].start()

    sends[1].start()
    for send in sends:
        send.wait()


def on_device(
    memory,
    ends_owner,
    ends_row,
    event_mask,
    edge_feat,
    msg_w1,
    msg_b1,
    msg_w2,
    msg_b2,
    gru_in,
    gru_hid,
    gru_bias,
):
    devices = lax.axis_size(AXES)
    events = ends_owner.shape[0]
    node_rows, width = memory.shape
    hid = msg_w2.shape[0]
    capacity = 5 * events // (2 * devices)
    slots = devices * capacity
    padded = pl.cdiv(slots, TILE) * TILE
    cells = width // LANES
    f32, bf16, i32 = jnp.float32, jnp.bfloat16, jnp.int32
    shape = jax.ShapeDtypeStruct

    ids, place = pl.pallas_call(
        lambda *refs: plan_kernel(capacity, *refs),
        out_shape=(shape((devices, LANES), i32), shape((2, events), i32)),
        in_specs=[VM, VM, VM],
        out_specs=(VM, VM),
        compiler_params=pltpu.CompilerParams(vmem_limit_bytes=WHOLE),
        name="plan",
    )(ends_owner.T, ends_row.T, event_mask.reshape(1, events))

    arrived = lax.all_to_all(
        ids.reshape(devices, 1, LANES), AXES, split_axis=0, concat_axis=0, tiled=True
    ).reshape(devices, LANES)
    tiles = memory.reshape(node_rows, cells, LANES)

    answers, codes = pl.pallas_call(
        lambda *refs: answer_kernel(capacity, *refs),
        out_shape=(pltpu.HBM((slots, cells, LANES), bf16), pltpu.HBM((SUB, devices), i32)),
        in_specs=[VM, VM],
        out_specs=(HBM, HBM),
        scratch_shapes=[
            pltpu.VMEM((SUB, devices), i32),
            pltpu.VMEM((SUB, devices), i32),
            pltpu.SMEM((SUB, devices), i32),
            pltpu.VMEM((slots, cells, LANES), bf16),
            pltpu.SemaphoreType.DMA,
            pltpu.SemaphoreType.DMA((4,)),
        ],
        compiler_params=pltpu.CompilerParams(vmem_limit_bytes=ANSWER),
        name="answer",
    )(arrived, tiles)
    returned = lax.all_to_all(
        answers.reshape(devices, capacity, cells, LANES), AXES, split_axis=0, concat_axis=0, tiled=True
    ).reshape(slots, cells, LANES)

    slot, index, count, node, of, size = pl.pallas_call(
        lambda *refs: compact_kernel(capacity, padded, *refs),
        out_shape=(
            shape((1024,), i32),
            shape((1024,), i32),
            shape((1024,), i32),
            shape((1024,), i32),
            shape((node_rows,), i32),
            shape((8,), i32),
        ),
        in_specs=[VM],
        out_specs=(SM, SM, SM, SM, SM, SM),
        scratch_shapes=[pltpu.SMEM((SUB, devices), i32), pltpu.SemaphoreType.DMA],
        compiler_params=pltpu.CompilerParams(vmem_limit_bytes=MOST),
        cost_estimate=pl.CostEstimate(flops=4_000_000_000, bytes_accessed=20_000_000, transcendentals=0),
        name="compact",
    )(codes)

    of = of.reshape(node_rows, 1)
    previous, gates, kept = pl.pallas_call(
        hidden_gates_kernel,
        out_shape=(
            shape((padded, width), bf16),
            shape((padded, 3 * width), GATES),
            shape((node_rows, width), bf16),
        ),
        in_specs=[SM, SM, VM, VM, VM, VM],
        out_specs=(HBM, HBM, HBM),
        scratch_shapes=[
            pltpu.VMEM((TILE * SUB, LANES), f32),
            pltpu.VMEM((TILE, width), bf16),
            pltpu.VMEM((TILE, 3 * width), GATES),
            pltpu.VMEM((node_rows, width), bf16),
            pltpu.SemaphoreType.DMA((3,)),
        ],
        compiler_params=pltpu.CompilerParams(vmem_limit_bytes=WHOLE),
        cost_estimate=pl.CostEstimate(flops=4_000_000_000, bytes_accessed=20_000_000, transcendentals=0),
        name="hidden_gates",
    )(node, size, tiles, gru_hid, memory, of)

    def fold(first, last):
        step = 512
        offset = first // step
        return pl.pallas_call(
            fold_kernel,
            out_shape=(shape((hid, last - first), bf16), shape((1, last - first), f32)),
            grid=((last - first) // step,),
            in_specs=[
                pl.BlockSpec((hid, width), lambda i: (0, 0)),
                pl.BlockSpec((1, width), lambda i: (0, 0)),
                pl.BlockSpec((width, step), lambda i: (0, i + offset)),
                pl.BlockSpec((1, step), lambda i: (0, i + offset)),
            ],
            out_specs=(pl.BlockSpec((hid, step), lambda i: (0, i)), pl.BlockSpec((1, step), lambda i: (0, i))),
            scratch_shapes=[pltpu.VMEM((hid + 2 * SUB, width), bf16)],
            compiler_params=pltpu.CompilerParams(vmem_limit_bytes=WHOLE),
            cost_estimate=pl.CostEstimate(
                flops=2 * hid * width * (last - first), bytes_accessed=4 * width * (last - first), transcendentals=0
            ),
            name="fold",
        )(msg_w2, msg_b2.reshape(1, width), gru_in, gru_bias.reshape(1, 3 * width))

    split = width
    left_in, left_bias = fold(0, split)
    returned, size, left_in = lax.optimization_barrier((returned, size, left_in))
    outgoing = pl.pallas_call(
        message_kernel,
        out_shape=pltpu.HBM((slots, cells, LANES), bf16),
        in_specs=[SM, VM, VM, VM, HBM, VM],
        out_specs=HBM,
        scratch_shapes=[
            pltpu.VMEM((msg_w1.shape[0] - width, hid), bf16),
            pltpu.VMEM((events * SUB, LANES), f32),
            pltpu.VMEM((events, msg_w1.shape[0]), bf16),
            pltpu.VMEM((events, hid), f32),
            pltpu.VMEM((events, cells, LANES), bf16),
            pltpu.VMEM((slots, cells, LANES), bf16),
            pltpu.SemaphoreType.DMA,
        ],
        compiler_params=pltpu.CompilerParams(vmem_limit_bytes=MESSAGE),
        name="message",
    )(place, returned, edge_feat, msg_w1[:width], msg_w1, msg_b1.reshape(1, hid))
    right_in, right_bias = fold(split, 3 * width)
    incoming = lax.all_to_all(
        outgoing.reshape(devices, capacity, cells, LANES), AXES, split_axis=0, concat_axis=0, tiled=True
    ).reshape(slots, cells, LANES)

    return pl.pallas_call(
        update_kernel,
        out_shape=pltpu.HBM((node_rows, width), bf16),
        in_specs=[SM, SM, SM, SM, VM, VM, HBM, HBM, HBM, VM, HBM, VM, VM],
        out_specs=HBM,
        scratch_shapes=[
            pltpu.VMEM((node_rows, width), bf16),
            pltpu.VMEM((TILE, width), bf16),
            pltpu.VMEM((TILE, 3 * width), GATES),
            pltpu.VMEM((width, 2 * width), bf16),
            pltpu.VMEM(((padded + 1) * SUB, LANES), f32),
            pltpu.VMEM(((padded + 1) * SUB, LANES), f32),
            pltpu.VMEM((TILE, width), bf16),
            pltpu.VMEM((node_rows, TILE), bf16),
            pltpu.SemaphoreType.DMA((2, 5)),
            pltpu.SemaphoreType.DMA((2,)),
        ],
        compiler_params=pltpu.CompilerParams(vmem_limit_bytes=SMALL),
        name="update",
    )(
        slot,
        index,
        count,
        size,
        incoming,
        of,
        kept,
        previous,
        gates,
        left_in,
        right_in,
        left_bias,
        right_bias,
    )


def solution(mesh):
    row = P(AXES, None)
    return jax.shard_map(
        on_device,
        mesh=mesh,
        in_specs=(row, row, row, P(AXES), row, P(), P(), P(), P(), P(), P(), P()),
        out_specs=row,
        check_vma=False,
    )
```

```python
import jax
import jax.numpy as jnp
from jax import lax
from jax.experimental import pallas as pl
from jax.experimental.pallas import tpu as pltpu
from jax.sharding import PartitionSpec as P

AXES = ("node", "tm")
LANES = 128
SUB = 8
ACTIVE = 1024
TILE = 256
COLS = 256
GATES = jnp.bfloat16
UNROLL = 16
BAND = 512
MIB = 1 << 20
WHOLE = 58 * MIB
MOST = 51 * MIB
MESSAGE = 48 * MIB
ANSWER = 48 * MIB

VM = pl.BlockSpec(memory_space=pltpu.VMEM)
SM = pl.BlockSpec(memory_space=pltpu.SMEM)
HBM = pl.BlockSpec(memory_space=pltpu.HBM)


def plan_kernel(capacity, owner_ref, row_ref, mask_ref, ids_ref, place_ref):
    devices = ids_ref.shape[0]
    events = owner_ref.shape[1]
    ends = 2 * events
    owner = jnp.concatenate([owner_ref[0:1, :], owner_ref[1:2, :]], axis=1)
    code = jnp.concatenate([row_ref[0:1, :], row_ref[1:2, :] + ACTIVE * mask_ref[...]], axis=1)
    named = lax.broadcasted_iota(jnp.int32, (devices, ends), 0) == owner
    named_b = named.astype(jnp.float32).astype(jnp.bfloat16)
    block = (LANES, LANES)
    before = lax.broadcasted_iota(jnp.int32, block, 0) < lax.broadcasted_iota(jnp.int32, block, 1)
    table = jnp.concatenate([before.astype(jnp.float32), jnp.ones(block, jnp.float32)], axis=1).astype(jnp.bfloat16)
    total = jnp.zeros((devices, LANES), jnp.float32)
    counts = []
    for i in range(ends // LANES):
        both = jnp.dot(named_b[:, i * LANES : (i + 1) * LANES], table, preferred_element_type=jnp.float32)
        counts.append(both[:, :LANES] + total)
        total = total + both[:, LANES:]
    count = jnp.concatenate(counts, axis=1)
    position = jnp.sum(jnp.where(named, count, 0.0), axis=0, keepdims=True).astype(jnp.int32)
    place = owner * capacity + position
    place_ref[0:1, :] = place[:, :events]
    place_ref[1:2, :] = place[:, events:]
    here = lax.broadcasted_iota(jnp.int32, (LANES, ends), 0) == position
    low = jnp.where(here, (code & 31).astype(jnp.float32), 0.0).astype(jnp.bfloat16)
    high = jnp.where(here, (code >> 5).astype(jnp.float32), 0.0).astype(jnp.bfloat16)
    contract = (((1,), (1,)), ((), ()))
    low_sum = lax.dot_general(named_b, low, contract, preferred_element_type=jnp.float32)
    high_sum = lax.dot_general(named_b, high, contract, preferred_element_type=jnp.float32)
    ids_ref[...] = (low_sum + 32.0 * high_sum).astype(jnp.int32)


def answer_kernel(
    capacity,
    ids_ref,
    memory_ref,
    out_ref,
    codes_ref,
    turned_ref,
    asked_ref,
    wanted_ref,
    rows_ref,
    load_sem,
    sems,
):
    devices = ids_ref.shape[0]
    turned = jnp.transpose(ids_ref[...])[:SUB, :]
    turned_ref[...] = turned
    asked_ref[...] = turned & (ACTIVE - 1)
    load = pltpu.make_async_copy(asked_ref, wanted_ref, load_sem)
    load.start()
    load.wait()
    keep = pltpu.make_async_copy(turned_ref, codes_ref, load_sem)
    keep.start()
    group = 8
    chunks = sems.shape[0]
    part = devices // chunks
    sends = []
    for q in range(chunks):

        def step(i, carry):
            for a in range(group):
                p = q * part + i * group + a
                for k in range(capacity):
                    rows_ref[p * capacity + k] = memory_ref[wanted_ref[k, p]]
            return carry

        lax.fori_loop(0, part // group, step, 0, unroll=True)
        here = pl.ds(q * part * capacity, part * capacity)
        send = pltpu.make_async_copy(rows_ref.at[here], out_ref.at[here], sems.at[q])
        send.start()
        sends.append(send)
    keep.wait()
    for send in sends:
        send.wait()


def compact_kernel(
    capacity, spare_row, codes_ref, slot_ref, index_ref, count_ref, node_ref, of_ref, size_ref, ids_ref, load_sem
):
    devices = ids_ref.shape[1]
    rows = of_ref.shape[0]
    load = pltpu.make_async_copy(codes_ref, ids_ref, load_sem)
    load.start()
    load.wait()

    def clear(i, carry):
        for a in range(16):
            of_ref[i * 16 + a] = -1
        return carry

    lax.fori_loop(0, rows // 16, clear, 0)

    def choose(p, taken):
        for k in range(capacity):
            code = ids_ref[k, p]
            slot_ref[taken] = p * capacity + k
            index_ref[taken] = code & (ACTIVE - 1)
            taken = taken + (code >= ACTIVE).astype(jnp.int32)
        return taken

    taken = lax.fori_loop(0, devices, choose, jnp.int32(0), unroll=2)

    def number(i, nodes):
        node = index_ref[i]
        known = of_ref[node]
        fresh = known < 0
        index = jnp.where(fresh, nodes, known)
        of_ref[node] = index
        index_ref[i] = index
        node_ref[index] = node
        count_ref[index] = jnp.where(fresh, 0, count_ref[index]) + 1
        return nodes + fresh.astype(jnp.int32)

    nodes = lax.fori_loop(0, taken, number, jnp.int32(0))
    size_ref[0] = taken
    size_ref[1] = nodes
    for a in range(UNROLL):
        slot_ref[taken + a] = 0
        index_ref[taken + a] = spare_row
        count_ref[nodes + a] = 1


def to_matrix(tiles_ref, start, rows):
    parts = [tiles_ref[pl.ds(start * SUB + c, rows, stride=SUB), :].astype(jnp.bfloat16) for c in range(SUB)]
    return jnp.concatenate(parts, axis=1)


def hidden_gates_kernel(
    node_ref,
    size_ref,
    memory_ref,
    gru_ref,
    plain_ref,
    of_ref,
    previous_ref,
    gates_ref,
    kept_ref,
    tiles_ref,
    rows_ref,
    made_ref,
    left_ref,
    sems,
):
    left_ref[...] = jnp.where(of_ref[...] < 0, plain_ref[...].astype(jnp.float32), 0.0).astype(jnp.bfloat16)
    third = pltpu.make_async_copy(left_ref, kept_ref, sems.at[2])
    third.start()
    steps = jnp.maximum(pl.cdiv(size_ref[1], TILE), 1)
    width = rows_ref.shape[1]

    def block(t, carry):
        def copy(i, c):
            for a in range(16):
                u = i * 16 + a
                row = node_ref[t * TILE + u] & (ACTIVE - 1)
                tiles_ref[pl.ds(pl.multiple_of(u * SUB, SUB), SUB), :] = memory_ref[row].astype(jnp.float32)
            return c

        lax.fori_loop(0, TILE // 16, copy, 0)
        here = pl.ds(pl.multiple_of(t * TILE, TILE), TILE)
        rows_ref[...] = to_matrix(tiles_ref, 0, TILE)
        for j in range(width // COLS):
            for g in range(3):
                made_ref[:, (j * 3 + g) * COLS : (j * 3 + g + 1) * COLS] = jnp.dot(
                    rows_ref[...],
                    gru_ref[:, g * width + j * COLS : g * width + (j + 1) * COLS],
                    preferred_element_type=jnp.float32,
                ).astype(made_ref.dtype)
        first = pltpu.make_async_copy(rows_ref, previous_ref.at[here], sems.at[0])
        second = pltpu.make_async_copy(made_ref, gates_ref.at[here], sems.at[1])
        first.start()
        second.start()
        first.wait()
        second.wait()
        return carry

    lax.fori_loop(0, steps, block, 0)
    third.wait()


def fold_kernel(w2_ref, b2_ref, gru_ref, bias_ref, folded_ref, shift_ref, left_ref):
    hid = w2_ref.shape[0]

    @pl.when(pl.program_id(0) == 0)
    def _():
        left_ref[:hid, :] = w2_ref[...]
        first = b2_ref[...].astype(jnp.bfloat16).astype(jnp.float32)
        rest = b2_ref[...] - first
        second = rest.astype(jnp.bfloat16).astype(jnp.float32)
        rows = lax.broadcasted_iota(jnp.int32, (2 * SUB, b2_ref.shape[1]), 0)
        terms = jnp.where(rows == 0, first, jnp.where(rows == 1, second, jnp.where(rows == 2, rest - second, 0.0)))
        left_ref[hid:, :] = terms.astype(jnp.bfloat16)

    both = jnp.dot(left_ref[...], gru_ref[...], preferred_element_type=jnp.float32)
    folded_ref[...] = both[:hid, :].astype(jnp.bfloat16)
    shift_ref[...] = bias_ref[...] + jnp.sum(both[hid:, :], axis=0, keepdims=True)


def message_kernel(
    place_ref,
    rows_ref,
    feat_ref,
    w1_first_ref,
    w1_hbm,
    b1_ref,
    out_ref,
    w1_ref,
    tiles_ref,
    inputs_ref,
    partial_ref,
    got_ref,
    sent_ref,
    sem,
):
    events = feat_ref.shape[0]
    width, hid = w1_first_ref.shape
    group = 16
    load = pltpu.make_async_copy(w1_hbm.at[pl.ds(width, w1_ref.shape[0])], w1_ref, sem)
    load.start()
    for half in range(2):

        def fetch(i, c):
            for a in range(group):
                e = i * group + a
                got_ref[e] = rows_ref[place_ref[half, e]]
            return c

        lax.fori_loop(0, events // group, fetch, 0, unroll=True)
        tiles_ref[...] = got_ref[...].astype(jnp.float32).reshape(events * SUB, LANES)
        inputs_ref[:, half * width : (half + 1) * width] = to_matrix(tiles_ref, 0, events)
    inputs_ref[:, 2 * width :] = feat_ref[...]
    for j in range(hid // COLS):
        cols = slice(j * COLS, (j + 1) * COLS)
        partial_ref[:, cols] = (
            jnp.dot(inputs_ref[:, :width], w1_first_ref[:, cols], preferred_element_type=jnp.float32) + b1_ref[:, cols]
        )
    load.wait()
    for j in range(hid // COLS):
        cols = slice(j * COLS, (j + 1) * COLS)
        h = partial_ref[:, cols] + jnp.dot(
            inputs_ref[:, width:], w1_ref[:, cols], preferred_element_type=jnp.float32
        )
        h = jnp.maximum(h, 0.0)
        for c in range(COLS // LANES):
            tiles_ref[pl.ds(j * (COLS // LANES) + c, events, stride=SUB), :] = h[:, c * LANES : (c + 1) * LANES]

    def send(i, c):
        for a in range(group):
            e = i * group + a
            sent_ref[place_ref[1, e]] = got_ref[e]
        return c

    got_ref[...] = tiles_ref[...].reshape(events, SUB, LANES).astype(jnp.bfloat16)
    lax.fori_loop(0, events // group, send, 0, unroll=True)
    leave = pltpu.make_async_copy(sent_ref, out_ref, sem)
    leave.start()
    leave.wait()


def update_kernel(
    slot_ref,
    index_ref,
    count_ref,
    size_ref,
    incoming_ref,
    of_ref,
    kept_hbm,
    previous_hbm,
    gates_hbm,
    left_in_hbm,
    right_in_hbm,
    left_bias_ref,
    right_bias_ref,
    out_ref,
    final_ref,
    previous_ref,
    gates_ref,
    gru_ref,
    even_ref,
    odd_ref,
    aggregate_ref,
    pick_ref,
    load_sems,
    sems,
):
    width = final_ref.shape[1]
    taken = size_ref[0]
    nodes = size_ref[1]
    steps = jnp.maximum(pl.cdiv(nodes, TILE), 1)
    half = width // 2
    split = left_in_hbm.shape[1]
    first_tile = pl.ds(0, TILE)
    halves = []
    for h in range(2):
        loads = [(gates_hbm.at[first_tile, pl.ds(h * 3 * half, 3 * half)], gates_ref.at[:, pl.ds(h * 3 * half, 3 * half)])]
        for g in range(3):
            first = g * width + h * half
            part, at = (left_in_hbm, first) if first < split else (right_in_hbm, first - split)
            loads.append((part.at[:, pl.ds(at, half)], gru_ref.at[:, pl.ds(first, half)]))
        if h == 0:
            loads.append((previous_hbm.at[first_tile], previous_ref))
        else:
            loads.append((kept_hbm, final_ref))
        halves.append([pltpu.make_async_copy(a, b, load_sems.at[h, i]) for i, (a, b) in enumerate(loads)])
    for copy in halves[0] + halves[1]:
        copy.start()

    def clear(t, c):
        here = pl.ds(pl.multiple_of(t * TILE * SUB, TILE * SUB), TILE * SUB)
        even_ref[here, :] = jnp.zeros((TILE * SUB, LANES), jnp.float32)
        odd_ref[here, :] = jnp.zeros((TILE * SUB, LANES), jnp.float32)
        return c

    lax.fori_loop(0, steps, clear, 0)

    def add(i, c):
        for a in range(UNROLL):
            into = odd_ref if a % 2 else even_ref
            here = pl.ds(pl.multiple_of(index_ref[i * UNROLL + a] * SUB, SUB), SUB)
            into[here, :] += incoming_ref[slot_ref[i * UNROLL + a]].astype(jnp.float32)
        return c

    lax.fori_loop(0, pl.cdiv(taken, UNROLL), add, 0)
    def mean(i, c):
        for a in range(UNROLL):
            u = i * UNROLL + a
            here = pl.ds(pl.multiple_of(u * SUB, SUB), SUB)
            even_ref[here, :] = (even_ref[here, :] + odd_ref[here, :]) / count_ref[u].astype(jnp.float32)
        return c

    lax.fori_loop(0, pl.cdiv(nodes, UNROLL), mean, 0)

    def prepare(t):
        aggregate_ref[...] = to_matrix(even_ref, pl.multiple_of(t * TILE, TILE), TILE)
        lane = lax.broadcasted_iota(jnp.int32, (of_ref.shape[0], TILE), 1) + t * TILE
        pick_ref[...] = (of_ref[...] == lane).astype(jnp.float32).astype(jnp.bfloat16)

    def renew(j):
        pre = []
        for g in range(3):
            cols = slice(g * width + j * COLS, g * width + (j + 1) * COLS)
            hid = gates_ref[:, (j * 3 + g) * COLS : (j * 3 + g + 1) * COLS].astype(jnp.float32)
            first = g * width + j * COLS
            part, at = (left_bias_ref, first) if first < split else (right_bias_ref, first - split)
            bias = part[:, at : at + COLS]
            into = jnp.dot(aggregate_ref[...], gru_ref[:, cols], preferred_element_type=jnp.float32) + bias
            pre.append((into, hid))
        reset = jax.nn.sigmoid(pre[0][0] + pre[0][1])
        update = jax.nn.sigmoid(pre[1][0] + pre[1][1])
        candidate = jnp.tanh(pre[2][0] + reset * pre[2][1])
        previous = previous_ref[:, j * COLS : (j + 1) * COLS].astype(jnp.float32)
        return ((1.0 - update) * candidate + update * previous).astype(jnp.bfloat16)

    def place(j, renewed):
        cols = slice(j * COLS, (j + 1) * COLS)
        for i in range(final_ref.shape[0] // BAND):
            rows = slice(i * BAND, (i + 1) * BAND)
            found = jnp.dot(pick_ref[rows, :], renewed, preferred_element_type=jnp.float32)
            final_ref[rows, cols] = found.astype(jnp.bfloat16) + final_ref[rows, cols]

    per = half // COLS
    prepare(0)
    for copy in halves[0]:
        copy.wait()
    made = [renew(j) for j in range(per)]
    for copy in halves[1]:
        copy.wait()
    sends = [
        pltpu.make_async_copy(
            final_ref.at[:, pl.ds(h * half, half)], out_ref.at[:, pl.ds(h * half, half)], sems.at[h]
        )
        for h in range(2)
    ]
    for j in range(per):
        place(j, made[j])

    @pl.when(steps == 1)
    def _():
        sends[0].start()

    for j in range(per, 2 * per):
        place(j, renew(j))

    @pl.when(steps > 1)
    def _():
        def block(t, c):
            here = pl.ds(pl.multiple_of(t * TILE, TILE), TILE)
            again = [
                pltpu.make_async_copy(gates_hbm.at[here], gates_ref, load_sems.at[0, 0]),
                pltpu.make_async_copy(previous_hbm.at[here], previous_ref, load_sems.at[0, 1]),
            ]
            for copy in again:
                copy.start()
            prepare(t)
            for copy in again:
                copy.wait()
            for j in range(2 * per):
                place(j, renew(j))
            return c

        lax.fori_loop(1, steps, block, 0)
        sends[0].start()

    sends[1].start()
    for send in sends:
        send.wait()


def on_device(
    memory,
    ends_owner,
    ends_row,
    event_mask,
    edge_feat,
    msg_w1,
    msg_b1,
    msg_w2,
    msg_b2,
    gru_in,
    gru_hid,
    gru_bias,
):
    devices = lax.axis_size(AXES)
    events = ends_owner.shape[0]
    node_rows, width = memory.shape
    hid = msg_w2.shape[0]
    capacity = 5 * events // (2 * devices)
    slots = devices * capacity
    padded = pl.cdiv(slots, TILE) * TILE
    cells = width // LANES
    f32, bf16, i32 = jnp.float32, jnp.bfloat16, jnp.int32
    shape = jax.ShapeDtypeStruct

    ids, place = pl.pallas_call(
        lambda *refs: plan_kernel(capacity, *refs),
        out_shape=(shape((devices, LANES), i32), shape((2, events), i32)),
        in_specs=[VM, VM, VM],
        out_specs=(VM, VM),
        compiler_params=pltpu.CompilerParams(vmem_limit_bytes=WHOLE),
        name="plan",
    )(ends_owner.T, ends_row.T, event_mask.reshape(1, events))

    arrived = lax.all_to_all(
        ids.reshape(devices, 1, LANES), AXES, split_axis=0, concat_axis=0, tiled=True
    ).reshape(devices, LANES)
    tiles = memory.reshape(node_rows, cells, LANES)

    answers, codes = pl.pallas_call(
        lambda *refs: answer_kernel(capacity, *refs),
        out_shape=(pltpu.HBM((slots, cells, LANES), bf16), pltpu.HBM((SUB, devices), i32)),
        in_specs=[VM, VM],
        out_specs=(HBM, HBM),
        scratch_shapes=[
            pltpu.VMEM((SUB, devices), i32),
            pltpu.VMEM((SUB, devices), i32),
            pltpu.SMEM((SUB, devices), i32),
            pltpu.VMEM((slots, cells, LANES), bf16),
            pltpu.SemaphoreType.DMA,
            pltpu.SemaphoreType.DMA((8,)),
        ],
        compiler_params=pltpu.CompilerParams(vmem_limit_bytes=ANSWER),
        name="answer",
    )(arrived, tiles)
    returned = lax.all_to_all(
        answers.reshape(devices, capacity, cells, LANES), AXES, split_axis=0, concat_axis=0, tiled=True
    ).reshape(slots, cells, LANES)

    slot, index, count, node, of, size = pl.pallas_call(
        lambda *refs: compact_kernel(capacity, padded, *refs),
        out_shape=(
            shape((1024,), i32),
            shape((1024,), i32),
            shape((1024,), i32),
            shape((1024,), i32),
            shape((node_rows,), i32),
            shape((8,), i32),
        ),
        in_specs=[VM],
        out_specs=(SM, SM, SM, SM, SM, SM),
        scratch_shapes=[pltpu.SMEM((SUB, devices), i32), pltpu.SemaphoreType.DMA],
        compiler_params=pltpu.CompilerParams(vmem_limit_bytes=MOST),
        cost_estimate=pl.CostEstimate(flops=4_000_000_000, bytes_accessed=20_000_000, transcendentals=0),
        name="compact",
    )(codes)

    of = of.reshape(node_rows, 1)
    previous, gates, kept = pl.pallas_call(
        hidden_gates_kernel,
        out_shape=(
            shape((padded, width), bf16),
            shape((padded, 3 * width), GATES),
            shape((node_rows, width), bf16),
        ),
        in_specs=[SM, SM, VM, VM, VM, VM],
        out_specs=(HBM, HBM, HBM),
        scratch_shapes=[
            pltpu.VMEM((TILE * SUB, LANES), f32),
            pltpu.VMEM((TILE, width), bf16),
            pltpu.VMEM((TILE, 3 * width), GATES),
            pltpu.VMEM((node_rows, width), bf16),
            pltpu.SemaphoreType.DMA((3,)),
        ],
        compiler_params=pltpu.CompilerParams(vmem_limit_bytes=WHOLE),
        cost_estimate=pl.CostEstimate(flops=4_000_000_000, bytes_accessed=20_000_000, transcendentals=0),
        name="hidden_gates",
    )(node, size, tiles, gru_hid, memory, of)

    def fold(first, last):
        step = 512
        offset = first // step
        return pl.pallas_call(
            fold_kernel,
            out_shape=(shape((hid, last - first), bf16), shape((1, last - first), f32)),
            grid=((last - first) // step,),
            in_specs=[
                pl.BlockSpec((hid, width), lambda i: (0, 0)),
                pl.BlockSpec((1, width), lambda i: (0, 0)),
                pl.BlockSpec((width, step), lambda i: (0, i + offset)),
                pl.BlockSpec((1, step), lambda i: (0, i + offset)),
            ],
            out_specs=(pl.BlockSpec((hid, step), lambda i: (0, i)), pl.BlockSpec((1, step), lambda i: (0, i))),
            scratch_shapes=[pltpu.VMEM((hid + 2 * SUB, width), bf16)],
            compiler_params=pltpu.CompilerParams(vmem_limit_bytes=WHOLE),
            cost_estimate=pl.CostEstimate(
                flops=2 * hid * width * (last - first), bytes_accessed=4 * width * (last - first), transcendentals=0
            ),
            name="fold",
        )(msg_w2, msg_b2.reshape(1, width), gru_in, gru_bias.reshape(1, 3 * width))

    split = width
    left_in, left_bias = fold(0, split)
    returned, size, left_in = lax.optimization_barrier((returned, size, left_in))
    outgoing = pl.pallas_call(
        message_kernel,
        out_shape=pltpu.HBM((slots, cells, LANES), bf16),
        in_specs=[SM, VM, VM, VM, HBM, VM],
        out_specs=HBM,
        scratch_shapes=[
            pltpu.VMEM((msg_w1.shape[0] - width, hid), bf16),
            pltpu.VMEM((events * SUB, LANES), f32),
            pltpu.VMEM((events, msg_w1.shape[0]), bf16),
            pltpu.VMEM((events, hid), f32),
            pltpu.VMEM((events, cells, LANES), bf16),
            pltpu.VMEM((slots, cells, LANES), bf16),
            pltpu.SemaphoreType.DMA,
        ],
        compiler_params=pltpu.CompilerParams(vmem_limit_bytes=MESSAGE),
        name="message",
    )(place, returned, edge_feat, msg_w1[:width], msg_w1, msg_b1.reshape(1, hid))
    right_in, right_bias = fold(split, 3 * width)
    incoming = lax.all_to_all(
        outgoing.reshape(devices, capacity, cells, LANES), AXES, split_axis=0, concat_axis=0, tiled=True
    ).reshape(slots, cells, LANES)

    return pl.pallas_call(
        update_kernel,
        out_shape=shape((node_rows, width), bf16),
        in_specs=[SM, SM, SM, SM, VM, VM, HBM, HBM, HBM, HBM, HBM, VM, VM],
        out_specs=HBM,
        scratch_shapes=[
            pltpu.VMEM((node_rows, width), bf16),
            pltpu.VMEM((TILE, width), bf16),
            pltpu.VMEM((TILE, 3 * width), GATES),
            pltpu.VMEM((width, 3 * width), bf16),
            pltpu.VMEM(((padded + 1) * SUB, LANES), f32),
            pltpu.VMEM(((padded + 1) * SUB, LANES), f32),
            pltpu.VMEM((TILE, width), bf16),
            pltpu.VMEM((node_rows, TILE), bf16),
            pltpu.SemaphoreType.DMA((2, 5)),
            pltpu.SemaphoreType.DMA((2,)),
        ],
        compiler_params=pltpu.CompilerParams(vmem_limit_bytes=MOST),
        name="update",
    )(
        slot,
        index,
        count,
        size,
        incoming,
        of,
        kept,
        previous,
        gates,
        left_in,
        right_in,
        left_bias,
        right_bias,
    )


def solution(mesh):
    row = P(AXES, None)
    return jax.shard_map(
        on_device,
        mesh=mesh,
        in_specs=(row, row, row, P(AXES), row, P(), P(), P(), P(), P(), P(), P()),
        out_specs=row,
        check_vma=False,
    )
```
